128 devices in a mesh: brick: 8 (over y, core), grp: 16 (over x, z).
Axes of the slice: x: 4, y: 4, z: 4, core: 2. Of those that a mesh axis runs over, the one named last changes fastest.
Arguments:
- source: float32 [16, 8, 2, 32, 1024], P('grp', 'brick'), may hold values from -21 to 21
- uptake: float32 [16, 8, 2, 32, 1024], P('grp', 'brick'), may hold values from 0.00015 to 0.006
- conductance: float32 [16, 8, 6, 2, 32, 1024], P('grp', 'brick'), may hold values from 0 to 3, as said below
- occupancy: int32 [16, 2, 8], replicated, may hold values from 0 to 1, as said below
- assignment: int32 [8], replicated, may hold values from 0 to 7, as said below
Outputs:
- solution_field: float32 [16, 8, 2, 32, 1024], P('grp', 'brick')
- residual: float32 [16, 8, 2, 32, 1024], P('grp', 'brick')
The draws below stay inside these ranges and needn't reach their ends.
Inputs may be any that keep to these rules, and one draw needn't show every extreme that they name: `occupancy`: 1 marks an occupied brick; in every draw one patch of some slab has all its bricks occupied. `assignment`: each patch is held by exactly one index of brick. `conductance`: equal at both ends of a bond: the value toward +x at a cell is the value toward -x at its +x neighbour, likewise for y and z, the lattice being read cyclically; values toward +z and -z are 0.3 or more.
All inputs are finite; a program needn't handle non-finite values.
Results may differ from the reference program's by a relative error of at most 0.0003.
Values sent between devices are 32-bit elements; how exact they have to be, the bound alone decides.
A program may use at most 128 MiB of HBM per device.

```python
import math
import jax
import jax.numpy as jnp
from jax import lax

BS = 32
PATCH_X = 1
PATCH_Y = 2
ITERS = 3
SWEEPS = 2
SLOTS = 2
NSLAB = 16
NPATCH = 8
PGY = 4
LXB = 2
LYB = 8
COARSE = 32


def patch_order(key):
    return jax.random.permutation(jax.random.fold_in(key, 11), NPATCH).astype(jnp.int32)


def draw_assignment(key, part):
    return patch_order(key)


def draw_occupancy(key, part):
    subkeys = jax.random.split(jax.random.fold_in(key, 23), 4)
    density = jax.random.randint(subkeys[0], (NSLAB, 2, PGY), 30, 101)
    density = jnp.repeat(jnp.repeat(density, PATCH_X, axis=1), PATCH_Y, axis=2)
    chances = jax.random.randint(subkeys[1], (NSLAB, LXB, LYB), 0, 100)
    chosen_slab = jax.random.randint(subkeys[2], (), 0, NSLAB)
    chosen_patch = jax.random.randint(subkeys[3], (), 0, NPATCH)
    slab_ids = jnp.arange(NSLAB)[:, None, None]
    row_ids = (jnp.arange(LXB) // PATCH_X)[None, :, None]
    column_ids = (jnp.arange(LYB) // PATCH_Y)[None, None, :]
    forced = (slab_ids == chosen_slab) & (row_ids == chosen_patch // PGY) & (column_ids == chosen_patch % PGY)
    return ((chances < density) | forced).astype(jnp.int32)


def to_devices_drawn(lattice, layout_order):
    shaped = lattice.reshape(NSLAB, BS, 2, PATCH_X, BS, PGY, PATCH_Y, BS)
    ordered = jnp.transpose(shaped, (0, 2, 5, 3, 6, 4, 7, 1)).reshape(NSLAB, NPATCH, SLOTS, BS, BS * BS)
    return jnp.take(ordered, layout_order, axis=1)


def strength(subkey, extent):
    return jnp.exp(jax.random.uniform(subkey, extent, jnp.float32, math.log(0.3), math.log(3.0)))


def draw_conductance(key, part):
    layout_order = patch_order(key)
    subkeys = jax.random.split(jax.random.fold_in(key, 31), 5)
    extent = (NSLAB * BS, LXB * BS, LYB * BS)
    dilution = 0.3
    kept_first = (jax.random.uniform(subkeys[1], extent, jnp.float32) >= dilution).astype(jnp.float32)
    kept_second = (jax.random.uniform(subkeys[3], extent, jnp.float32) >= dilution).astype(jnp.float32)
    along_first = strength(subkeys[0], extent) * kept_first
    along_second = strength(subkeys[2], extent) * kept_second
    along_third = strength(subkeys[4], extent)
    pieces = [along_first, jnp.roll(along_first, 1, axis=1), along_second, jnp.roll(along_second, 1, axis=2), along_third, jnp.roll(along_third, 1, axis=0)]
    return jnp.stack([to_devices_drawn(piece, layout_order) for piece in pieces], axis=2)


def draw_source(key, part):
    subkeys = jax.random.split(jax.random.fold_in(key, 41), 1)
    extent = (NSLAB, NPATCH, SLOTS, BS, BS * BS)
    rising = (1.0 + 2.0 * jnp.arange(NSLAB, dtype=jnp.float32) / max(NSLAB - 1, 1)).reshape(NSLAB, 1, 1, 1, 1)
    values = jnp.clip(jax.random.normal(subkeys[0], extent, jnp.float32), -7.0, 7.0)
    return values * rising


def draw_uptake(key, part):
    subkeys = jax.random.split(jax.random.fold_in(key, 53), 2)
    extent = (NSLAB, NPATCH, SLOTS, BS, BS * BS)
    per_brick = jnp.exp(jax.random.uniform(subkeys[0], (NSLAB, NPATCH, SLOTS, 1, 1), jnp.float32, math.log(0.0003), math.log(0.003)))
    per_cell = jnp.exp(jax.random.uniform(subkeys[1], extent, jnp.float32, math.log(0.5), math.log(2.0)))
    return per_brick * per_cell


def setup_inputs(seed: int = 0) -> dict:
    key_list = jax.random.split(jax.random.key(seed), 6)
    return {
        "source": draw_source(jax.random.fold_in(key_list[5], 71), 0),
        "uptake": draw_uptake(jax.random.fold_in(key_list[5], 71), 0),
        "conductance": draw_conductance(jax.random.fold_in(key_list[5], 71), 0),
        "occupancy": draw_occupancy(jax.random.fold_in(key_list[5], 71), 0),
        "assignment": draw_assignment(jax.random.fold_in(key_list[5], 71), 0),
    }


OMEGA = 0.6

def assemble(coarse_diag, couplings, strides):
    extent = coarse_diag.shape[0]
    matrix = jnp.diag(coarse_diag)
    for coupling, stride in zip(couplings, strides):
        if stride < extent:
            banded = coupling[:extent - stride]
            matrix = matrix - jnp.diag(banded, stride) - jnp.diag(banded, -stride)
    return matrix

def to_lattice(field, owners):
    ordered = jnp.take(field, owners, axis=1)
    shaped = ordered.reshape(NSLAB, 2, PGY, PATCH_X, PATCH_Y, BS, BS, BS)
    return jnp.transpose(shaped, (0, 7, 1, 3, 5, 2, 4, 6)).reshape(NSLAB * BS, LXB * BS, LYB * BS)

def to_devices(lattice, assignment):
    shaped = lattice.reshape(NSLAB, BS, 2, PATCH_X, BS, PGY, PATCH_Y, BS)
    ordered = jnp.transpose(shaped, (0, 2, 5, 3, 6, 4, 7, 1)).reshape(NSLAB, NPATCH, SLOTS, BS, BS * BS)
    return jnp.take(ordered, assignment, axis=1)

def ahead(field, axis):
    extent = field.shape[axis]
    rest = lax.slice_in_dim(field, 1, extent, axis=axis)
    zeros = jnp.zeros_like(lax.slice_in_dim(field, 0, 1, axis=axis))
    return jnp.concatenate([rest, zeros], axis=axis)

def behind(field, axis):
    extent = field.shape[axis]
    rest = lax.slice_in_dim(field, 0, extent - 1, axis=axis)
    zeros = jnp.zeros_like(lax.slice_in_dim(field, 0, 1, axis=axis))
    return jnp.concatenate([zeros, rest], axis=axis)
MOVES = ((1, True), (1, False), (2, True), (2, False), (0, True), (0, False))

def neighbour(field, move):
    if move[1]:
        return ahead(field, move[0])
    return behind(field, move[0])

def brick_sums(field):
    return field.reshape(NSLAB, BS, LXB, BS, LYB, BS).sum(axis=(1, 3, 5))

def per_patch(grid):
    return jnp.transpose(grid.reshape(NSLAB, 2, PATCH_X, PGY, PATCH_Y), (1, 3, 0, 2, 4)).reshape(NPATCH, COARSE)

def from_patches(vectors):
    return jnp.transpose(vectors.reshape(2, PGY, NSLAB, PATCH_X, PATCH_Y), (2, 0, 3, 1, 4)).reshape(NSLAB, LXB, LYB)

def build(coarse_diag, first, second, third):
    return assemble(coarse_diag, (first, second, third), (PATCH_Y, 1, SLOTS))

def reference(source, uptake, conductance, occupancy, assignment):
    owners = jnp.zeros((NPATCH,), jnp.int32).at[assignment].set(jnp.arange(NPATCH, dtype=jnp.int32))
    live = occupancy.astype(jnp.float32)
    cube_shape = (NSLAB * BS, LXB * BS, LYB * BS)
    live_cells = jnp.broadcast_to(live[:, None, :, None, :, None], (NSLAB, BS, LXB, BS, LYB, BS)).reshape(cube_shape)
    effective = []
    for direction in range(6):
        bonds = to_lattice(conductance[:, :, direction], owners)
        effective.append(bonds * live_cells * neighbour(live_cells, MOVES[direction]))
    absorb = to_lattice(uptake, owners)
    diagonal = absorb
    for direction in range(6):
        diagonal = diagonal + effective[direction]

    def operate(field):
        total = diagonal * field
        for direction in range(6):
            total = total - effective[direction] * neighbour(field, MOVES[direction])
        return total

    def shaped(field):
        return field.reshape(NSLAB, BS, LXB, BS, LYB, BS)
    face_sums = [jnp.take(shaped(effective[0]), BS - 1, axis=3).sum(axis=(1, 4)), jnp.take(shaped(effective[1]), 0, axis=3).sum(axis=(1, 4)), jnp.take(shaped(effective[2]), BS - 1, axis=5).sum(axis=(1, 3)), jnp.take(shaped(effective[3]), 0, axis=5).sum(axis=(1, 3)), jnp.take(shaped(effective[4]), BS - 1, axis=1).sum(axis=(2, 4)), jnp.take(shaped(effective[5]), 0, axis=1).sum(axis=(2, 4))]
    position_x = jnp.arange(LXB) % PATCH_X
    position_y = jnp.arange(LYB) % PATCH_Y
    inside = [(position_x < PATCH_X - 1).astype(jnp.float32)[None, :, None], (position_x > 0).astype(jnp.float32)[None, :, None], (position_y < PATCH_Y - 1).astype(jnp.float32)[None, None, :], (position_y > 0).astype(jnp.float32)[None, None, :]]
    coarse_diag = brick_sums(absorb)
    for direction in range(4):
        coarse_diag = coarse_diag + face_sums[direction] * inside[direction]
    coarse_diag = coarse_diag + face_sums[4] + face_sums[5]
    matrices = jax.vmap(build)(per_patch(coarse_diag), per_patch(face_sums[0] * inside[0]), per_patch(face_sums[2] * inside[2]), per_patch(face_sums[4]))
    factors = jnp.linalg.cholesky(matrices)

    def coarse(residual_field):
        terms = per_patch(brick_sums(residual_field))[:, :, None]
        middle = lax.linalg.triangular_solve(factors, terms, left_side=True, lower=True)
        result = lax.linalg.triangular_solve(factors, middle, left_side=True, lower=True, transpose_a=True)
        grid = from_patches(result[:, :, 0])
        return jnp.broadcast_to(grid[:, None, :, None, :, None], (NSLAB, BS, LXB, BS, LYB, BS)).reshape(cube_shape)

    def precondition(residual_field):
        smoothed = OMEGA * residual_field / diagonal
        for _ in range(SWEEPS - 1):
            smoothed = smoothed + OMEGA * (residual_field - operate(smoothed)) / diagonal
        return smoothed + coarse(residual_field)
    forcing = to_lattice(source, owners) * live_cells
    solution_field = jnp.zeros_like(forcing)
    residual = forcing
    search = precondition(residual)
    energy = jnp.sum(residual * search)
    for iteration in range(ITERS):
        mapped = operate(search)
        step_size = energy / jnp.sum(search * mapped)
        solution_field = solution_field + step_size * search
        residual = residual - step_size * mapped
        if iteration + 1 < ITERS:
            smoothed = precondition(residual)
            renewed = jnp.sum(residual * smoothed)
            search = smoothed + renewed / energy * search
            energy = renewed
    return (to_devices(solution_field, assignment), to_devices(residual, assignment))
```

```python
import jax
import jax.numpy as jnp
from jax import lax
from jax.sharding import PartitionSpec as P

BS = 32
PATCH_X = 1
PATCH_Y = 2
ITERS = 3


OMEGA = 0.6


def extended_2(block, sides, width):
    for axis, dim in sides:
        count = lax.axis_size(axis)
        forward = [(i, i + 1) for i in range(count - 1)]
        backward = [(target, source) for source, target in forward]
        low = lax.ppermute(
            lax.slice_in_dim(block, block.shape[dim] - width, None, axis=dim), axis, forward
        )
        high = lax.ppermute(lax.slice_in_dim(block, 0, width, axis=dim), axis, backward)
        block = jnp.concatenate([low, block, high], axis=dim)
    return block


def assemble(coarse_diag, couplings, strides):
    extent = coarse_diag.shape[0]
    matrix = jnp.diag(coarse_diag)
    for coupling, stride in zip(couplings, strides):
        banded = coupling[: extent - stride]
        matrix = matrix - jnp.diag(banded, stride) - jnp.diag(banded, -stride)
    return matrix


def pad_rows(block, capacity):
    return jnp.pad(block, ((0, capacity - block.shape[0]), (0, 0)))


def on_device(source, uptake, conductance, occupancy, assignment):
    face_size = BS * BS
    capacity = max(PATCH_X, PATCH_Y)
    slot_count = PATCH_X * PATCH_Y
    slab_index = lax.axis_index("grp")
    brick_index = lax.axis_index("brick")
    brick_count = lax.axis_size("brick")
    across = brick_count // 2
    peer_ids = jnp.arange(brick_count, dtype=jnp.int32)
    patch_index = assignment[brick_index]
    patch_row = patch_index // across
    patch_column = patch_index % across

    def owner_of(row_shift, column_shift):
        row_target = patch_row + row_shift
        column_target = patch_column + column_shift
        inside = (
            (row_target >= 0) & (row_target < 2) & (column_target >= 0) & (column_target < across)
        )
        holder = jnp.sum(jnp.where(assignment == row_target * across + column_target, peer_ids, 0))
        return jnp.where(inside, holder, -1)

    wanted = jnp.stack([owner_of(1, 0), owner_of(-1, 0), owner_of(0, 1), owner_of(0, -1)])
    padded = jnp.pad(occupancy, 1)
    window = lax.dynamic_slice(
        padded,
        (slab_index, patch_row * PATCH_X, patch_column * PATCH_Y),
        (3, PATCH_X + 2, PATCH_Y + 2),
    ).astype(jnp.float32)
    centre = window[1, 1:-1, 1:-1].reshape(slot_count)
    toward = [
        window[1, 2:, 1:-1],
        window[1, :-2, 1:-1],
        window[1, 1:-1, 2:],
        window[1, 1:-1, :-2],
        window[2, 1:-1, 1:-1],
        window[0, 1:-1, 1:-1],
    ]
    first_axis = lax.broadcasted_iota(jnp.int32, (1, BS, face_size), 1)
    flat_axis = lax.broadcasted_iota(jnp.int32, (1, BS, face_size), 2)
    second_axis = flat_axis // BS
    third_axis = flat_axis % BS
    cube_third = lax.broadcasted_iota(jnp.int32, (1, BS, BS, BS), 3)
    borders = [
        first_axis == BS - 1,
        first_axis == 0,
        second_axis == BS - 1,
        second_axis == 0,
        third_axis == BS - 1,
        third_axis == 0,
    ]
    bonds = conductance[0, 0]
    live_here = centre[:, None, None]
    effective = []
    for direction in range(6):
        neighbour_live = toward[direction].reshape(slot_count)[:, None, None]
        active = jnp.where(borders[direction], live_here * neighbour_live, live_here)
        effective.append(bonds[direction] * active)
    absorb = uptake[0, 0]
    diagonal = absorb
    for direction in range(6):
        diagonal = diagonal + effective[direction]

    def apply_operator(field):
        lower_x = field[:, 0, :]
        upper_x = field[:, BS - 1, :]
        lower_y = field[:, :, :BS].reshape(slot_count, face_size)
        upper_y = field[:, :, face_size - BS :].reshape(slot_count, face_size)
        cube = field.reshape(slot_count, BS, BS, BS)
        lower_z = cube[:, :, :, 0].reshape(slot_count, face_size)
        upper_z = cube[:, :, :, BS - 1].reshape(slot_count, face_size)
        grid_lower_x = lower_x.reshape(PATCH_X, PATCH_Y, face_size)
        grid_upper_x = upper_x.reshape(PATCH_X, PATCH_Y, face_size)
        grid_lower_y = lower_y.reshape(PATCH_X, PATCH_Y, face_size)
        grid_upper_y = upper_y.reshape(PATCH_X, PATCH_Y, face_size)
        outgoing_sides = jnp.stack(
            [
                pad_rows(grid_lower_x[0], capacity),
                pad_rows(grid_upper_x[PATCH_X - 1], capacity),
                pad_rows(grid_lower_y[:, 0], capacity),
                pad_rows(grid_upper_y[:, PATCH_Y - 1], capacity),
            ]
        )
        portion = lax.all_gather(outgoing_sides[None], "brick", axis=0, tiled=True)
        sources = jnp.arange(portion.shape[0], dtype=jnp.int32)
        matches = sources[:, None] == wanted[None, :]
        remote = jnp.zeros((4, capacity, face_size), jnp.float32) + jnp.sum(
            jnp.where(matches[:, :, None, None], portion, 0.0), axis=0
        )
        stacked = jnp.stack([lower_z, upper_z])
        extended = extended_2(stacked, (("grp", 0),), 1)
        from_below = extended[0].reshape(slot_count, BS, BS, 1)
        from_above = extended[3].reshape(slot_count, BS, BS, 1)
        beyond_xplus = jnp.concatenate(
            [grid_lower_x[1:], remote[0, :PATCH_Y][None]], axis=0
        ).reshape(slot_count, face_size)
        beyond_xminus = jnp.concatenate(
            [remote[1, :PATCH_Y][None], grid_upper_x[:-1]], axis=0
        ).reshape(slot_count, face_size)
        beyond_yplus = jnp.concatenate(
            [grid_lower_y[:, 1:], remote[2, :PATCH_X][:, None]], axis=1
        ).reshape(slot_count, BS, BS)
        beyond_yminus = jnp.concatenate(
            [remote[3, :PATCH_X][:, None], grid_upper_y[:, :-1]], axis=1
        ).reshape(slot_count, BS, BS)
        upper_neighbour = jnp.where(
            cube_third == BS - 1, from_above, jnp.roll(cube, -1, axis=3)
        ).reshape(slot_count, BS, face_size)
        lower_neighbour = jnp.where(cube_third == 0, from_below, jnp.roll(cube, 1, axis=3)).reshape(
            slot_count, BS, face_size
        )
        total = diagonal * field
        total = total - effective[0] * jnp.concatenate(
            [field[:, 1:, :], beyond_xplus[:, None, :]], axis=1
        )
        total = total - effective[1] * jnp.concatenate(
            [beyond_xminus[:, None, :], field[:, :-1, :]], axis=1
        )
        total = total - effective[2] * jnp.concatenate([field[:, :, BS:], beyond_yplus], axis=2)
        total = total - effective[3] * jnp.concatenate(
            [beyond_yminus, field[:, :, : face_size - BS]], axis=2
        )
        total = total - effective[4] * upper_neighbour
        total = total - effective[5] * lower_neighbour
        return total

    slot_ids = jnp.arange(slot_count)
    brick_first = slot_ids // PATCH_Y
    brick_second = slot_ids % PATCH_Y
    inside = [
        (brick_first < PATCH_X - 1).astype(jnp.float32),
        (brick_first > 0).astype(jnp.float32),
        (brick_second < PATCH_Y - 1).astype(jnp.float32),
        (brick_second > 0).astype(jnp.float32),
    ]
    face_sums = [
        jnp.sum(effective[0][:, BS - 1, :], axis=1),
        jnp.sum(effective[1][:, 0, :], axis=1),
        jnp.sum(effective[2][:, :, face_size - BS :], axis=(1, 2)),
        jnp.sum(effective[3][:, :, :BS], axis=(1, 2)),
        jnp.sum(effective[4].reshape(slot_count, BS, BS, BS)[:, :, :, BS - 1], axis=(1, 2)),
        jnp.sum(effective[5].reshape(slot_count, BS, BS, BS)[:, :, :, 0], axis=(1, 2)),
    ]
    coarse_diag = jnp.sum(absorb, axis=(1, 2))
    for direction in range(4):
        coarse_diag = coarse_diag + face_sums[direction] * inside[direction]
    coarse_diag = coarse_diag + face_sums[4] + face_sums[5]
    grp_count = lax.axis_size("grp")
    grp_ids = jnp.arange(grp_count, dtype=jnp.int32)

    def butterfly(values, axes):
        for axis in axes:
            count = lax.axis_size(axis)
            if count & (count - 1):
                values = lax.psum(values, axis)
                continue
            stride = 1
            while stride < count:
                pairs = [(i, i ^ stride) for i in range(count)]
                values = values + lax.ppermute(values, axis, pairs)
                stride *= 2
        return values

    def slab_slot(values):
        here = (grp_ids == slab_index).astype(jnp.float32)
        return here[:, None, None] * values[None]

    forcing = source[0, 0] * live_here
    record = jnp.stack(
        [
            coarse_diag,
            face_sums[0] * inside[0],
            face_sums[2] * inside[2],
            face_sums[4],
            jnp.sum(forcing, axis=(1, 2)),
        ]
    )
    gathered = butterfly(slab_slot(record), ("grp",))
    columns = jnp.transpose(gathered, (1, 0, 2)).reshape(5, -1)
    matrix = assemble(columns[0], (columns[1], columns[2], columns[3]), (PATCH_Y, 1, slot_count))
    factor = jnp.linalg.cholesky(matrix)

    def coarse_solve(terms):
        middle = lax.linalg.triangular_solve(factor, terms[:, None], left_side=True, lower=True)
        result = lax.linalg.triangular_solve(
            factor, middle, left_side=True, lower=True, transpose_a=True
        )
        return lax.dynamic_slice_in_dim(result[:, 0], slab_index * slot_count, slot_count)

    def precondition(residual_field, terms):
        smoothed = OMEGA * residual_field / diagonal
        smoothed = smoothed + OMEGA * (residual_field - apply_operator(smoothed)) / diagonal
        return smoothed + coarse_solve(terms)[:, None, None]

    brick_here = (peer_ids == brick_index).astype(jnp.float32)

    def dot_and_sums(product, field):
        sums = slab_slot(jnp.sum(field, axis=(1, 2))[None])[:, 0]
        spread = brick_here[:, None, None] * sums[None]
        packed = jnp.concatenate([jnp.sum(product)[None], spread.reshape(-1)])
        total = butterfly(packed, ("brick", "grp"))
        mine = lax.dynamic_index_in_dim(
            total[1:].reshape(brick_count, -1), brick_index, keepdims=False
        )
        return total[0], mine

    def global_sum(values):
        return butterfly(jnp.sum(values)[None], ("brick", "grp"))[0]

    terms = columns[4]
    solution_field = jnp.zeros_like(forcing)
    residual = forcing
    search = precondition(residual, terms)
    energy = global_sum(residual * search)
    for iteration in range(ITERS):
        mapped = apply_operator(search)
        curvature, mapped_terms = dot_and_sums(search * mapped, mapped)
        step_size = energy / curvature
        solution_field = solution_field + step_size * search
        residual = residual - step_size * mapped
        if iteration + 1 < ITERS:
            terms = terms - step_size * mapped_terms
            smoothed = precondition(residual, terms)
            renewed = global_sum(residual * smoothed)
            search = smoothed + renewed / energy * search
            energy = renewed
    return (solution_field[None, None], residual[None, None])


def solution(mesh):
    return jax.shard_map(
        on_device,
        mesh=mesh,
        in_specs=(
            P("grp", "brick", None, None, None),
            P("grp", "brick", None, None, None),
            P("grp", "brick", None, None, None, None),
            P(),
            P(),
        ),
        out_specs=(P("grp", "brick", None, None, None), P("grp", "brick", None, None, None)),
        check_vma=False,
    )
```

```python
import functools

import jax
import jax.numpy as jnp
from jax import lax
from jax.experimental import pallas as pl
from jax.experimental.pallas import tpu as pltpu
from jax.sharding import PartitionSpec as P

MESH_IDS = pl.DeviceIdType.MESH

BS = 32
PATCH_X = 1
PATCH_Y = 2
ITERS = 3


OMEGA = 0.6


def allsum2_kernel(x_ref, o_ref, landed_b, landed_g, send_b, recv_b, send_g, recv_g):
    here_brick = lax.axis_index("brick")
    here_grp = lax.axis_index("grp")
    n_brick = landed_b.shape[0]
    n_grp = landed_g.shape[0]
    brick_peers = [(lax.rem(here_brick + k, n_brick), here_grp) for k in range(1, n_brick)]
    grp_peers = [(here_brick, lax.rem(here_grp + k, n_grp)) for k in range(1, n_grp)]
    barrier = pltpu.get_barrier_semaphore()
    for peer in brick_peers + grp_peers:
        pl.semaphore_signal(barrier, inc=1, device_id=peer, device_id_type=MESH_IDS)
    pl.semaphore_wait(barrier, len(brick_peers) + len(grp_peers))

    def exchange(src, landed, sends, recvs, peers):
        copies = []
        for k, peer in enumerate(peers, start=1):
            copy = pltpu.make_async_remote_copy(
                src_ref=src,
                dst_ref=landed.at[k],
                send_sem=sends.at[k],
                recv_sem=recvs.at[k],
                device_id=peer,
                device_id_type=MESH_IDS,
            )
            copy.start()
            copies.append(copy)
        for copy in copies:
            copy.wait()

    landed_b[0] = x_ref[...]
    exchange(x_ref, landed_b, send_b, recv_b, brick_peers)
    total = landed_b[lax.rem(here_brick, n_brick)]
    for j in range(1, n_brick):
        total = total + landed_b[lax.rem(here_brick + n_brick - j, n_brick)]
    o_ref[...] = total
    landed_g[0] = total
    exchange(o_ref, landed_g, send_g, recv_g, grp_peers)
    total = landed_g[lax.rem(here_grp, n_grp)]
    for j in range(1, n_grp):
        total = total + landed_g[lax.rem(here_grp + n_grp - j, n_grp)]
    o_ref[...] = total


def allsum2_tile(tile, kernel_id):
    n_brick = lax.axis_size("brick")
    n_grp = lax.axis_size("grp")
    return pl.pallas_call(
        allsum2_kernel,
        out_shape=jax.ShapeDtypeStruct(tile.shape, jnp.float32),
        in_specs=[pl.BlockSpec(memory_space=pltpu.VMEM)],
        out_specs=pl.BlockSpec(memory_space=pltpu.VMEM),
        scratch_shapes=[
            pltpu.VMEM((n_brick,) + tile.shape, jnp.float32),
            pltpu.VMEM((n_grp,) + tile.shape, jnp.float32),
            pltpu.SemaphoreType.DMA((n_brick,)),
            pltpu.SemaphoreType.DMA((n_brick,)),
            pltpu.SemaphoreType.DMA((n_grp,)),
            pltpu.SemaphoreType.DMA((n_grp,)),
        ],
        compiler_params=pltpu.CompilerParams(collective_id=kernel_id, has_side_effects=True),
    )(tile)


def extended_2(block, sides, width):
    for axis, dim in sides:
        count = lax.axis_size(axis)
        forward = [(i, i + 1) for i in range(count - 1)]
        backward = [(target, source) for source, target in forward]
        low = lax.ppermute(
            lax.slice_in_dim(block, block.shape[dim] - width, None, axis=dim), axis, forward
        )
        high = lax.ppermute(lax.slice_in_dim(block, 0, width, axis=dim), axis, backward)
        block = jnp.concatenate([low, block, high], axis=dim)
    return block


def assemble(coarse_diag, couplings, strides):
    extent = coarse_diag.shape[0]
    matrix = jnp.diag(coarse_diag)
    for coupling, stride in zip(couplings, strides):
        banded = coupling[: extent - stride]
        matrix = matrix - jnp.diag(banded, stride) - jnp.diag(banded, -stride)
    return matrix


def pad_rows(block, capacity):
    return jnp.pad(block, ((0, capacity - block.shape[0]), (0, 0)))


def on_device(source, uptake, conductance, occupancy, assignment):
    face_size = BS * BS
    capacity = max(PATCH_X, PATCH_Y)
    slot_count = PATCH_X * PATCH_Y
    slab_index = lax.axis_index("grp")
    brick_index = lax.axis_index("brick")
    brick_count = lax.axis_size("brick")
    across = brick_count // 2
    peer_ids = jnp.arange(brick_count, dtype=jnp.int32)
    patch_index = assignment[brick_index]
    patch_row = patch_index // across
    patch_column = patch_index % across

    def owner_of(row_shift, column_shift):
        row_target = patch_row + row_shift
        column_target = patch_column + column_shift
        inside = (
            (row_target >= 0) & (row_target < 2) & (column_target >= 0) & (column_target < across)
        )
        holder = jnp.sum(jnp.where(assignment == row_target * across + column_target, peer_ids, 0))
        return jnp.where(inside, holder, -1)

    wanted = jnp.stack([owner_of(1, 0), owner_of(-1, 0), owner_of(0, 1), owner_of(0, -1)])
    padded = jnp.pad(occupancy, 1)
    window = lax.dynamic_slice(
        padded,
        (slab_index, patch_row * PATCH_X, patch_column * PATCH_Y),
        (3, PATCH_X + 2, PATCH_Y + 2),
    ).astype(jnp.float32)
    centre = window[1, 1:-1, 1:-1].reshape(slot_count)
    toward = [
        window[1, 2:, 1:-1],
        window[1, :-2, 1:-1],
        window[1, 1:-1, 2:],
        window[1, 1:-1, :-2],
        window[2, 1:-1, 1:-1],
        window[0, 1:-1, 1:-1],
    ]
    first_axis = lax.broadcasted_iota(jnp.int32, (1, BS, face_size), 1)
    flat_axis = lax.broadcasted_iota(jnp.int32, (1, BS, face_size), 2)
    second_axis = flat_axis // BS
    third_axis = flat_axis % BS
    cube_third = lax.broadcasted_iota(jnp.int32, (1, BS, BS, BS), 3)
    borders = [
        first_axis == BS - 1,
        first_axis == 0,
        second_axis == BS - 1,
        second_axis == 0,
        third_axis == BS - 1,
        third_axis == 0,
    ]
    bonds = conductance[0, 0]
    live_here = centre[:, None, None]
    effective = []
    for direction in range(6):
        neighbour_live = toward[direction].reshape(slot_count)[:, None, None]
        active = jnp.where(borders[direction], live_here * neighbour_live, live_here)
        effective.append(bonds[direction] * active)
    absorb = uptake[0, 0]
    diagonal = absorb
    for direction in range(6):
        diagonal = diagonal + effective[direction]

    def apply_operator(field):
        lower_x = field[:, 0, :]
        upper_x = field[:, BS - 1, :]
        lower_y = field[:, :, :BS].reshape(slot_count, face_size)
        upper_y = field[:, :, face_size - BS :].reshape(slot_count, face_size)
        cube = field.reshape(slot_count, BS, BS, BS)
        lower_z = cube[:, :, :, 0].reshape(slot_count, face_size)
        upper_z = cube[:, :, :, BS - 1].reshape(slot_count, face_size)
        grid_lower_x = lower_x.reshape(PATCH_X, PATCH_Y, face_size)
        grid_upper_x = upper_x.reshape(PATCH_X, PATCH_Y, face_size)
        grid_lower_y = lower_y.reshape(PATCH_X, PATCH_Y, face_size)
        grid_upper_y = upper_y.reshape(PATCH_X, PATCH_Y, face_size)
        outgoing_sides = jnp.stack(
            [
                pad_rows(grid_lower_x[0], capacity),
                pad_rows(grid_upper_x[PATCH_X - 1], capacity),
                pad_rows(grid_lower_y[:, 0], capacity),
                pad_rows(grid_upper_y[:, PATCH_Y - 1], capacity),
            ]
        )
        portion = lax.all_gather(outgoing_sides[None], "brick", axis=0, tiled=True)
        sources = jnp.arange(portion.shape[0], dtype=jnp.int32)
        matches = sources[:, None] == wanted[None, :]
        remote = jnp.zeros((4, capacity, face_size), jnp.float32) + jnp.sum(
            jnp.where(matches[:, :, None, None], portion, 0.0), axis=0
        )
        stacked = jnp.stack([lower_z, upper_z])
        extended = extended_2(stacked, (("grp", 0),), 1)
        from_below = extended[0].reshape(slot_count, BS, BS, 1)
        from_above = extended[3].reshape(slot_count, BS, BS, 1)
        beyond_xplus = jnp.concatenate(
            [grid_lower_x[1:], remote[0, :PATCH_Y][None]], axis=0
        ).reshape(slot_count, face_size)
        beyond_xminus = jnp.concatenate(
            [remote[1, :PATCH_Y][None], grid_upper_x[:-1]], axis=0
        ).reshape(slot_count, face_size)
        beyond_yplus = jnp.concatenate(
            [grid_lower_y[:, 1:], remote[2, :PATCH_X][:, None]], axis=1
        ).reshape(slot_count, BS, BS)
        beyond_yminus = jnp.concatenate(
            [remote[3, :PATCH_X][:, None], grid_upper_y[:, :-1]], axis=1
        ).reshape(slot_count, BS, BS)
        upper_neighbour = jnp.where(
            cube_third == BS - 1, from_above, jnp.roll(cube, -1, axis=3)
        ).reshape(slot_count, BS, face_size)
        lower_neighbour = jnp.where(cube_third == 0, from_below, jnp.roll(cube, 1, axis=3)).reshape(
            slot_count, BS, face_size
        )
        total = diagonal * field
        total = total - effective[0] * jnp.concatenate(
            [field[:, 1:, :], beyond_xplus[:, None, :]], axis=1
        )
        total = total - effective[1] * jnp.concatenate(
            [beyond_xminus[:, None, :], field[:, :-1, :]], axis=1
        )
        total = total - effective[2] * jnp.concatenate([field[:, :, BS:], beyond_yplus], axis=2)
        total = total - effective[3] * jnp.concatenate(
            [beyond_yminus, field[:, :, : face_size - BS]], axis=2
        )
        total = total - effective[4] * upper_neighbour
        total = total - effective[5] * lower_neighbour
        return total

    slot_ids = jnp.arange(slot_count)
    brick_first = slot_ids // PATCH_Y
    brick_second = slot_ids % PATCH_Y
    inside = [
        (brick_first < PATCH_X - 1).astype(jnp.float32),
        (brick_first > 0).astype(jnp.float32),
        (brick_second < PATCH_Y - 1).astype(jnp.float32),
        (brick_second > 0).astype(jnp.float32),
    ]
    face_sums = [
        jnp.sum(effective[0][:, BS - 1, :], axis=1),
        jnp.sum(effective[1][:, 0, :], axis=1),
        jnp.sum(effective[2][:, :, face_size - BS :], axis=(1, 2)),
        jnp.sum(effective[3][:, :, :BS], axis=(1, 2)),
        jnp.sum(effective[4].reshape(slot_count, BS, BS, BS)[:, :, :, BS - 1], axis=(1, 2)),
        jnp.sum(effective[5].reshape(slot_count, BS, BS, BS)[:, :, :, 0], axis=(1, 2)),
    ]
    coarse_diag = jnp.sum(absorb, axis=(1, 2))
    for direction in range(4):
        coarse_diag = coarse_diag + face_sums[direction] * inside[direction]
    coarse_diag = coarse_diag + face_sums[4] + face_sums[5]
    grp_count = lax.axis_size("grp")
    grp_ids = jnp.arange(grp_count, dtype=jnp.int32)

    def butterfly(values, axes):
        for axis in axes:
            count = lax.axis_size(axis)
            if count & (count - 1):
                values = lax.psum(values, axis)
                continue
            stride = 1
            while stride < count:
                pairs = [(i, i ^ stride) for i in range(count)]
                values = values + lax.ppermute(values, axis, pairs)
                stride *= 2
        return values

    def slab_slot(values):
        here = (grp_ids == slab_index).astype(jnp.float32)
        return here[:, None, None] * values[None]

    forcing = source[0, 0] * live_here
    record = jnp.stack(
        [
            coarse_diag,
            face_sums[0] * inside[0],
            face_sums[2] * inside[2],
            face_sums[4],
            jnp.sum(forcing, axis=(1, 2)),
        ]
    )
    brick_here = (peer_ids == brick_index).astype(jnp.float32)
    spread = (brick_here[:, None, None, None] * slab_slot(record)[None]).reshape(-1)
    rows = -(-spread.shape[0] // 128)
    rows = -(-rows // 8) * 8
    tile = jnp.pad(spread, (0, rows * 128 - spread.shape[0])).reshape(rows, 128)
    summed = allsum2_tile(tile, 2).reshape(-1)[: spread.shape[0]]
    gathered = lax.dynamic_index_in_dim(
        summed.reshape(brick_count, grp_count, 5, slot_count), brick_index, keepdims=False
    )
    columns = jnp.transpose(gathered, (1, 0, 2)).reshape(5, -1)
    matrix = assemble(columns[0], (columns[1], columns[2], columns[3]), (PATCH_Y, 1, slot_count))
    factor = jnp.linalg.cholesky(matrix)

    def coarse_solve(terms):
        middle = lax.linalg.triangular_solve(factor, terms[:, None], left_side=True, lower=True)
        result = lax.linalg.triangular_solve(
            factor, middle, left_side=True, lower=True, transpose_a=True
        )
        return lax.dynamic_slice_in_dim(result[:, 0], slab_index * slot_count, slot_count)

    def precondition(residual_field, terms):
        smoothed = OMEGA * residual_field / diagonal
        smoothed = smoothed + OMEGA * (residual_field - apply_operator(smoothed)) / diagonal
        return smoothed + coarse_solve(terms)[:, None, None]

    def allsum(values):
        rows = -(-values.shape[0] // 128)
        rows = -(-rows // 8) * 8
        tile = jnp.pad(values, (0, rows * 128 - values.shape[0])).reshape(rows, 128)
        return allsum2_tile(tile, 1).reshape(-1)[: values.shape[0]]

    def dot_and_sums(product, field):
        sums = slab_slot(jnp.sum(field, axis=(1, 2))[None])[:, 0]
        spread = brick_here[:, None, None] * sums[None]
        packed = jnp.concatenate([jnp.sum(product)[None], spread.reshape(-1)])
        total = allsum(packed)
        mine = lax.dynamic_index_in_dim(
            total[1:].reshape(brick_count, -1), brick_index, keepdims=False
        )
        return total[0], mine

    def global_sum(values):
        return allsum(jnp.sum(values)[None])[0]

    terms = columns[4]
    solution_field = jnp.zeros_like(forcing)
    residual = forcing
    search = precondition(residual, terms)
    energy = global_sum(residual * search)
    for iteration in range(ITERS):
        mapped = apply_operator(search)
        curvature, mapped_terms = dot_and_sums(search * mapped, mapped)
        step_size = energy / curvature
        solution_field = solution_field + step_size * search
        residual = residual - step_size * mapped
        if iteration + 1 < ITERS:
            terms = terms - step_size * mapped_terms
            smoothed = precondition(residual, terms)
            renewed = global_sum(residual * smoothed)
            search = smoothed + renewed / energy * search
            energy = renewed
    return (solution_field[None, None], residual[None, None])


def solution(mesh):
    return jax.shard_map(
        on_device,
        mesh=mesh,
        in_specs=(
            P("grp", "brick", None, None, None),
            P("grp", "brick", None, None, None),
            P("grp", "brick", None, None, None, None),
            P(),
            P(),
        ),
        out_specs=(P("grp", "brick", None, None, None), P("grp", "brick", None, None, None)),
        check_vma=False,
    )
```

```python
import functools

import jax
import jax.numpy as jnp
from jax import lax
from jax.experimental import pallas as pl
from jax.experimental.pallas import tpu as pltpu
from jax.sharding import PartitionSpec as P

MESH_IDS = pl.DeviceIdType.MESH

BS = 32
PATCH_X = 1
PATCH_Y = 2
ITERS = 3


OMEGA = 0.6


def allsum2_kernel(x_ref, o_ref, landed_b, landed_g, send_b, recv_b, send_g, recv_g):
    here_brick = lax.axis_index("brick")
    here_grp = lax.axis_index("grp")
    n_brick = landed_b.shape[0]
    n_grp = landed_g.shape[0]
    brick_peers = [(lax.rem(here_brick + k, n_brick), here_grp) for k in range(1, n_brick)]
    grp_peers = [(here_brick, lax.rem(here_grp + k, n_grp)) for k in range(1, n_grp)]
    barrier = pltpu.get_barrier_semaphore()
    for peer in brick_peers + grp_peers:
        pl.semaphore_signal(barrier, inc=1, device_id=peer, device_id_type=MESH_IDS)
    pl.semaphore_wait(barrier, len(brick_peers) + len(grp_peers))

    def exchange(src, landed, sends, recvs, peers):
        copies = []
        for k, peer in enumerate(peers, start=1):
            copy = pltpu.make_async_remote_copy(
                src_ref=src,
                dst_ref=landed.at[k],
                send_sem=sends.at[k],
                recv_sem=recvs.at[k],
                device_id=peer,
                device_id_type=MESH_IDS,
            )
            copy.start()
            copies.append(copy)
        for copy in copies:
            copy.wait()

    landed_b[0] = x_ref[...]
    exchange(x_ref, landed_b, send_b, recv_b, brick_peers)
    total = landed_b[lax.rem(here_brick, n_brick)]
    for j in range(1, n_brick):
        total = total + landed_b[lax.rem(here_brick + n_brick - j, n_brick)]
    o_ref[...] = total
    landed_g[0] = total
    exchange(o_ref, landed_g, send_g, recv_g, grp_peers)
    total = landed_g[lax.rem(here_grp, n_grp)]
    for j in range(1, n_grp):
        total = total + landed_g[lax.rem(here_grp + n_grp - j, n_grp)]
    o_ref[...] = total


def allsum2_tile(tile, kernel_id):
    n_brick = lax.axis_size("brick")
    n_grp = lax.axis_size("grp")
    return pl.pallas_call(
        allsum2_kernel,
        out_shape=jax.ShapeDtypeStruct(tile.shape, jnp.float32),
        in_specs=[pl.BlockSpec(memory_space=pltpu.VMEM)],
        out_specs=pl.BlockSpec(memory_space=pltpu.VMEM),
        scratch_shapes=[
            pltpu.VMEM((n_brick,) + tile.shape, jnp.float32),
            pltpu.VMEM((n_grp,) + tile.shape, jnp.float32),
            pltpu.SemaphoreType.DMA((n_brick,)),
            pltpu.SemaphoreType.DMA((n_brick,)),
            pltpu.SemaphoreType.DMA((n_grp,)),
            pltpu.SemaphoreType.DMA((n_grp,)),
        ],
        compiler_params=pltpu.CompilerParams(collective_id=kernel_id, has_side_effects=True),
    )(tile)


def stencil_kernel(f_ref, eff_ref, diag_ref, rows_ref, faces_ref, o_ref):
    slots, width, lanes = f_ref.shape
    row = lax.broadcasted_iota(jnp.int32, (width, lanes), 0)
    lane = lax.broadcasted_iota(jnp.int32, (width, lanes), 1)
    pick = lax.broadcasted_iota(jnp.int32, (BS, lanes), 0)
    spot = lax.broadcasted_iota(jnp.int32, (BS, lanes), 1)
    spread_z = (spot // BS == pick).astype(jnp.float32)
    spread_y = (spot % BS == pick).astype(jnp.float32)

    def spread(face, table):
        return jnp.dot(face, table, precision=lax.Precision.HIGHEST, preferred_element_type=jnp.float32)

    for s in range(slots):
        fs = f_ref[s]
        xp = jnp.where(row == width - 1, rows_ref[0, s], pltpu.roll(fs, width - 1, 0))
        xm = jnp.where(row == 0, rows_ref[1, s], pltpu.roll(fs, 1, 0))
        yp = jnp.where(lane >= lanes - BS, spread(faces_ref[0, s], spread_y), pltpu.roll(fs, lanes - BS, 1))
        ym = jnp.where(lane < BS, spread(faces_ref[1, s], spread_y), pltpu.roll(fs, BS, 1))
        zp = jnp.where(lane % BS == BS - 1, spread(faces_ref[2, s], spread_z), pltpu.roll(fs, lanes - 1, 1))
        zm = jnp.where(lane % BS == 0, spread(faces_ref[3, s], spread_z), pltpu.roll(fs, 1, 1))
        total = diag_ref[s] * fs
        total = total - eff_ref[0, s] * xp
        total = total - eff_ref[1, s] * xm
        total = total - eff_ref[2, s] * yp
        total = total - eff_ref[3, s] * ym
        total = total - eff_ref[4, s] * zp
        total = total - eff_ref[5, s] * zm
        o_ref[s] = total


def stencil(field, eff, diag, rows, faces):
    vmem = pl.BlockSpec(memory_space=pltpu.VMEM)
    return pl.pallas_call(
        stencil_kernel,
        out_shape=jax.ShapeDtypeStruct(field.shape, jnp.float32),
        in_specs=[vmem] * 5,
        out_specs=vmem,
    )(field, eff, diag, rows, faces)


def extended_2(block, sides, width):
    for axis, dim in sides:
        count = lax.axis_size(axis)
        forward = [(i, i + 1) for i in range(count - 1)]
        backward = [(target, source) for source, target in forward]
        low = lax.ppermute(
            lax.slice_in_dim(block, block.shape[dim] - width, None, axis=dim), axis, forward
        )
        high = lax.ppermute(lax.slice_in_dim(block, 0, width, axis=dim), axis, backward)
        block = jnp.concatenate([low, block, high], axis=dim)
    return block


def assemble(coarse_diag, couplings, strides):
    extent = coarse_diag.shape[0]
    matrix = jnp.diag(coarse_diag)
    for coupling, stride in zip(couplings, strides):
        banded = coupling[: extent - stride]
        matrix = matrix - jnp.diag(banded, stride) - jnp.diag(banded, -stride)
    return matrix


def pad_rows(block, capacity):
    return jnp.pad(block, ((0, capacity - block.shape[0]), (0, 0)))


def on_device(source, uptake, conductance, occupancy, assignment):
    face_size = BS * BS
    capacity = max(PATCH_X, PATCH_Y)
    slot_count = PATCH_X * PATCH_Y
    slab_index = lax.axis_index("grp")
    brick_index = lax.axis_index("brick")
    brick_count = lax.axis_size("brick")
    across = brick_count // 2
    peer_ids = jnp.arange(brick_count, dtype=jnp.int32)
    patch_index = assignment[brick_index]
    patch_row = patch_index // across
    patch_column = patch_index % across

    def owner_of(row_shift, column_shift):
        row_target = patch_row + row_shift
        column_target = patch_column + column_shift
        inside = (
            (row_target >= 0) & (row_target < 2) & (column_target >= 0) & (column_target < across)
        )
        holder = jnp.sum(jnp.where(assignment == row_target * across + column_target, peer_ids, 0))
        return jnp.where(inside, holder, -1)

    wanted = jnp.stack([owner_of(1, 0), owner_of(-1, 0), owner_of(0, 1), owner_of(0, -1)])
    padded = jnp.pad(occupancy, 1)
    window = lax.dynamic_slice(
        padded,
        (slab_index, patch_row * PATCH_X, patch_column * PATCH_Y),
        (3, PATCH_X + 2, PATCH_Y + 2),
    ).astype(jnp.float32)
    centre = window[1, 1:-1, 1:-1].reshape(slot_count)
    toward = [
        window[1, 2:, 1:-1],
        window[1, :-2, 1:-1],
        window[1, 1:-1, 2:],
        window[1, 1:-1, :-2],
        window[2, 1:-1, 1:-1],
        window[0, 1:-1, 1:-1],
    ]
    first_axis = lax.broadcasted_iota(jnp.int32, (1, BS, face_size), 1)
    flat_axis = lax.broadcasted_iota(jnp.int32, (1, BS, face_size), 2)
    second_axis = flat_axis // BS
    third_axis = flat_axis % BS
    cube_third = lax.broadcasted_iota(jnp.int32, (1, BS, BS, BS), 3)
    borders = [
        first_axis == BS - 1,
        first_axis == 0,
        second_axis == BS - 1,
        second_axis == 0,
        third_axis == BS - 1,
        third_axis == 0,
    ]
    bonds = conductance[0, 0]
    live_here = centre[:, None, None]
    effective = []
    for direction in range(6):
        neighbour_live = toward[direction].reshape(slot_count)[:, None, None]
        active = jnp.where(borders[direction], live_here * neighbour_live, live_here)
        effective.append(bonds[direction] * active)
    absorb = uptake[0, 0]
    diagonal = absorb
    for direction in range(6):
        diagonal = diagonal + effective[direction]

    stacked_effective = jnp.stack(effective)

    def apply_operator(field):
        lower_x = field[:, 0, :]
        upper_x = field[:, BS - 1, :]
        lower_y = field[:, :, :BS].reshape(slot_count, face_size)
        upper_y = field[:, :, face_size - BS :].reshape(slot_count, face_size)
        cube = field.reshape(slot_count, BS, BS, BS)
        lower_z = cube[:, :, :, 0].reshape(slot_count, face_size)
        upper_z = cube[:, :, :, BS - 1].reshape(slot_count, face_size)
        grid_lower_x = lower_x.reshape(PATCH_X, PATCH_Y, face_size)
        grid_upper_x = upper_x.reshape(PATCH_X, PATCH_Y, face_size)
        grid_lower_y = lower_y.reshape(PATCH_X, PATCH_Y, face_size)
        grid_upper_y = upper_y.reshape(PATCH_X, PATCH_Y, face_size)
        outgoing_sides = jnp.stack(
            [
                pad_rows(grid_lower_x[0], capacity),
                pad_rows(grid_upper_x[PATCH_X - 1], capacity),
                pad_rows(grid_lower_y[:, 0], capacity),
                pad_rows(grid_upper_y[:, PATCH_Y - 1], capacity),
            ]
        )
        portion = lax.all_gather(outgoing_sides[None], "brick", axis=0, tiled=True)
        sources = jnp.arange(portion.shape[0], dtype=jnp.int32)
        matches = sources[:, None] == wanted[None, :]
        remote = jnp.zeros((4, capacity, face_size), jnp.float32) + jnp.sum(
            jnp.where(matches[:, :, None, None], portion, 0.0), axis=0
        )
        stacked = jnp.stack([lower_z, upper_z])
        extended = extended_2(stacked, (("grp", 0),), 1)
        from_below = extended[0].reshape(slot_count, BS, BS, 1)
        from_above = extended[3].reshape(slot_count, BS, BS, 1)
        beyond_xplus = jnp.concatenate(
            [grid_lower_x[1:], remote[0, :PATCH_Y][None]], axis=0
        ).reshape(slot_count, face_size)
        beyond_xminus = jnp.concatenate(
            [remote[1, :PATCH_Y][None], grid_upper_x[:-1]], axis=0
        ).reshape(slot_count, face_size)
        beyond_yplus = jnp.concatenate(
            [grid_lower_y[:, 1:], remote[2, :PATCH_X][:, None]], axis=1
        ).reshape(slot_count, BS, BS)
        beyond_yminus = jnp.concatenate(
            [remote[3, :PATCH_X][:, None], grid_upper_y[:, :-1]], axis=1
        ).reshape(slot_count, BS, BS)
        rows = jnp.stack([beyond_xplus, beyond_xminus])[:, :, None, :]
        faces = jnp.stack(
            [
                beyond_yplus,
                beyond_yminus,
                from_above.reshape(slot_count, BS, BS),
                from_below.reshape(slot_count, BS, BS),
            ]
        )
        return stencil(field, stacked_effective, diagonal, rows, faces)

    slot_ids = jnp.arange(slot_count)
    brick_first = slot_ids // PATCH_Y
    brick_second = slot_ids % PATCH_Y
    inside = [
        (brick_first < PATCH_X - 1).astype(jnp.float32),
        (brick_first > 0).astype(jnp.float32),
        (brick_second < PATCH_Y - 1).astype(jnp.float32),
        (brick_second > 0).astype(jnp.float32),
    ]
    face_sums = [
        jnp.sum(effective[0][:, BS - 1, :], axis=1),
        jnp.sum(effective[1][:, 0, :], axis=1),
        jnp.sum(effective[2][:, :, face_size - BS :], axis=(1, 2)),
        jnp.sum(effective[3][:, :, :BS], axis=(1, 2)),
        jnp.sum(effective[4].reshape(slot_count, BS, BS, BS)[:, :, :, BS - 1], axis=(1, 2)),
        jnp.sum(effective[5].reshape(slot_count, BS, BS, BS)[:, :, :, 0], axis=(1, 2)),
    ]
    coarse_diag = jnp.sum(absorb, axis=(1, 2))
    for direction in range(4):
        coarse_diag = coarse_diag + face_sums[direction] * inside[direction]
    coarse_diag = coarse_diag + face_sums[4] + face_sums[5]
    grp_count = lax.axis_size("grp")
    grp_ids = jnp.arange(grp_count, dtype=jnp.int32)

    def butterfly(values, axes):
        for axis in axes:
            count = lax.axis_size(axis)
            if count & (count - 1):
                values = lax.psum(values, axis)
                continue
            stride = 1
            while stride < count:
                pairs = [(i, i ^ stride) for i in range(count)]
                values = values + lax.ppermute(values, axis, pairs)
                stride *= 2
        return values

    def slab_slot(values):
        here = (grp_ids == slab_index).astype(jnp.float32)
        return here[:, None, None] * values[None]

    forcing = source[0, 0] * live_here
    record = jnp.stack(
        [
            coarse_diag,
            face_sums[0] * inside[0],
            face_sums[2] * inside[2],
            face_sums[4],
            jnp.sum(forcing, axis=(1, 2)),
        ]
    )
    brick_here = (peer_ids == brick_index).astype(jnp.float32)
    spread = (brick_here[:, None, None, None] * slab_slot(record)[None]).reshape(-1)
    rows = -(-spread.shape[0] // 128)
    rows = -(-rows // 8) * 8
    tile = jnp.pad(spread, (0, rows * 128 - spread.shape[0])).reshape(rows, 128)
    summed = allsum2_tile(tile, 2).reshape(-1)[: spread.shape[0]]
    gathered = lax.dynamic_index_in_dim(
        summed.reshape(brick_count, grp_count, 5, slot_count), brick_index, keepdims=False
    )
    columns = jnp.transpose(gathered, (1, 0, 2)).reshape(5, -1)
    matrix = assemble(columns[0], (columns[1], columns[2], columns[3]), (PATCH_Y, 1, slot_count))
    factor = jnp.linalg.cholesky(matrix)

    def coarse_solve(terms):
        middle = lax.linalg.triangular_solve(factor, terms[:, None], left_side=True, lower=True)
        result = lax.linalg.triangular_solve(
            factor, middle, left_side=True, lower=True, transpose_a=True
        )
        return lax.dynamic_slice_in_dim(result[:, 0], slab_index * slot_count, slot_count)

    def precondition(residual_field, terms):
        smoothed = OMEGA * residual_field / diagonal
        smoothed = smoothed + OMEGA * (residual_field - apply_operator(smoothed)) / diagonal
        return smoothed + coarse_solve(terms)[:, None, None]

    def allsum(values):
        rows = -(-values.shape[0] // 128)
        rows = -(-rows // 8) * 8
        tile = jnp.pad(values, (0, rows * 128 - values.shape[0])).reshape(rows, 128)
        return allsum2_tile(tile, 1).reshape(-1)[: values.shape[0]]

    def dot_and_sums(product, field):
        sums = slab_slot(jnp.sum(field, axis=(1, 2))[None])[:, 0]
        spread = brick_here[:, None, None] * sums[None]
        packed = jnp.concatenate([jnp.sum(product)[None], spread.reshape(-1)])
        total = allsum(packed)
        mine = lax.dynamic_index_in_dim(
            total[1:].reshape(brick_count, -1), brick_index, keepdims=False
        )
        return total[0], mine

    def global_sum(values):
        return allsum(jnp.sum(values)[None])[0]

    terms = columns[4]
    solution_field = jnp.zeros_like(forcing)
    residual = forcing
    search = precondition(residual, terms)
    energy = global_sum(residual * search)
    for iteration in range(ITERS):
        mapped = apply_operator(search)
        curvature, mapped_terms = dot_and_sums(search * mapped, mapped)
        step_size = energy / curvature
        solution_field = solution_field + step_size * search
        residual = residual - step_size * mapped
        if iteration + 1 < ITERS:
            terms = terms - step_size * mapped_terms
            smoothed = precondition(residual, terms)
            renewed = global_sum(residual * smoothed)
            search = smoothed + renewed / energy * search
            energy = renewed
    return (solution_field[None, None], residual[None, None])


def solution(mesh):
    return jax.shard_map(
        on_device,
        mesh=mesh,
        in_specs=(
            P("grp", "brick", None, None, None),
            P("grp", "brick", None, None, None),
            P("grp", "brick", None, None, None, None),
            P(),
            P(),
        ),
        out_specs=(P("grp", "brick", None, None, None), P("grp", "brick", None, None, None)),
        check_vma=False,
    )
```

```python
import functools

import jax
import jax.numpy as jnp
from jax import lax
from jax.experimental import pallas as pl
from jax.experimental.pallas import tpu as pltpu
from jax.sharding import PartitionSpec as P

MESH_IDS = pl.DeviceIdType.MESH

BS = 32
PATCH_X = 1
PATCH_Y = 2
ITERS = 3


OMEGA = 0.6


def exchange_kernel(
    x_ref, xy_ref, z_ref, o_ref, xy_out, z_out,
    landed_b, landed_g, landed_xy, landed_z,
    send_b, recv_b, send_g, recv_g, send_xy, recv_xy, send_z, recv_z,
):
    here_brick = lax.axis_index("brick")
    here_grp = lax.axis_index("grp")
    n_brick = landed_b.shape[0]
    n_grp = landed_g.shape[0]
    brick_peers = [(lax.rem(here_brick + k, n_brick), here_grp) for k in range(1, n_brick)]
    grp_peers = [(here_brick, lax.rem(here_grp + k, n_grp)) for k in range(1, n_grp)]
    barrier = pltpu.get_barrier_semaphore()
    for peer in brick_peers + grp_peers:
        pl.semaphore_signal(barrier, inc=1, device_id=peer, device_id_type=MESH_IDS)
    pl.semaphore_wait(barrier, len(brick_peers) + len(grp_peers))

    def send(src, dst, sends, recvs, index, peer):
        copy = pltpu.make_async_remote_copy(
            src_ref=src,
            dst_ref=dst.at[index],
            send_sem=sends.at[index],
            recv_sem=recvs.at[index],
            device_id=peer,
            device_id_type=MESH_IDS,
        )
        copy.start()
        return copy

    face_copies = [
        send(z_ref, landed_z, send_z, recv_z, 0, grp_peers[0]),
        send(z_ref, landed_z, send_z, recv_z, 1, grp_peers[-1]),
    ]
    face_copies += [
        send(xy_ref, landed_xy, send_xy, recv_xy, k, peer)
        for k, peer in enumerate(brick_peers, start=1)
    ]
    copies = [
        send(x_ref, landed_b, send_b, recv_b, k, peer)
        for k, peer in enumerate(brick_peers, start=1)
    ]
    landed_b[0] = x_ref[...]
    for copy in copies:
        copy.wait()
    total = landed_b[lax.rem(here_brick, n_brick)]
    for j in range(1, n_brick):
        total = total + landed_b[lax.rem(here_brick + n_brick - j, n_brick)]
    o_ref[...] = total
    landed_g[0] = total
    copies = [
        send(o_ref, landed_g, send_g, recv_g, k, peer)
        for k, peer in enumerate(grp_peers, start=1)
    ]
    for copy in copies:
        copy.wait()
    total = landed_g[lax.rem(here_grp, n_grp)]
    for j in range(1, n_grp):
        total = total + landed_g[lax.rem(here_grp + n_grp - j, n_grp)]
    o_ref[...] = total
    for copy in face_copies:
        copy.wait()
    landed_xy[0] = xy_ref[...]
    xy_out[...] = landed_xy[...]
    z_out[...] = landed_z[...]


def exchange(tile, xy, z, kernel_id):
    n_brick = lax.axis_size("brick")
    n_grp = lax.axis_size("grp")
    vmem = pl.BlockSpec(memory_space=pltpu.VMEM)
    dma = pltpu.SemaphoreType.DMA
    return pl.pallas_call(
        exchange_kernel,
        out_shape=(
            jax.ShapeDtypeStruct(tile.shape, jnp.float32),
            jax.ShapeDtypeStruct((n_brick,) + xy.shape, jnp.float32),
            jax.ShapeDtypeStruct((2,) + z.shape, jnp.float32),
        ),
        in_specs=[vmem] * 3,
        out_specs=(vmem, vmem, vmem),
        scratch_shapes=[
            pltpu.VMEM((n_brick,) + tile.shape, jnp.float32),
            pltpu.VMEM((n_grp,) + tile.shape, jnp.float32),
            pltpu.VMEM((n_brick,) + xy.shape, jnp.float32),
            pltpu.VMEM((2,) + z.shape, jnp.float32),
            dma((n_brick,)),
            dma((n_brick,)),
            dma((n_grp,)),
            dma((n_grp,)),
            dma((n_brick,)),
            dma((n_brick,)),
            dma((2,)),
            dma((2,)),
        ],
        compiler_params=pltpu.CompilerParams(collective_id=kernel_id, has_side_effects=True),
    )(tile, xy, z)


def stencil_kernel(f_ref, eff_ref, diag_ref, rows_ref, faces_ref, o_ref):
    slots, width, lanes = f_ref.shape
    row = lax.broadcasted_iota(jnp.int32, (width, lanes), 0)
    lane = lax.broadcasted_iota(jnp.int32, (width, lanes), 1)
    pick = lax.broadcasted_iota(jnp.int32, (BS, lanes), 0)
    spot = lax.broadcasted_iota(jnp.int32, (BS, lanes), 1)
    spread_z = (spot // BS == pick).astype(jnp.float32)
    spread_y = (spot % BS == pick).astype(jnp.float32)

    def spread(face, table):
        return jnp.dot(face, table, precision=lax.Precision.HIGHEST, preferred_element_type=jnp.float32)

    for s in range(slots):
        fs = f_ref[s]
        xp = jnp.where(row == width - 1, rows_ref[0, s], pltpu.roll(fs, width - 1, 0))
        xm = jnp.where(row == 0, rows_ref[1, s], pltpu.roll(fs, 1, 0))
        yp = jnp.where(lane >= lanes - BS, spread(faces_ref[0, s], spread_y), pltpu.roll(fs, lanes - BS, 1))
        ym = jnp.where(lane < BS, spread(faces_ref[1, s], spread_y), pltpu.roll(fs, BS, 1))
        zp = jnp.where(lane % BS == BS - 1, spread(faces_ref[2, s], spread_z), pltpu.roll(fs, lanes - 1, 1))
        zm = jnp.where(lane % BS == 0, spread(faces_ref[3, s], spread_z), pltpu.roll(fs, 1, 1))
        total = diag_ref[s] * fs
        total = total - eff_ref[0, s] * xp
        total = total - eff_ref[1, s] * xm
        total = total - eff_ref[2, s] * yp
        total = total - eff_ref[3, s] * ym
        total = total - eff_ref[4, s] * zp
        total = total - eff_ref[5, s] * zm
        o_ref[s] = total


def stencil(field, eff, diag, rows, faces):
    vmem = pl.BlockSpec(memory_space=pltpu.VMEM)
    return pl.pallas_call(
        stencil_kernel,
        out_shape=jax.ShapeDtypeStruct(field.shape, jnp.float32),
        in_specs=[vmem] * 5,
        out_specs=vmem,
    )(field, eff, diag, rows, faces)


def assemble(coarse_diag, couplings, strides):
    extent = coarse_diag.shape[0]
    matrix = jnp.diag(coarse_diag)
    for coupling, stride in zip(couplings, strides):
        banded = coupling[: extent - stride]
        matrix = matrix - jnp.diag(banded, stride) - jnp.diag(banded, -stride)
    return matrix


def on_device(source, uptake, conductance, occupancy, assignment):
    face_size = BS * BS
    slot_count = PATCH_X * PATCH_Y
    slab_index = lax.axis_index("grp")
    brick_index = lax.axis_index("brick")
    brick_count = lax.axis_size("brick")
    across = brick_count // 2
    peer_ids = jnp.arange(brick_count, dtype=jnp.int32)
    patch_index = assignment[brick_index]
    patch_row = patch_index // across
    patch_column = patch_index % across

    def owner_of(row_shift, column_shift):
        row_target = patch_row + row_shift
        column_target = patch_column + column_shift
        inside = (
            (row_target >= 0) & (row_target < 2) & (column_target >= 0) & (column_target < across)
        )
        holder = jnp.sum(jnp.where(assignment == row_target * across + column_target, peer_ids, 0))
        return jnp.where(inside, holder, -1)

    wanted = jnp.stack([owner_of(1, 0), owner_of(-1, 0), owner_of(0, 1), owner_of(0, -1)])
    padded = jnp.pad(occupancy, 1)
    window = lax.dynamic_slice(
        padded,
        (slab_index, patch_row * PATCH_X, patch_column * PATCH_Y),
        (3, PATCH_X + 2, PATCH_Y + 2),
    ).astype(jnp.float32)
    centre = window[1, 1:-1, 1:-1].reshape(slot_count)
    toward = [
        window[1, 2:, 1:-1],
        window[1, :-2, 1:-1],
        window[1, 1:-1, 2:],
        window[1, 1:-1, :-2],
        window[2, 1:-1, 1:-1],
        window[0, 1:-1, 1:-1],
    ]
    first_axis = lax.broadcasted_iota(jnp.int32, (1, BS, face_size), 1)
    flat_axis = lax.broadcasted_iota(jnp.int32, (1, BS, face_size), 2)
    second_axis = flat_axis // BS
    third_axis = flat_axis % BS
    cube_third = lax.broadcasted_iota(jnp.int32, (1, BS, BS, BS), 3)
    borders = [
        first_axis == BS - 1,
        first_axis == 0,
        second_axis == BS - 1,
        second_axis == 0,
        third_axis == BS - 1,
        third_axis == 0,
    ]
    bonds = conductance[0, 0]
    live_here = centre[:, None, None]
    effective = []
    for direction in range(6):
        neighbour_live = toward[direction].reshape(slot_count)[:, None, None]
        active = jnp.where(borders[direction], live_here * neighbour_live, live_here)
        effective.append(bonds[direction] * active)
    absorb = uptake[0, 0]
    diagonal = absorb
    for direction in range(6):
        diagonal = diagonal + effective[direction]

    stacked_effective = jnp.stack(effective)

    def side_faces(field):
        cube = field.reshape(slot_count, BS, BS, BS)
        xy = jnp.concatenate(
            [
                field[:, 0, :],
                field[:, BS - 1, :],
                field[0, :, :BS].reshape(1, face_size),
                field[slot_count - 1, :, face_size - BS :].reshape(1, face_size),
            ]
        )
        z = jnp.concatenate(
            [
                cube[:, :, :, 0].reshape(slot_count, face_size),
                cube[:, :, :, BS - 1].reshape(slot_count, face_size),
            ]
        )
        return xy, z

    def pick(landed, holder, fill):
        offset = lax.rem(brick_index - holder + brick_count, brick_count)
        got = lax.dynamic_index_in_dim(landed, offset, keepdims=False)
        return jnp.where(holder >= 0, got, fill)

    def halo(field, xy_land, z_land, fill):
        xplus = pick(xy_land, wanted[0], fill)
        xminus = pick(xy_land, wanted[1], fill)
        yplus = pick(xy_land, wanted[2], fill)
        yminus = pick(xy_land, wanted[3], fill)
        rows = jnp.stack([xplus[:slot_count], xminus[slot_count : 2 * slot_count]])[:, :, None, :]
        beyond_yplus = jnp.stack([field[1, :, :BS], yplus[2 * slot_count].reshape(BS, BS)])
        beyond_yminus = jnp.stack(
            [yminus[2 * slot_count + 1].reshape(BS, BS), field[0, :, face_size - BS :]]
        )
        above = jnp.where(slab_index < grp_count - 1, z_land[1, :slot_count], fill)
        below = jnp.where(slab_index > 0, z_land[0, slot_count:], fill)
        faces = jnp.stack(
            [
                beyond_yplus,
                beyond_yminus,
                above.reshape(slot_count, BS, BS),
                below.reshape(slot_count, BS, BS),
            ]
        )
        return rows, faces

    slot_ids = jnp.arange(slot_count)
    brick_first = slot_ids // PATCH_Y
    brick_second = slot_ids % PATCH_Y
    inside = [
        (brick_first < PATCH_X - 1).astype(jnp.float32),
        (brick_first > 0).astype(jnp.float32),
        (brick_second < PATCH_Y - 1).astype(jnp.float32),
        (brick_second > 0).astype(jnp.float32),
    ]
    face_sums = [
        jnp.sum(effective[0][:, BS - 1, :], axis=1),
        jnp.sum(effective[1][:, 0, :], axis=1),
        jnp.sum(effective[2][:, :, face_size - BS :], axis=(1, 2)),
        jnp.sum(effective[3][:, :, :BS], axis=(1, 2)),
        jnp.sum(effective[4].reshape(slot_count, BS, BS, BS)[:, :, :, BS - 1], axis=(1, 2)),
        jnp.sum(effective[5].reshape(slot_count, BS, BS, BS)[:, :, :, 0], axis=(1, 2)),
    ]
    coarse_diag = jnp.sum(absorb, axis=(1, 2))
    for direction in range(4):
        coarse_diag = coarse_diag + face_sums[direction] * inside[direction]
    coarse_diag = coarse_diag + face_sums[4] + face_sums[5]
    grp_count = lax.axis_size("grp")
    grp_ids = jnp.arange(grp_count, dtype=jnp.int32)

    def slab_slot(values):
        here = (grp_ids == slab_index).astype(jnp.float32)
        return here[:, None, None] * values[None]

    forcing = source[0, 0] * live_here

    def as_tile(values):
        rows = -(-values.shape[0] // 128)
        rows = -(-rows // 8) * 8
        return jnp.pad(values, (0, rows * 128 - values.shape[0])).reshape(rows, 128)

    record = jnp.stack(
        [
            coarse_diag,
            face_sums[0] * inside[0],
            face_sums[2] * inside[2],
            face_sums[4],
            jnp.sum(forcing, axis=(1, 2)),
        ]
    )
    brick_here = (peer_ids == brick_index).astype(jnp.float32)
    spread = (brick_here[:, None, None, None] * slab_slot(record)[None]).reshape(-1)
    forcing_xy, forcing_z = side_faces(forcing)
    diagonal_xy, diagonal_z = side_faces(diagonal)
    summed, xy_land, z_land = exchange(
        as_tile(spread),
        jnp.concatenate([forcing_xy, diagonal_xy]),
        jnp.concatenate([forcing_z, diagonal_z]),
        2,
    )
    summed = summed.reshape(-1)[: spread.shape[0]]
    xy_rows = forcing_xy.shape[0]
    z_rows = forcing_z.shape[0]
    residual_halo = halo(forcing, xy_land[:, :xy_rows], z_land[:, :z_rows], 0.0)
    diagonal_halo = halo(diagonal, xy_land[:, xy_rows:], z_land[:, z_rows:], 1.0)
    gathered = lax.dynamic_index_in_dim(
        summed.reshape(brick_count, grp_count, 5, slot_count), brick_index, keepdims=False
    )
    columns = jnp.transpose(gathered, (1, 0, 2)).reshape(5, -1)
    matrix = assemble(columns[0], (columns[1], columns[2], columns[3]), (PATCH_Y, 1, slot_count))
    factor = jnp.linalg.cholesky(matrix)

    def coarse_solve(terms):
        middle = lax.linalg.triangular_solve(factor, terms[:, None], left_side=True, lower=True)
        result = lax.linalg.triangular_solve(
            factor, middle, left_side=True, lower=True, transpose_a=True
        )
        return lax.dynamic_slice_in_dim(result[:, 0], slab_index * slot_count, slot_count)

    def precondition(residual_field, field_halo, terms):
        smoothed = OMEGA * residual_field / diagonal
        smoothed_halo = [OMEGA * part / scale for part, scale in zip(field_halo, diagonal_halo)]
        applied = stencil(smoothed, stacked_effective, diagonal, *smoothed_halo)
        smoothed = smoothed + OMEGA * (residual_field - applied) / diagonal
        return smoothed + coarse_solve(terms)[:, None, None]

    def sum_and_share(product, field, with_sums):
        values = [jnp.sum(product)[None]]
        if with_sums:
            sums = slab_slot(jnp.sum(field, axis=(1, 2))[None])[:, 0]
            values.append((brick_here[:, None, None] * sums[None]).reshape(-1))
        packed = jnp.concatenate(values)
        xy, z = side_faces(field)
        total, xy_land, z_land = exchange(as_tile(packed), xy, z, 1)
        total = total.reshape(-1)[: packed.shape[0]]
        field_halo = halo(field, xy_land, z_land, 0.0)
        if not with_sums:
            return total[0], None, field_halo
        mine = lax.dynamic_index_in_dim(
            total[1:].reshape(brick_count, -1), brick_index, keepdims=False
        )
        return total[0], mine, field_halo

    terms = columns[4]
    solution_field = jnp.zeros_like(forcing)
    residual = forcing
    search = precondition(residual, residual_halo, terms)
    energy, _, search_halo = sum_and_share(residual * search, search, False)
    for iteration in range(ITERS):
        mapped = stencil(search, stacked_effective, diagonal, *search_halo)
        curvature, mapped_terms, mapped_halo = sum_and_share(search * mapped, mapped, True)
        step_size = energy / curvature
        solution_field = solution_field + step_size * search
        residual = residual - step_size * mapped
        if iteration + 1 < ITERS:
            residual_halo = [
                part - step_size * change for part, change in zip(residual_halo, mapped_halo)
            ]
            terms = terms - step_size * mapped_terms
            smoothed = precondition(residual, residual_halo, terms)
            renewed, _, smoothed_halo = sum_and_share(residual * smoothed, smoothed, False)
            search = smoothed + renewed / energy * search
            search_halo = [
                part + renewed / energy * old for part, old in zip(smoothed_halo, search_halo)
            ]
            energy = renewed
    return (solution_field[None, None], residual[None, None])


def solution(mesh):
    return jax.shard_map(
        on_device,
        mesh=mesh,
        in_specs=(
            P("grp", "brick", None, None, None),
            P("grp", "brick", None, None, None),
            P("grp", "brick", None, None, None, None),
            P(),
            P(),
        ),
        out_specs=(P("grp", "brick", None, None, None), P("grp", "brick", None, None, None)),
        check_vma=False,
    )
```

```python
import functools

import jax
import jax.numpy as jnp
from jax import lax
from jax.experimental import pallas as pl
from jax.experimental.pallas import tpu as pltpu
from jax.sharding import PartitionSpec as P

MESH_IDS = pl.DeviceIdType.MESH

BS = 32
PATCH_X = 1
PATCH_Y = 2
ITERS = 3


OMEGA = 0.6


def exchange_kernel(
    x_ref, xy_ref, z_ref, o_ref, xy_out, z_out,
    landed_b, landed_g, landed_xy, landed_z,
    send_b, recv_b, send_g, recv_g, send_xy, recv_xy, send_z, recv_z,
):
    here_brick = lax.axis_index("brick")
    here_grp = lax.axis_index("grp")
    n_brick = landed_b.shape[0]
    n_grp = landed_g.shape[0]
    brick_peers = [(lax.rem(here_brick + k, n_brick), here_grp) for k in range(1, n_brick)]
    grp_peers = [(here_brick, lax.rem(here_grp + k, n_grp)) for k in range(1, n_grp)]
    barrier = pltpu.get_barrier_semaphore()
    for peer in brick_peers + grp_peers:
        pl.semaphore_signal(barrier, inc=1, device_id=peer, device_id_type=MESH_IDS)
    pl.semaphore_wait(barrier, len(brick_peers) + len(grp_peers))

    def send(src, dst, sends, recvs, index, peer):
        copy = pltpu.make_async_remote_copy(
            src_ref=src,
            dst_ref=dst.at[index],
            send_sem=sends.at[index],
            recv_sem=recvs.at[index],
            device_id=peer,
            device_id_type=MESH_IDS,
        )
        copy.start()
        return copy

    face_copies = [
        send(z_ref, landed_z, send_z, recv_z, 0, grp_peers[0]),
        send(z_ref, landed_z, send_z, recv_z, 1, grp_peers[-1]),
    ]
    face_copies += [
        send(xy_ref, landed_xy, send_xy, recv_xy, k, peer)
        for k, peer in enumerate(brick_peers, start=1)
    ]
    copies = [
        send(x_ref, landed_b, send_b, recv_b, k, peer)
        for k, peer in enumerate(brick_peers, start=1)
    ]
    landed_b[0] = x_ref[...]
    for copy in copies:
        copy.wait()
    total = landed_b[lax.rem(here_brick, n_brick)]
    for j in range(1, n_brick):
        total = total + landed_b[lax.rem(here_brick + n_brick - j, n_brick)]
    o_ref[...] = total
    landed_g[0] = total
    copies = [
        send(o_ref, landed_g, send_g, recv_g, k, peer)
        for k, peer in enumerate(grp_peers, start=1)
    ]
    for copy in copies:
        copy.wait()
    total = landed_g[lax.rem(here_grp, n_grp)]
    for j in range(1, n_grp):
        total = total + landed_g[lax.rem(here_grp + n_grp - j, n_grp)]
    o_ref[...] = total
    for copy in face_copies:
        copy.wait()
    landed_xy[0] = xy_ref[...]
    xy_out[...] = landed_xy[...]
    z_out[...] = landed_z[...]


def exchange(tile, xy, z, kernel_id):
    n_brick = lax.axis_size("brick")
    n_grp = lax.axis_size("grp")
    vmem = pl.BlockSpec(memory_space=pltpu.VMEM)
    dma = pltpu.SemaphoreType.DMA
    return pl.pallas_call(
        exchange_kernel,
        out_shape=(
            jax.ShapeDtypeStruct(tile.shape, jnp.float32),
            jax.ShapeDtypeStruct((n_brick,) + xy.shape, jnp.float32),
            jax.ShapeDtypeStruct((2,) + z.shape, jnp.float32),
        ),
        in_specs=[vmem] * 3,
        out_specs=(vmem, vmem, vmem),
        scratch_shapes=[
            pltpu.VMEM((n_brick,) + tile.shape, jnp.float32),
            pltpu.VMEM((n_grp,) + tile.shape, jnp.float32),
            pltpu.VMEM((n_brick,) + xy.shape, jnp.float32),
            pltpu.VMEM((2,) + z.shape, jnp.float32),
            dma((n_brick,)),
            dma((n_brick,)),
            dma((n_grp,)),
            dma((n_grp,)),
            dma((n_brick,)),
            dma((n_brick,)),
            dma((2,)),
            dma((2,)),
        ],
        compiler_params=pltpu.CompilerParams(collective_id=kernel_id, has_side_effects=True),
    )(tile, xy, z)


def stencil_kernel(f_ref, bonds_ref, masks_ref, diag_ref, rows_ref, faces_ref, o_ref):
    slots, width, lanes = f_ref.shape
    row = lax.broadcasted_iota(jnp.int32, (width, lanes), 0)
    lane = lax.broadcasted_iota(jnp.int32, (width, lanes), 1)
    pick = lax.broadcasted_iota(jnp.int32, (BS, lanes), 0)
    spot = lax.broadcasted_iota(jnp.int32, (BS, lanes), 1)
    spread_z = (spot // BS == pick).astype(jnp.float32)
    spread_y = (spot % BS == pick).astype(jnp.float32)

    def spread(face, table):
        return jnp.dot(face, table, precision=lax.Precision.HIGHEST, preferred_element_type=jnp.float32)

    for s in range(slots):
        fs = f_ref[s]
        xp = jnp.where(row == width - 1, rows_ref[0, s], pltpu.roll(fs, width - 1, 0))
        xm = jnp.where(row == 0, rows_ref[1, s], pltpu.roll(fs, 1, 0))
        yp = jnp.where(lane >= lanes - BS, spread(faces_ref[0, s], spread_y), pltpu.roll(fs, lanes - BS, 1))
        ym = jnp.where(lane < BS, spread(faces_ref[1, s], spread_y), pltpu.roll(fs, BS, 1))
        zp = jnp.where(lane % BS == BS - 1, spread(faces_ref[2, s], spread_z), pltpu.roll(fs, lanes - 1, 1))
        zm = jnp.where(lane % BS == 0, spread(faces_ref[3, s], spread_z), pltpu.roll(fs, 1, 1))
        borders = [
            row == width - 1,
            row == 0,
            lane >= lanes - BS,
            lane < BS,
            lane % BS == BS - 1,
            lane % BS == 0,
        ]
        total = diag_ref[s] * fs
        for d, beyond in enumerate([xp, xm, yp, ym, zp, zm]):
            base = 2 * (d * slots + s)
            active = jnp.where(borders[d], masks_ref[base + 1], masks_ref[base])
            total = total - bonds_ref[d, s] * active * beyond
        o_ref[s] = total


def stencil(field, bonds, masks, diag, rows, faces):
    vmem = pl.BlockSpec(memory_space=pltpu.VMEM)
    smem = pl.BlockSpec(memory_space=pltpu.SMEM)
    return pl.pallas_call(
        stencil_kernel,
        out_shape=jax.ShapeDtypeStruct(field.shape, jnp.float32),
        in_specs=[vmem, vmem, smem, vmem, vmem, vmem],
        out_specs=vmem,
    )(field, bonds, masks, diag, rows, faces)


def assemble(coarse_diag, couplings, strides):
    extent = coarse_diag.shape[0]
    matrix = jnp.diag(coarse_diag)
    for coupling, stride in zip(couplings, strides):
        banded = coupling[: extent - stride]
        matrix = matrix - jnp.diag(banded, stride) - jnp.diag(banded, -stride)
    return matrix


def on_device(source, uptake, conductance, occupancy, assignment):
    face_size = BS * BS
    slot_count = PATCH_X * PATCH_Y
    slab_index = lax.axis_index("grp")
    brick_index = lax.axis_index("brick")
    brick_count = lax.axis_size("brick")
    across = brick_count // 2
    peer_ids = jnp.arange(brick_count, dtype=jnp.int32)
    patch_index = assignment[brick_index]
    patch_row = patch_index // across
    patch_column = patch_index % across

    def owner_of(row_shift, column_shift):
        row_target = patch_row + row_shift
        column_target = patch_column + column_shift
        inside = (
            (row_target >= 0) & (row_target < 2) & (column_target >= 0) & (column_target < across)
        )
        holder = jnp.sum(jnp.where(assignment == row_target * across + column_target, peer_ids, 0))
        return jnp.where(inside, holder, -1)

    wanted = jnp.stack([owner_of(1, 0), owner_of(-1, 0), owner_of(0, 1), owner_of(0, -1)])
    padded = jnp.pad(occupancy, 1)
    window = lax.dynamic_slice(
        padded,
        (slab_index, patch_row * PATCH_X, patch_column * PATCH_Y),
        (3, PATCH_X + 2, PATCH_Y + 2),
    ).astype(jnp.float32)
    centre = window[1, 1:-1, 1:-1].reshape(slot_count)
    toward = [
        window[1, 2:, 1:-1],
        window[1, :-2, 1:-1],
        window[1, 1:-1, 2:],
        window[1, 1:-1, :-2],
        window[2, 1:-1, 1:-1],
        window[0, 1:-1, 1:-1],
    ]
    first_axis = lax.broadcasted_iota(jnp.int32, (1, BS, face_size), 1)
    flat_axis = lax.broadcasted_iota(jnp.int32, (1, BS, face_size), 2)
    second_axis = flat_axis // BS
    third_axis = flat_axis % BS
    cube_third = lax.broadcasted_iota(jnp.int32, (1, BS, BS, BS), 3)
    borders = [
        first_axis == BS - 1,
        first_axis == 0,
        second_axis == BS - 1,
        second_axis == 0,
        third_axis == BS - 1,
        third_axis == 0,
    ]
    bonds = conductance[0, 0]
    live_here = centre[:, None, None]
    effective = []
    for direction in range(6):
        neighbour_live = toward[direction].reshape(slot_count)[:, None, None]
        active = jnp.where(borders[direction], live_here * neighbour_live, live_here)
        effective.append(bonds[direction] * active)
    absorb = uptake[0, 0]
    diagonal = absorb
    for direction in range(6):
        diagonal = diagonal + effective[direction]

    masks = jnp.stack(
        [
            jnp.stack([centre, centre * toward[direction].reshape(slot_count)], axis=1)
            for direction in range(6)
        ]
    ).reshape(-1)

    def side_faces(field):
        cube = field.reshape(slot_count, BS, BS, BS)
        xy = jnp.concatenate(
            [
                field[:, 0, :],
                field[:, BS - 1, :],
                field[0, :, :BS].reshape(1, face_size),
                field[slot_count - 1, :, face_size - BS :].reshape(1, face_size),
            ]
        )
        z = jnp.concatenate(
            [
                cube[:, :, :, 0].reshape(slot_count, face_size),
                cube[:, :, :, BS - 1].reshape(slot_count, face_size),
            ]
        )
        return xy, z

    def pick(landed, holder, fill):
        offset = lax.rem(brick_index - holder + brick_count, brick_count)
        got = lax.dynamic_index_in_dim(landed, offset, keepdims=False)
        return jnp.where(holder >= 0, got, fill)

    def halo(field, xy_land, z_land, fill):
        xplus = pick(xy_land, wanted[0], fill)
        xminus = pick(xy_land, wanted[1], fill)
        yplus = pick(xy_land, wanted[2], fill)
        yminus = pick(xy_land, wanted[3], fill)
        rows = jnp.stack([xplus[:slot_count], xminus[slot_count : 2 * slot_count]])[:, :, None, :]
        beyond_yplus = jnp.stack([field[1, :, :BS], yplus[2 * slot_count].reshape(BS, BS)])
        beyond_yminus = jnp.stack(
            [yminus[2 * slot_count + 1].reshape(BS, BS), field[0, :, face_size - BS :]]
        )
        above = jnp.where(slab_index < grp_count - 1, z_land[1, :slot_count], fill)
        below = jnp.where(slab_index > 0, z_land[0, slot_count:], fill)
        faces = jnp.stack(
            [
                beyond_yplus,
                beyond_yminus,
                above.reshape(slot_count, BS, BS),
                below.reshape(slot_count, BS, BS),
            ]
        )
        return rows, faces

    slot_ids = jnp.arange(slot_count)
    brick_first = slot_ids // PATCH_Y
    brick_second = slot_ids % PATCH_Y
    inside = [
        (brick_first < PATCH_X - 1).astype(jnp.float32),
        (brick_first > 0).astype(jnp.float32),
        (brick_second < PATCH_Y - 1).astype(jnp.float32),
        (brick_second > 0).astype(jnp.float32),
    ]
    face_sums = [
        jnp.sum(effective[0][:, BS - 1, :], axis=1),
        jnp.sum(effective[1][:, 0, :], axis=1),
        jnp.sum(effective[2][:, :, face_size - BS :], axis=(1, 2)),
        jnp.sum(effective[3][:, :, :BS], axis=(1, 2)),
        jnp.sum(effective[4].reshape(slot_count, BS, BS, BS)[:, :, :, BS - 1], axis=(1, 2)),
        jnp.sum(effective[5].reshape(slot_count, BS, BS, BS)[:, :, :, 0], axis=(1, 2)),
    ]
    coarse_diag = jnp.sum(absorb, axis=(1, 2))
    for direction in range(4):
        coarse_diag = coarse_diag + face_sums[direction] * inside[direction]
    coarse_diag = coarse_diag + face_sums[4] + face_sums[5]
    grp_count = lax.axis_size("grp")
    grp_ids = jnp.arange(grp_count, dtype=jnp.int32)

    def slab_slot(values):
        here = (grp_ids == slab_index).astype(jnp.float32)
        return here[:, None, None] * values[None]

    forcing = source[0, 0] * live_here

    def as_tile(values):
        rows = -(-values.shape[0] // 128)
        rows = -(-rows // 8) * 8
        return jnp.pad(values, (0, rows * 128 - values.shape[0])).reshape(rows, 128)

    record = jnp.stack(
        [
            coarse_diag,
            face_sums[0] * inside[0],
            face_sums[2] * inside[2],
            face_sums[4],
            jnp.sum(forcing, axis=(1, 2)),
        ]
    )
    brick_here = (peer_ids == brick_index).astype(jnp.float32)
    spread = (brick_here[:, None, None, None] * slab_slot(record)[None]).reshape(-1)
    forcing_xy, forcing_z = side_faces(forcing)
    diagonal_xy, diagonal_z = side_faces(diagonal)
    summed, xy_land, z_land = exchange(
        as_tile(spread),
        jnp.concatenate([forcing_xy, diagonal_xy]),
        jnp.concatenate([forcing_z, diagonal_z]),
        2,
    )
    summed = summed.reshape(-1)[: spread.shape[0]]
    xy_rows = forcing_xy.shape[0]
    z_rows = forcing_z.shape[0]
    residual_halo = halo(forcing, xy_land[:, :xy_rows], z_land[:, :z_rows], 0.0)
    diagonal_halo = halo(diagonal, xy_land[:, xy_rows:], z_land[:, z_rows:], 1.0)
    gathered = lax.dynamic_index_in_dim(
        summed.reshape(brick_count, grp_count, 5, slot_count), brick_index, keepdims=False
    )
    columns = jnp.transpose(gathered, (1, 0, 2)).reshape(5, -1)
    matrix = assemble(columns[0], (columns[1], columns[2], columns[3]), (PATCH_Y, 1, slot_count))
    factor = jnp.linalg.cholesky(matrix)

    def coarse_solve(terms):
        middle = lax.linalg.triangular_solve(factor, terms[:, None], left_side=True, lower=True)
        result = lax.linalg.triangular_solve(
            factor, middle, left_side=True, lower=True, transpose_a=True
        )
        return lax.dynamic_slice_in_dim(result[:, 0], slab_index * slot_count, slot_count)

    def precondition(residual_field, field_halo, terms):
        smoothed = OMEGA * residual_field / diagonal
        smoothed_halo = [OMEGA * part / scale for part, scale in zip(field_halo, diagonal_halo)]
        applied = stencil(smoothed, bonds, masks, diagonal, *smoothed_halo)
        smoothed = smoothed + OMEGA * (residual_field - applied) / diagonal
        return smoothed + coarse_solve(terms)[:, None, None]

    def sum_and_share(product, field, with_sums):
        values = [jnp.sum(product)[None]]
        if with_sums:
            sums = slab_slot(jnp.sum(field, axis=(1, 2))[None])[:, 0]
            values.append((brick_here[:, None, None] * sums[None]).reshape(-1))
        packed = jnp.concatenate(values)
        xy, z = side_faces(field)
        total, xy_land, z_land = exchange(as_tile(packed), xy, z, 1)
        total = total.reshape(-1)[: packed.shape[0]]
        field_halo = halo(field, xy_land, z_land, 0.0)
        if not with_sums:
            return total[0], None, field_halo
        mine = lax.dynamic_index_in_dim(
            total[1:].reshape(brick_count, -1), brick_index, keepdims=False
        )
        return total[0], mine, field_halo

    terms = columns[4]
    solution_field = jnp.zeros_like(forcing)
    residual = forcing
    search = precondition(residual, residual_halo, terms)
    energy, _, search_halo = sum_and_share(residual * search, search, False)
    for iteration in range(ITERS):
        mapped = stencil(search, bonds, masks, diagonal, *search_halo)
        curvature, mapped_terms, mapped_halo = sum_and_share(search * mapped, mapped, True)
        step_size = energy / curvature
        solution_field = solution_field + step_size * search
        residual = residual - step_size * mapped
        if iteration + 1 < ITERS:
            residual_halo = [
                part - step_size * change for part, change in zip(residual_halo, mapped_halo)
            ]
            terms = terms - step_size * mapped_terms
            smoothed = precondition(residual, residual_halo, terms)
            renewed, _, smoothed_halo = sum_and_share(residual * smoothed, smoothed, False)
            search = smoothed + renewed / energy * search
            search_halo = [
                part + renewed / energy * old for part, old in zip(smoothed_halo, search_halo)
            ]
            energy = renewed
    return (solution_field[None, None], residual[None, None])


def solution(mesh):
    return jax.shard_map(
        on_device,
        mesh=mesh,
        in_specs=(
            P("grp", "brick", None, None, None),
            P("grp", "brick", None, None, None),
            P("grp", "brick", None, None, None, None),
            P(),
            P(),
        ),
        out_specs=(P("grp", "brick", None, None, None), P("grp", "brick", None, None, None)),
        check_vma=False,
    )
```

```python
import functools

import jax
import jax.numpy as jnp
from jax import lax
from jax.experimental import pallas as pl
from jax.experimental.pallas import tpu as pltpu
from jax.sharding import PartitionSpec as P

MESH_IDS = pl.DeviceIdType.MESH

BS = 32
PATCH_X = 1
PATCH_Y = 2
ITERS = 3


OMEGA = 0.6


def exchange_kernel(
    x_ref, xy_ref, z_ref, o_ref, xy_out, z_out,
    landed_b, landed_g, landed_xy, landed_z,
    send_b, recv_b, send_g, recv_g, send_xy, recv_xy, send_z, recv_z,
):
    here_brick = lax.axis_index("brick")
    here_grp = lax.axis_index("grp")
    n_brick = landed_b.shape[0]
    n_grp = landed_g.shape[0]
    brick_peers = [(lax.rem(here_brick + k, n_brick), here_grp) for k in range(1, n_brick)]
    grp_peers = [(here_brick, lax.rem(here_grp + k, n_grp)) for k in range(1, n_grp)]
    barrier = pltpu.get_barrier_semaphore()
    for peer in brick_peers + grp_peers:
        pl.semaphore_signal(barrier, inc=1, device_id=peer, device_id_type=MESH_IDS)
    pl.semaphore_wait(barrier, len(brick_peers) + len(grp_peers))

    def send(src, dst, sends, recvs, index, peer):
        copy = pltpu.make_async_remote_copy(
            src_ref=src,
            dst_ref=dst.at[index],
            send_sem=sends.at[index],
            recv_sem=recvs.at[index],
            device_id=peer,
            device_id_type=MESH_IDS,
        )
        copy.start()
        return copy

    face_copies = [
        send(z_ref, landed_z, send_z, recv_z, 0, grp_peers[0]),
        send(z_ref, landed_z, send_z, recv_z, 1, grp_peers[-1]),
    ]
    face_copies += [
        send(xy_ref, landed_xy, send_xy, recv_xy, k, peer)
        for k, peer in enumerate(brick_peers, start=1)
    ]
    copies = [
        send(x_ref, landed_b, send_b, recv_b, k, peer)
        for k, peer in enumerate(brick_peers, start=1)
    ]
    landed_b[0] = x_ref[...]
    for copy in copies:
        copy.wait()
    total = landed_b[lax.rem(here_brick, n_brick)]
    for j in range(1, n_brick):
        total = total + landed_b[lax.rem(here_brick + n_brick - j, n_brick)]
    o_ref[...] = total
    landed_g[0] = total
    copies = [
        send(o_ref, landed_g, send_g, recv_g, k, peer)
        for k, peer in enumerate(grp_peers, start=1)
    ]
    for copy in copies:
        copy.wait()
    total = landed_g[lax.rem(here_grp, n_grp)]
    for j in range(1, n_grp):
        total = total + landed_g[lax.rem(here_grp + n_grp - j, n_grp)]
    o_ref[...] = total
    for copy in face_copies:
        copy.wait()
    landed_xy[0] = xy_ref[...]
    xy_out[...] = landed_xy[...]
    z_out[...] = landed_z[...]


def exchange(tile, xy, z, kernel_id):
    n_brick = lax.axis_size("brick")
    n_grp = lax.axis_size("grp")
    vmem = pl.BlockSpec(memory_space=pltpu.VMEM)
    dma = pltpu.SemaphoreType.DMA
    return pl.pallas_call(
        exchange_kernel,
        out_shape=(
            jax.ShapeDtypeStruct(tile.shape, jnp.float32),
            jax.ShapeDtypeStruct((n_brick,) + xy.shape, jnp.float32),
            jax.ShapeDtypeStruct((2,) + z.shape, jnp.float32),
        ),
        in_specs=[vmem] * 3,
        out_specs=(vmem, vmem, vmem),
        scratch_shapes=[
            pltpu.VMEM((n_brick,) + tile.shape, jnp.float32),
            pltpu.VMEM((n_grp,) + tile.shape, jnp.float32),
            pltpu.VMEM((n_brick,) + xy.shape, jnp.float32),
            pltpu.VMEM((2,) + z.shape, jnp.float32),
            dma((n_brick,)),
            dma((n_brick,)),
            dma((n_grp,)),
            dma((n_grp,)),
            dma((n_brick,)),
            dma((n_brick,)),
            dma((2,)),
            dma((2,)),
        ],
        compiler_params=pltpu.CompilerParams(collective_id=kernel_id, has_side_effects=True),
    )(tile, xy, z)


def stencil_kernel(f_ref, bonds_ref, masks_ref, diag_ref, rows_ref, faces_ref, o_ref):
    slots, width, lanes = f_ref.shape
    row = lax.broadcasted_iota(jnp.int32, (width, lanes), 0)
    lane = lax.broadcasted_iota(jnp.int32, (width, lanes), 1)
    pick = lax.broadcasted_iota(jnp.int32, (BS, lanes), 0)
    spot = lax.broadcasted_iota(jnp.int32, (BS, lanes), 1)
    spread_z = (spot // BS == pick).astype(jnp.float32)
    spread_y = (spot % BS == pick).astype(jnp.float32)

    def spread(face, table):
        return jnp.dot(face, table, precision=lax.Precision.HIGHEST, preferred_element_type=jnp.float32)

    for s in range(slots):
        fs = f_ref[s]
        xp = jnp.where(row == width - 1, rows_ref[0, s], pltpu.roll(fs, width - 1, 0))
        xm = jnp.where(row == 0, rows_ref[1, s], pltpu.roll(fs, 1, 0))
        yp = jnp.where(lane >= lanes - BS, spread(faces_ref[0, s], spread_y), pltpu.roll(fs, lanes - BS, 1))
        ym = jnp.where(lane < BS, spread(faces_ref[1, s], spread_y), pltpu.roll(fs, BS, 1))
        zp = jnp.where(lane % BS == BS - 1, spread(faces_ref[2, s], spread_z), pltpu.roll(fs, lanes - 1, 1))
        zm = jnp.where(lane % BS == 0, spread(faces_ref[3, s], spread_z), pltpu.roll(fs, 1, 1))
        borders = [
            row == width - 1,
            row == 0,
            lane >= lanes - BS,
            lane < BS,
            lane % BS == BS - 1,
            lane % BS == 0,
        ]
        total = diag_ref[s] * fs
        for d, beyond in enumerate([xp, xm, yp, ym, zp, zm]):
            base = 2 * (d * slots + s)
            active = jnp.where(borders[d], masks_ref[base + 1], masks_ref[base])
            total = total - bonds_ref[d, s] * active * beyond
        o_ref[s] = total


def stencil(field, bonds, masks, diag, rows, faces):
    vmem = pl.BlockSpec(memory_space=pltpu.VMEM)
    smem = pl.BlockSpec(memory_space=pltpu.SMEM)
    return pl.pallas_call(
        stencil_kernel,
        out_shape=jax.ShapeDtypeStruct(field.shape, jnp.float32),
        in_specs=[vmem, vmem, smem, vmem, vmem, vmem],
        out_specs=vmem,
    )(field, bonds, masks, diag, rows, faces)


def assemble(coarse_diag, couplings, strides):
    extent = coarse_diag.shape[0]
    matrix = jnp.diag(coarse_diag)
    for coupling, stride in zip(couplings, strides):
        banded = coupling[: extent - stride]
        matrix = matrix - jnp.diag(banded, stride) - jnp.diag(banded, -stride)
    return matrix


def on_device(source, uptake, conductance, occupancy, assignment):
    face_size = BS * BS
    slot_count = PATCH_X * PATCH_Y
    slab_index = lax.axis_index("grp")
    brick_index = lax.axis_index("brick")
    brick_count = lax.axis_size("brick")
    across = brick_count // 2
    peer_ids = jnp.arange(brick_count, dtype=jnp.int32)
    patch_index = assignment[brick_index]
    patch_row = patch_index // across
    patch_column = patch_index % across

    def owner_of(row_shift, column_shift):
        row_target = patch_row + row_shift
        column_target = patch_column + column_shift
        inside = (
            (row_target >= 0) & (row_target < 2) & (column_target >= 0) & (column_target < across)
        )
        holder = jnp.sum(jnp.where(assignment == row_target * across + column_target, peer_ids, 0))
        return jnp.where(inside, holder, -1)

    wanted = jnp.stack([owner_of(1, 0), owner_of(-1, 0), owner_of(0, 1), owner_of(0, -1)])
    padded = jnp.pad(occupancy, 1)
    window = lax.dynamic_slice(
        padded,
        (slab_index, patch_row * PATCH_X, patch_column * PATCH_Y),
        (3, PATCH_X + 2, PATCH_Y + 2),
    ).astype(jnp.float32)
    centre = window[1, 1:-1, 1:-1].reshape(slot_count)
    toward = [
        window[1, 2:, 1:-1],
        window[1, :-2, 1:-1],
        window[1, 1:-1, 2:],
        window[1, 1:-1, :-2],
        window[2, 1:-1, 1:-1],
        window[0, 1:-1, 1:-1],
    ]
    first_axis = lax.broadcasted_iota(jnp.int32, (1, BS, face_size), 1)
    flat_axis = lax.broadcasted_iota(jnp.int32, (1, BS, face_size), 2)
    second_axis = flat_axis // BS
    third_axis = flat_axis % BS
    cube_third = lax.broadcasted_iota(jnp.int32, (1, BS, BS, BS), 3)
    borders = [
        first_axis == BS - 1,
        first_axis == 0,
        second_axis == BS - 1,
        second_axis == 0,
        third_axis == BS - 1,
        third_axis == 0,
    ]
    bonds = conductance[0, 0]
    live_here = centre[:, None, None]
    effective = []
    for direction in range(6):
        neighbour_live = toward[direction].reshape(slot_count)[:, None, None]
        active = jnp.where(borders[direction], live_here * neighbour_live, live_here)
        effective.append(bonds[direction] * active)
    absorb = uptake[0, 0]
    diagonal = absorb
    for direction in range(6):
        diagonal = diagonal + effective[direction]

    masks = jnp.stack(
        [
            jnp.stack([centre, centre * toward[direction].reshape(slot_count)], axis=1)
            for direction in range(6)
        ]
    ).reshape(-1)

    lane_ids = jnp.arange(face_size, dtype=jnp.int32)[:, None]
    layer_ids = BS * jnp.arange(BS, dtype=jnp.int32)[None, :]
    picker = jnp.concatenate([lane_ids == layer_ids, lane_ids == layer_ids + BS - 1], axis=1)
    picker = picker.astype(jnp.float32)

    def side_faces(field):
        picked = jnp.dot(
            field.reshape(slot_count * BS, face_size), picker, precision=lax.Precision.HIGHEST
        )
        z = picked.reshape(slot_count, BS, 2, BS).transpose(2, 0, 1, 3)
        xy = jnp.concatenate(
            [
                field[:, 0, :],
                field[:, BS - 1, :],
                field[0, :, :BS].reshape(1, face_size),
                field[slot_count - 1, :, face_size - BS :].reshape(1, face_size),
            ]
        )
        return xy, z.reshape(2 * slot_count, face_size)

    def pick(landed, holder, fill):
        offset = lax.rem(brick_index - holder + brick_count, brick_count)
        got = lax.dynamic_index_in_dim(landed, offset, keepdims=False)
        return jnp.where(holder >= 0, got, fill)

    def halo(field, xy_land, z_land, fill):
        xplus = pick(xy_land, wanted[0], fill)
        xminus = pick(xy_land, wanted[1], fill)
        yplus = pick(xy_land, wanted[2], fill)
        yminus = pick(xy_land, wanted[3], fill)
        rows = jnp.stack([xplus[:slot_count], xminus[slot_count : 2 * slot_count]])[:, :, None, :]
        beyond_yplus = jnp.stack([field[1, :, :BS], yplus[2 * slot_count].reshape(BS, BS)])
        beyond_yminus = jnp.stack(
            [yminus[2 * slot_count + 1].reshape(BS, BS), field[0, :, face_size - BS :]]
        )
        above = jnp.where(slab_index < grp_count - 1, z_land[1, :slot_count], fill)
        below = jnp.where(slab_index > 0, z_land[0, slot_count:], fill)
        faces = jnp.stack(
            [
                beyond_yplus,
                beyond_yminus,
                above.reshape(slot_count, BS, BS),
                below.reshape(slot_count, BS, BS),
            ]
        )
        return rows, faces

    slot_ids = jnp.arange(slot_count)
    brick_first = slot_ids // PATCH_Y
    brick_second = slot_ids % PATCH_Y
    inside = [
        (brick_first < PATCH_X - 1).astype(jnp.float32),
        (brick_first > 0).astype(jnp.float32),
        (brick_second < PATCH_Y - 1).astype(jnp.float32),
        (brick_second > 0).astype(jnp.float32),
    ]
    face_sums = [
        jnp.sum(effective[0][:, BS - 1, :], axis=1),
        jnp.sum(effective[1][:, 0, :], axis=1),
        jnp.sum(effective[2][:, :, face_size - BS :], axis=(1, 2)),
        jnp.sum(effective[3][:, :, :BS], axis=(1, 2)),
        jnp.sum(jnp.where(borders[4], effective[4], 0.0), axis=(1, 2)),
        jnp.sum(jnp.where(borders[5], effective[5], 0.0), axis=(1, 2)),
    ]
    coarse_diag = jnp.sum(absorb, axis=(1, 2))
    for direction in range(4):
        coarse_diag = coarse_diag + face_sums[direction] * inside[direction]
    coarse_diag = coarse_diag + face_sums[4] + face_sums[5]
    grp_count = lax.axis_size("grp")
    grp_ids = jnp.arange(grp_count, dtype=jnp.int32)

    def slab_slot(values):
        here = (grp_ids == slab_index).astype(jnp.float32)
        return here[:, None, None] * values[None]

    forcing = source[0, 0] * live_here

    def as_tile(values):
        rows = -(-values.shape[0] // 128)
        rows = -(-rows // 8) * 8
        return jnp.pad(values, (0, rows * 128 - values.shape[0])).reshape(rows, 128)

    record = jnp.stack(
        [
            coarse_diag,
            face_sums[0] * inside[0],
            face_sums[2] * inside[2],
            face_sums[4],
            jnp.sum(forcing, axis=(1, 2)),
        ]
    )
    brick_here = (peer_ids == brick_index).astype(jnp.float32)
    spread = (brick_here[:, None, None, None] * slab_slot(record)[None]).reshape(-1)
    forcing_xy, forcing_z = side_faces(forcing)
    diagonal_xy, diagonal_z = side_faces(diagonal)
    summed, xy_land, z_land = exchange(
        as_tile(spread),
        jnp.concatenate([forcing_xy, diagonal_xy]),
        jnp.concatenate([forcing_z, diagonal_z]),
        2,
    )
    summed = summed.reshape(-1)[: spread.shape[0]]
    xy_rows = forcing_xy.shape[0]
    z_rows = forcing_z.shape[0]
    residual_halo = halo(forcing, xy_land[:, :xy_rows], z_land[:, :z_rows], 0.0)
    diagonal_halo = halo(diagonal, xy_land[:, xy_rows:], z_land[:, z_rows:], 1.0)
    gathered = lax.dynamic_index_in_dim(
        summed.reshape(brick_count, grp_count, 5, slot_count), brick_index, keepdims=False
    )
    columns = jnp.transpose(gathered, (1, 0, 2)).reshape(5, -1)
    matrix = assemble(columns[0], (columns[1], columns[2], columns[3]), (PATCH_Y, 1, slot_count))
    factor = jnp.linalg.cholesky(matrix)

    def coarse_solve(terms):
        middle = lax.linalg.triangular_solve(factor, terms[:, None], left_side=True, lower=True)
        result = lax.linalg.triangular_solve(
            factor, middle, left_side=True, lower=True, transpose_a=True
        )
        return lax.dynamic_slice_in_dim(result[:, 0], slab_index * slot_count, slot_count)

    def precondition(residual_field, field_halo, terms):
        smoothed = OMEGA * residual_field / diagonal
        smoothed_halo = [OMEGA * part / scale for part, scale in zip(field_halo, diagonal_halo)]
        applied = stencil(smoothed, bonds, masks, diagonal, *smoothed_halo)
        smoothed = smoothed + OMEGA * (residual_field - applied) / diagonal
        return smoothed + coarse_solve(terms)[:, None, None]

    def sum_and_share(product, field, with_sums):
        values = [jnp.sum(product)[None]]
        if with_sums:
            sums = slab_slot(jnp.sum(field, axis=(1, 2))[None])[:, 0]
            values.append((brick_here[:, None, None] * sums[None]).reshape(-1))
        packed = jnp.concatenate(values)
        xy, z = side_faces(field)
        total, xy_land, z_land = exchange(as_tile(packed), xy, z, 1)
        total = total.reshape(-1)[: packed.shape[0]]
        field_halo = halo(field, xy_land, z_land, 0.0)
        if not with_sums:
            return total[0], None, field_halo
        mine = lax.dynamic_index_in_dim(
            total[1:].reshape(brick_count, -1), brick_index, keepdims=False
        )
        return total[0], mine, field_halo

    terms = columns[4]
    solution_field = jnp.zeros_like(forcing)
    residual = forcing
    search = precondition(residual, residual_halo, terms)
    energy, _, search_halo = sum_and_share(residual * search, search, False)
    for iteration in range(ITERS):
        mapped = stencil(search, bonds, masks, diagonal, *search_halo)
        curvature, mapped_terms, mapped_halo = sum_and_share(search * mapped, mapped, True)
        step_size = energy / curvature
        solution_field = solution_field + step_size * search
        residual = residual - step_size * mapped
        if iteration + 1 < ITERS:
            residual_halo = [
                part - step_size * change for part, change in zip(residual_halo, mapped_halo)
            ]
            terms = terms - step_size * mapped_terms
            smoothed = precondition(residual, residual_halo, terms)
            renewed, _, smoothed_halo = sum_and_share(residual * smoothed, smoothed, False)
            search = smoothed + renewed / energy * search
            search_halo = [
                part + renewed / energy * old for part, old in zip(smoothed_halo, search_halo)
            ]
            energy = renewed
    return (solution_field[None, None], residual[None, None])


def solution(mesh):
    return jax.shard_map(
        on_device,
        mesh=mesh,
        in_specs=(
            P("grp", "brick", None, None, None),
            P("grp", "brick", None, None, None),
            P("grp", "brick", None, None, None, None),
            P(),
            P(),
        ),
        out_specs=(P("grp", "brick", None, None, None), P("grp", "brick", None, None, None)),
        check_vma=False,
    )
```

```python
import functools

import jax
import jax.numpy as jnp
from jax import lax
from jax.experimental import pallas as pl
from jax.experimental.pallas import tpu as pltpu
from jax.sharding import PartitionSpec as P

MESH_IDS = pl.DeviceIdType.MESH

BS = 32
PATCH_X = 1
PATCH_Y = 2
ITERS = 3


OMEGA = 0.6


def exchange_kernel(
    x_ref, xy_ref, z_ref, o_ref, xy_out, z_out,
    landed_b, landed_g, landed_xy, landed_z,
    send_b, recv_b, send_g, recv_g, send_xy, recv_xy, send_z, recv_z,
):
    here_brick = lax.axis_index("brick")
    here_grp = lax.axis_index("grp")
    n_brick = landed_b.shape[0]
    n_grp = landed_g.shape[0]
    brick_peers = [(lax.rem(here_brick + k, n_brick), here_grp) for k in range(1, n_brick)]
    grp_peers = [(here_brick, lax.rem(here_grp + k, n_grp)) for k in range(1, n_grp)]
    barrier = pltpu.get_barrier_semaphore()
    for peer in brick_peers + grp_peers:
        pl.semaphore_signal(barrier, inc=1, device_id=peer, device_id_type=MESH_IDS)
    pl.semaphore_wait(barrier, len(brick_peers) + len(grp_peers))

    def send(src, dst, sends, recvs, index, peer):
        copy = pltpu.make_async_remote_copy(
            src_ref=src,
            dst_ref=dst.at[index],
            send_sem=sends.at[index],
            recv_sem=recvs.at[index],
            device_id=peer,
            device_id_type=MESH_IDS,
        )
        copy.start()
        return copy

    face_copies = [
        send(z_ref, landed_z, send_z, recv_z, 0, grp_peers[0]),
        send(z_ref, landed_z, send_z, recv_z, 1, grp_peers[-1]),
    ]
    face_copies += [
        send(xy_ref, landed_xy, send_xy, recv_xy, k, peer)
        for k, peer in enumerate(brick_peers, start=1)
    ]
    copies = [
        send(x_ref, landed_b, send_b, recv_b, k, peer)
        for k, peer in enumerate(brick_peers, start=1)
    ]
    landed_b[0] = x_ref[...]
    for copy in copies:
        copy.wait()
    total = landed_b[lax.rem(here_brick, n_brick)]
    for j in range(1, n_brick):
        total = total + landed_b[lax.rem(here_brick + n_brick - j, n_brick)]
    o_ref[...] = total
    landed_g[0] = total
    copies = [
        send(o_ref, landed_g, send_g, recv_g, k, peer)
        for k, peer in enumerate(grp_peers, start=1)
    ]
    for copy in copies:
        copy.wait()
    total = landed_g[lax.rem(here_grp, n_grp)]
    for j in range(1, n_grp):
        total = total + landed_g[lax.rem(here_grp + n_grp - j, n_grp)]
    o_ref[...] = total
    for copy in face_copies:
        copy.wait()
    landed_xy[0] = xy_ref[...]
    xy_out[...] = landed_xy[...]
    z_out[...] = landed_z[...]


def exchange(tile, xy, z, kernel_id):
    n_brick = lax.axis_size("brick")
    n_grp = lax.axis_size("grp")
    vmem = pl.BlockSpec(memory_space=pltpu.VMEM)
    dma = pltpu.SemaphoreType.DMA
    return pl.pallas_call(
        exchange_kernel,
        out_shape=(
            jax.ShapeDtypeStruct(tile.shape, jnp.float32),
            jax.ShapeDtypeStruct((n_brick,) + xy.shape, jnp.float32),
            jax.ShapeDtypeStruct((2,) + z.shape, jnp.float32),
        ),
        in_specs=[vmem] * 3,
        out_specs=(vmem, vmem, vmem),
        scratch_shapes=[
            pltpu.VMEM((n_brick,) + tile.shape, jnp.float32),
            pltpu.VMEM((n_grp,) + tile.shape, jnp.float32),
            pltpu.VMEM((n_brick,) + xy.shape, jnp.float32),
            pltpu.VMEM((2,) + z.shape, jnp.float32),
            dma((n_brick,)),
            dma((n_brick,)),
            dma((n_grp,)),
            dma((n_grp,)),
            dma((n_brick,)),
            dma((n_brick,)),
            dma((2,)),
            dma((2,)),
        ],
        compiler_params=pltpu.CompilerParams(collective_id=kernel_id, has_side_effects=True),
    )(tile, xy, z)


def stencil_kernel(
    coef_ref, f_ref, bonds_ref, masks_ref, diag_ref, rows_ref, faces_ref, o_ref, part_ref, *, smooth
):
    slots, width, lanes = f_ref.shape
    row = lax.broadcasted_iota(jnp.int32, (width, lanes), 0)
    lane = lax.broadcasted_iota(jnp.int32, (width, lanes), 1)
    pick = lax.broadcasted_iota(jnp.int32, (BS, lanes), 0)
    spot = lax.broadcasted_iota(jnp.int32, (BS, lanes), 1)
    spread_z = (spot // BS == pick).astype(jnp.float32)
    spread_y = (spot % BS == pick).astype(jnp.float32)

    def spread(face, table):
        return jnp.dot(face, table, precision=lax.Precision.HIGHEST, preferred_element_type=jnp.float32)

    borders = [
        row == width - 1,
        row == 0,
        lane >= lanes - BS,
        lane < BS,
        lane % BS == BS - 1,
        lane % BS == 0,
    ]
    dot = jnp.float32(0.0)
    for s in range(slots):
        ds = diag_ref[s]
        if smooth:
            rs = f_ref[s]
            fs = OMEGA * rs / ds
        else:
            fs = f_ref[s]
        xp = jnp.where(row == width - 1, rows_ref[0, s], pltpu.roll(fs, width - 1, 0))
        xm = jnp.where(row == 0, rows_ref[1, s], pltpu.roll(fs, 1, 0))
        yp = jnp.where(lane >= lanes - BS, spread(faces_ref[0, s], spread_y), pltpu.roll(fs, lanes - BS, 1))
        ym = jnp.where(lane < BS, spread(faces_ref[1, s], spread_y), pltpu.roll(fs, BS, 1))
        zp = jnp.where(lane % BS == BS - 1, spread(faces_ref[2, s], spread_z), pltpu.roll(fs, lanes - 1, 1))
        zm = jnp.where(lane % BS == 0, spread(faces_ref[3, s], spread_z), pltpu.roll(fs, 1, 1))
        total = ds * fs
        for d, beyond in enumerate([xp, xm, yp, ym, zp, zm]):
            base = 2 * (d * slots + s)
            active = jnp.where(borders[d], masks_ref[base + 1], masks_ref[base])
            total = total - bonds_ref[d, s] * active * beyond
        if smooth:
            total = fs + OMEGA * (rs - total) / ds
            total = total + coef_ref[s]
            dot = dot + jnp.sum(rs * total)
        else:
            dot = dot + jnp.sum(fs * total)
            part_ref[1 + s] = jnp.sum(total)
        o_ref[s] = total
    part_ref[0] = dot
    if smooth:
        for s in range(slots):
            part_ref[1 + s] = jnp.float32(0.0)


def stencil(field, bonds, masks, diag, rows, faces, coef=None):
    slots = field.shape[0]
    smooth = coef is not None
    if coef is None:
        coef = jnp.zeros((slots,), jnp.float32)
    vmem = pl.BlockSpec(memory_space=pltpu.VMEM)
    smem = pl.BlockSpec(memory_space=pltpu.SMEM)
    return pl.pallas_call(
        functools.partial(stencil_kernel, smooth=smooth),
        out_shape=(
            jax.ShapeDtypeStruct(field.shape, jnp.float32),
            jax.ShapeDtypeStruct((1 + slots,), jnp.float32),
        ),
        in_specs=[smem, vmem, vmem, smem, vmem, vmem, vmem],
        out_specs=(vmem, smem),
    )(coef, field, bonds, masks, diag, rows, faces)


def assemble(coarse_diag, couplings, strides):
    extent = coarse_diag.shape[0]
    matrix = jnp.diag(coarse_diag)
    for coupling, stride in zip(couplings, strides):
        banded = coupling[: extent - stride]
        matrix = matrix - jnp.diag(banded, stride) - jnp.diag(banded, -stride)
    return matrix


def on_device(source, uptake, conductance, occupancy, assignment):
    face_size = BS * BS
    slot_count = PATCH_X * PATCH_Y
    slab_index = lax.axis_index("grp")
    brick_index = lax.axis_index("brick")
    brick_count = lax.axis_size("brick")
    across = brick_count // 2
    peer_ids = jnp.arange(brick_count, dtype=jnp.int32)
    patch_index = assignment[brick_index]
    patch_row = patch_index // across
    patch_column = patch_index % across

    def owner_of(row_shift, column_shift):
        row_target = patch_row + row_shift
        column_target = patch_column + column_shift
        inside = (
            (row_target >= 0) & (row_target < 2) & (column_target >= 0) & (column_target < across)
        )
        holder = jnp.sum(jnp.where(assignment == row_target * across + column_target, peer_ids, 0))
        return jnp.where(inside, holder, -1)

    wanted = jnp.stack([owner_of(1, 0), owner_of(-1, 0), owner_of(0, 1), owner_of(0, -1)])
    padded = jnp.pad(occupancy, 1)
    window = lax.dynamic_slice(
        padded,
        (slab_index, patch_row * PATCH_X, patch_column * PATCH_Y),
        (3, PATCH_X + 2, PATCH_Y + 2),
    ).astype(jnp.float32)
    centre = window[1, 1:-1, 1:-1].reshape(slot_count)
    toward = [
        window[1, 2:, 1:-1],
        window[1, :-2, 1:-1],
        window[1, 1:-1, 2:],
        window[1, 1:-1, :-2],
        window[2, 1:-1, 1:-1],
        window[0, 1:-1, 1:-1],
    ]
    first_axis = lax.broadcasted_iota(jnp.int32, (1, BS, face_size), 1)
    flat_axis = lax.broadcasted_iota(jnp.int32, (1, BS, face_size), 2)
    second_axis = flat_axis // BS
    third_axis = flat_axis % BS
    cube_third = lax.broadcasted_iota(jnp.int32, (1, BS, BS, BS), 3)
    borders = [
        first_axis == BS - 1,
        first_axis == 0,
        second_axis == BS - 1,
        second_axis == 0,
        third_axis == BS - 1,
        third_axis == 0,
    ]
    bonds = conductance[0, 0]
    live_here = centre[:, None, None]
    effective = []
    for direction in range(6):
        neighbour_live = toward[direction].reshape(slot_count)[:, None, None]
        active = jnp.where(borders[direction], live_here * neighbour_live, live_here)
        effective.append(bonds[direction] * active)
    absorb = uptake[0, 0]
    diagonal = absorb
    for direction in range(6):
        diagonal = diagonal + effective[direction]

    masks = jnp.stack(
        [
            jnp.stack([centre, centre * toward[direction].reshape(slot_count)], axis=1)
            for direction in range(6)
        ]
    ).reshape(-1)

    lane_ids = jnp.arange(face_size, dtype=jnp.int32)[:, None]
    layer_ids = BS * jnp.arange(BS, dtype=jnp.int32)[None, :]
    picker = jnp.concatenate([lane_ids == layer_ids, lane_ids == layer_ids + BS - 1], axis=1)
    picker = picker.astype(jnp.float32)

    def side_faces(field):
        picked = jnp.dot(
            field.reshape(slot_count * BS, face_size), picker, precision=lax.Precision.HIGHEST
        )
        z = picked.reshape(slot_count, BS, 2, BS).transpose(2, 0, 1, 3)
        xy = jnp.concatenate(
            [
                field[:, 0, :],
                field[:, BS - 1, :],
                field[0, :, :BS].reshape(1, face_size),
                field[slot_count - 1, :, face_size - BS :].reshape(1, face_size),
            ]
        )
        return xy, z.reshape(2 * slot_count, face_size)

    def pick(landed, holder, fill):
        offset = lax.rem(brick_index - holder + brick_count, brick_count)
        got = lax.dynamic_index_in_dim(landed, offset, keepdims=False)
        return jnp.where(holder >= 0, got, fill)

    def halo(field, xy_land, z_land, fill):
        xplus = pick(xy_land, wanted[0], fill)
        xminus = pick(xy_land, wanted[1], fill)
        yplus = pick(xy_land, wanted[2], fill)
        yminus = pick(xy_land, wanted[3], fill)
        rows = jnp.stack([xplus[:slot_count], xminus[slot_count : 2 * slot_count]])[:, :, None, :]
        beyond_yplus = jnp.stack([field[1, :, :BS], yplus[2 * slot_count].reshape(BS, BS)])
        beyond_yminus = jnp.stack(
            [yminus[2 * slot_count + 1].reshape(BS, BS), field[0, :, face_size - BS :]]
        )
        above = jnp.where(slab_index < grp_count - 1, z_land[1, :slot_count], fill)
        below = jnp.where(slab_index > 0, z_land[0, slot_count:], fill)
        faces = jnp.stack(
            [
                beyond_yplus,
                beyond_yminus,
                above.reshape(slot_count, BS, BS),
                below.reshape(slot_count, BS, BS),
            ]
        )
        return rows, faces

    slot_ids = jnp.arange(slot_count)
    brick_first = slot_ids // PATCH_Y
    brick_second = slot_ids % PATCH_Y
    inside = [
        (brick_first < PATCH_X - 1).astype(jnp.float32),
        (brick_first > 0).astype(jnp.float32),
        (brick_second < PATCH_Y - 1).astype(jnp.float32),
        (brick_second > 0).astype(jnp.float32),
    ]
    face_sums = [
        jnp.sum(effective[0][:, BS - 1, :], axis=1),
        jnp.sum(effective[1][:, 0, :], axis=1),
        jnp.sum(effective[2][:, :, face_size - BS :], axis=(1, 2)),
        jnp.sum(effective[3][:, :, :BS], axis=(1, 2)),
        jnp.sum(jnp.where(borders[4], effective[4], 0.0), axis=(1, 2)),
        jnp.sum(jnp.where(borders[5], effective[5], 0.0), axis=(1, 2)),
    ]
    coarse_diag = jnp.sum(absorb, axis=(1, 2))
    for direction in range(4):
        coarse_diag = coarse_diag + face_sums[direction] * inside[direction]
    coarse_diag = coarse_diag + face_sums[4] + face_sums[5]
    grp_count = lax.axis_size("grp")
    grp_ids = jnp.arange(grp_count, dtype=jnp.int32)

    def slab_slot(values):
        here = (grp_ids == slab_index).astype(jnp.float32)
        return here[:, None, None] * values[None]

    forcing = source[0, 0] * live_here

    def as_tile(values):
        rows = -(-values.shape[0] // 128)
        rows = -(-rows // 8) * 8
        return jnp.pad(values, (0, rows * 128 - values.shape[0])).reshape(rows, 128)

    record = jnp.stack(
        [
            coarse_diag,
            face_sums[0] * inside[0],
            face_sums[2] * inside[2],
            face_sums[4],
            jnp.sum(forcing, axis=(1, 2)),
        ]
    )
    brick_here = (peer_ids == brick_index).astype(jnp.float32)
    spread = (brick_here[:, None, None, None] * slab_slot(record)[None]).reshape(-1)
    forcing_xy, forcing_z = side_faces(forcing)
    diagonal_xy, diagonal_z = side_faces(diagonal)
    summed, xy_land, z_land = exchange(
        as_tile(spread),
        jnp.concatenate([forcing_xy, diagonal_xy]),
        jnp.concatenate([forcing_z, diagonal_z]),
        2,
    )
    summed = summed.reshape(-1)[: spread.shape[0]]
    xy_rows = forcing_xy.shape[0]
    z_rows = forcing_z.shape[0]
    residual_halo = halo(forcing, xy_land[:, :xy_rows], z_land[:, :z_rows], 0.0)
    diagonal_halo = halo(diagonal, xy_land[:, xy_rows:], z_land[:, z_rows:], 1.0)
    gathered = lax.dynamic_index_in_dim(
        summed.reshape(brick_count, grp_count, 5, slot_count), brick_index, keepdims=False
    )
    columns = jnp.transpose(gathered, (1, 0, 2)).reshape(5, -1)
    matrix = assemble(columns[0], (columns[1], columns[2], columns[3]), (PATCH_Y, 1, slot_count))
    factor = jnp.linalg.cholesky(matrix)

    def coarse_solve(terms):
        middle = lax.linalg.triangular_solve(factor, terms[:, None], left_side=True, lower=True)
        result = lax.linalg.triangular_solve(
            factor, middle, left_side=True, lower=True, transpose_a=True
        )
        return lax.dynamic_slice_in_dim(result[:, 0], slab_index * slot_count, slot_count)

    def precondition(residual_field, field_halo, terms):
        smoothed_halo = [OMEGA * part / scale for part, scale in zip(field_halo, diagonal_halo)]
        return stencil(
            residual_field, bonds, masks, diagonal, *smoothed_halo, coef=coarse_solve(terms)
        )

    def sum_and_share(part, field, with_sums):
        values = [part[:1]]
        if with_sums:
            sums = slab_slot(part[1:][None])[:, 0]
            values.append((brick_here[:, None, None] * sums[None]).reshape(-1))
        packed = jnp.concatenate(values)
        xy, z = side_faces(field)
        total, xy_land, z_land = exchange(as_tile(packed), xy, z, 1)
        total = total.reshape(-1)[: packed.shape[0]]
        field_halo = halo(field, xy_land, z_land, 0.0)
        if not with_sums:
            return total[0], None, field_halo
        mine = lax.dynamic_index_in_dim(
            total[1:].reshape(brick_count, -1), brick_index, keepdims=False
        )
        return total[0], mine, field_halo

    terms = columns[4]
    solution_field = jnp.zeros_like(forcing)
    residual = forcing
    search, part = precondition(residual, residual_halo, terms)
    energy, _, search_halo = sum_and_share(part, search, False)
    for iteration in range(ITERS):
        mapped, part = stencil(search, bonds, masks, diagonal, *search_halo)
        curvature, mapped_terms, mapped_halo = sum_and_share(part, mapped, True)
        step_size = energy / curvature
        solution_field = solution_field + step_size * search
        residual = residual - step_size * mapped
        if iteration + 1 < ITERS:
            residual_halo = [
                part - step_size * change for part, change in zip(residual_halo, mapped_halo)
            ]
            terms = terms - step_size * mapped_terms
            smoothed, part = precondition(residual, residual_halo, terms)
            renewed, _, smoothed_halo = sum_and_share(part, smoothed, False)
            search = smoothed + renewed / energy * search
            search_halo = [
                part + renewed / energy * old for part, old in zip(smoothed_halo, search_halo)
            ]
            energy = renewed
    return (solution_field[None, None], residual[None, None])


def solution(mesh):
    return jax.shard_map(
        on_device,
        mesh=mesh,
        in_specs=(
            P("grp", "brick", None, None, None),
            P("grp", "brick", None, None, None),
            P("grp", "brick", None, None, None, None),
            P(),
            P(),
        ),
        out_specs=(P("grp", "brick", None, None, None), P("grp", "brick", None, None, None)),
        check_vma=False,
    )
```

```python
import functools

import jax
import jax.numpy as jnp
from jax import lax
from jax.experimental import pallas as pl
from jax.experimental.pallas import tpu as pltpu
from jax.sharding import PartitionSpec as P

MESH_IDS = pl.DeviceIdType.MESH

BS = 32
PATCH_X = 1
PATCH_Y = 2
ITERS = 3


OMEGA = 0.6


def exchange_kernel(
    x_ref, xy_ref, z_ref, o_ref, xy_out, z_out,
    landed_b, landed_g, landed_xy, landed_z,
    send_b, recv_b, send_g, recv_g, send_xy, recv_xy, send_z, recv_z,
):
    here_brick = lax.axis_index("brick")
    here_grp = lax.axis_index("grp")
    n_brick = landed_b.shape[0]
    n_grp = landed_g.shape[0]
    brick_peers = [(lax.rem(here_brick + k, n_brick), here_grp) for k in range(1, n_brick)]
    grp_peers = [(here_brick, lax.rem(here_grp + k, n_grp)) for k in range(1, n_grp)]
    barrier = pltpu.get_barrier_semaphore()
    for peer in brick_peers + grp_peers:
        pl.semaphore_signal(barrier, inc=1, device_id=peer, device_id_type=MESH_IDS)
    pl.semaphore_wait(barrier, len(brick_peers) + len(grp_peers))

    def send(src, dst, sends, recvs, index, peer):
        copy = pltpu.make_async_remote_copy(
            src_ref=src,
            dst_ref=dst.at[index],
            send_sem=sends.at[index],
            recv_sem=recvs.at[index],
            device_id=peer,
            device_id_type=MESH_IDS,
        )
        copy.start()
        return copy

    face_copies = [
        send(z_ref, landed_z, send_z, recv_z, 0, grp_peers[0]),
        send(z_ref, landed_z, send_z, recv_z, 1, grp_peers[-1]),
    ]
    face_copies += [
        send(xy_ref, landed_xy, send_xy, recv_xy, k, peer)
        for k, peer in enumerate(brick_peers, start=1)
    ]
    copies = [
        send(x_ref, landed_b, send_b, recv_b, k, peer)
        for k, peer in enumerate(brick_peers, start=1)
    ]
    landed_b[0] = x_ref[...]
    for copy in copies:
        copy.wait()
    total = landed_b[lax.rem(here_brick, n_brick)]
    for j in range(1, n_brick):
        total = total + landed_b[lax.rem(here_brick + n_brick - j, n_brick)]
    o_ref[...] = total
    landed_g[0] = total
    copies = [
        send(o_ref, landed_g, send_g, recv_g, k, peer)
        for k, peer in enumerate(grp_peers, start=1)
    ]
    for copy in copies:
        copy.wait()
    total = landed_g[lax.rem(here_grp, n_grp)]
    for j in range(1, n_grp):
        total = total + landed_g[lax.rem(here_grp + n_grp - j, n_grp)]
    o_ref[...] = total
    for copy in face_copies:
        copy.wait()
    landed_xy[0] = xy_ref[...]
    xy_out[...] = landed_xy[...]
    z_out[...] = landed_z[...]


def exchange(tile, xy, z, kernel_id):
    n_brick = lax.axis_size("brick")
    n_grp = lax.axis_size("grp")
    vmem = pl.BlockSpec(memory_space=pltpu.VMEM)
    dma = pltpu.SemaphoreType.DMA
    return pl.pallas_call(
        exchange_kernel,
        out_shape=(
            jax.ShapeDtypeStruct(tile.shape, jnp.float32),
            jax.ShapeDtypeStruct((n_brick,) + xy.shape, jnp.float32),
            jax.ShapeDtypeStruct((2,) + z.shape, jnp.float32),
        ),
        in_specs=[vmem] * 3,
        out_specs=(vmem, vmem, vmem),
        scratch_shapes=[
            pltpu.VMEM((n_brick,) + tile.shape, jnp.float32),
            pltpu.VMEM((n_grp,) + tile.shape, jnp.float32),
            pltpu.VMEM((n_brick,) + xy.shape, jnp.float32),
            pltpu.VMEM((2,) + z.shape, jnp.float32),
            dma((n_brick,)),
            dma((n_brick,)),
            dma((n_grp,)),
            dma((n_grp,)),
            dma((n_brick,)),
            dma((n_brick,)),
            dma((2,)),
            dma((2,)),
        ],
        compiler_params=pltpu.CompilerParams(collective_id=kernel_id, has_side_effects=True),
    )(tile, xy, z)


def stencil_kernel(
    coef_ref, f_ref, bonds_ref, masks_ref, diag_ref, rows_ref, faces_ref,
    o_ref, part_ref, xy_ref, z_ref, *, smooth
):
    slots, width, lanes = f_ref.shape
    row = lax.broadcasted_iota(jnp.int32, (width, lanes), 0)
    lane = lax.broadcasted_iota(jnp.int32, (width, lanes), 1)
    pick = lax.broadcasted_iota(jnp.int32, (BS, lanes), 0)
    spot = lax.broadcasted_iota(jnp.int32, (BS, lanes), 1)
    spread_z = (spot // BS == pick).astype(jnp.float32)
    spread_y = (spot % BS == pick).astype(jnp.float32)

    def spread(face, table):
        return jnp.dot(face, table, precision=lax.Precision.HIGHEST, preferred_element_type=jnp.float32)

    borders = [
        row == width - 1,
        row == 0,
        lane >= lanes - BS,
        lane < BS,
        lane % BS == BS - 1,
        lane % BS == 0,
    ]
    source_lane = lax.broadcasted_iota(jnp.int32, (lanes, BS), 0)
    place = lax.broadcasted_iota(jnp.int32, (lanes, BS), 1)
    layers = [
        (source_lane == offset + step * place).astype(jnp.float32)
        for offset, step in ((0, 1), (lanes - BS, 1), (0, BS), (BS - 1, BS))
    ]
    flat_mask = spot // BS == pick

    def flatten(layer):
        spread_out = jnp.where(flat_mask, spread(layer, spread_y), 0.0)
        return jnp.sum(spread_out, axis=0, keepdims=True)

    dot = jnp.float32(0.0)
    for s in range(slots):
        ds = diag_ref[s]
        if smooth:
            rs = f_ref[s]
            fs = OMEGA * rs / ds
        else:
            fs = f_ref[s]
        xp = jnp.where(row == width - 1, rows_ref[0, s], pltpu.roll(fs, width - 1, 0))
        xm = jnp.where(row == 0, rows_ref[1, s], pltpu.roll(fs, 1, 0))
        yp = jnp.where(lane >= lanes - BS, spread(faces_ref[0, s], spread_y), pltpu.roll(fs, lanes - BS, 1))
        ym = jnp.where(lane < BS, spread(faces_ref[1, s], spread_y), pltpu.roll(fs, BS, 1))
        zp = jnp.where(lane % BS == BS - 1, spread(faces_ref[2, s], spread_z), pltpu.roll(fs, lanes - 1, 1))
        zm = jnp.where(lane % BS == 0, spread(faces_ref[3, s], spread_z), pltpu.roll(fs, 1, 1))
        total = ds * fs
        for d, beyond in enumerate([xp, xm, yp, ym, zp, zm]):
            base = 2 * (d * slots + s)
            active = jnp.where(borders[d], masks_ref[base + 1], masks_ref[base])
            total = total - bonds_ref[d, s] * active * beyond
        if smooth:
            total = fs + OMEGA * (rs - total) / ds
            total = total + coef_ref[s]
            dot = dot + jnp.sum(rs * total)
        else:
            dot = dot + jnp.sum(fs * total)
            part_ref[1 + s] = jnp.sum(total)
        o_ref[s] = total
        xy_ref[pl.ds(s, 1), :] = total[0:1, :]
        xy_ref[pl.ds(slots + s, 1), :] = total[width - 1 : width, :]
        if s == 0:
            xy_ref[pl.ds(2 * slots, 1), :] = flatten(spread(total, layers[0]))
        if s == slots - 1:
            xy_ref[pl.ds(2 * slots + 1, 1), :] = flatten(spread(total, layers[1]))
        z_ref[pl.ds(s, 1), :] = flatten(spread(total, layers[2]))
        z_ref[pl.ds(slots + s, 1), :] = flatten(spread(total, layers[3]))
    part_ref[0] = dot
    if smooth:
        for s in range(slots):
            part_ref[1 + s] = jnp.float32(0.0)


def stencil(field, bonds, masks, diag, rows, faces, coef=None):
    slots = field.shape[0]
    smooth = coef is not None
    if coef is None:
        coef = jnp.zeros((slots,), jnp.float32)
    vmem = pl.BlockSpec(memory_space=pltpu.VMEM)
    smem = pl.BlockSpec(memory_space=pltpu.SMEM)
    return pl.pallas_call(
        functools.partial(stencil_kernel, smooth=smooth),
        out_shape=(
            jax.ShapeDtypeStruct(field.shape, jnp.float32),
            jax.ShapeDtypeStruct((1 + slots,), jnp.float32),
            jax.ShapeDtypeStruct((2 * slots + 2, field.shape[2]), jnp.float32),
            jax.ShapeDtypeStruct((2 * slots, field.shape[2]), jnp.float32),
        ),
        in_specs=[smem, vmem, vmem, smem, vmem, vmem, vmem],
        out_specs=(vmem, smem, vmem, vmem),
    )(coef, field, bonds, masks, diag, rows, faces)


def assemble(coarse_diag, couplings, strides):
    extent = coarse_diag.shape[0]
    matrix = jnp.diag(coarse_diag)
    for coupling, stride in zip(couplings, strides):
        banded = coupling[: extent - stride]
        matrix = matrix - jnp.diag(banded, stride) - jnp.diag(banded, -stride)
    return matrix


def on_device(source, uptake, conductance, occupancy, assignment):
    face_size = BS * BS
    slot_count = PATCH_X * PATCH_Y
    slab_index = lax.axis_index("grp")
    brick_index = lax.axis_index("brick")
    brick_count = lax.axis_size("brick")
    across = brick_count // 2
    peer_ids = jnp.arange(brick_count, dtype=jnp.int32)
    patch_index = assignment[brick_index]
    patch_row = patch_index // across
    patch_column = patch_index % across

    def owner_of(row_shift, column_shift):
        row_target = patch_row + row_shift
        column_target = patch_column + column_shift
        inside = (
            (row_target >= 0) & (row_target < 2) & (column_target >= 0) & (column_target < across)
        )
        holder = jnp.sum(jnp.where(assignment == row_target * across + column_target, peer_ids, 0))
        return jnp.where(inside, holder, -1)

    wanted = jnp.stack([owner_of(1, 0), owner_of(-1, 0), owner_of(0, 1), owner_of(0, -1)])
    padded = jnp.pad(occupancy, 1)
    window = lax.dynamic_slice(
        padded,
        (slab_index, patch_row * PATCH_X, patch_column * PATCH_Y),
        (3, PATCH_X + 2, PATCH_Y + 2),
    ).astype(jnp.float32)
    centre = window[1, 1:-1, 1:-1].reshape(slot_count)
    toward = [
        window[1, 2:, 1:-1],
        window[1, :-2, 1:-1],
        window[1, 1:-1, 2:],
        window[1, 1:-1, :-2],
        window[2, 1:-1, 1:-1],
        window[0, 1:-1, 1:-1],
    ]
    first_axis = lax.broadcasted_iota(jnp.int32, (1, BS, face_size), 1)
    flat_axis = lax.broadcasted_iota(jnp.int32, (1, BS, face_size), 2)
    second_axis = flat_axis // BS
    third_axis = flat_axis % BS
    cube_third = lax.broadcasted_iota(jnp.int32, (1, BS, BS, BS), 3)
    borders = [
        first_axis == BS - 1,
        first_axis == 0,
        second_axis == BS - 1,
        second_axis == 0,
        third_axis == BS - 1,
        third_axis == 0,
    ]
    bonds = conductance[0, 0]
    live_here = centre[:, None, None]
    effective = []
    for direction in range(6):
        neighbour_live = toward[direction].reshape(slot_count)[:, None, None]
        active = jnp.where(borders[direction], live_here * neighbour_live, live_here)
        effective.append(bonds[direction] * active)
    absorb = uptake[0, 0]
    diagonal = absorb
    for direction in range(6):
        diagonal = diagonal + effective[direction]

    masks = jnp.stack(
        [
            jnp.stack([centre, centre * toward[direction].reshape(slot_count)], axis=1)
            for direction in range(6)
        ]
    ).reshape(-1)

    lane_ids = jnp.arange(face_size, dtype=jnp.int32)[:, None]
    layer_ids = BS * jnp.arange(BS, dtype=jnp.int32)[None, :]
    picker = jnp.concatenate([lane_ids == layer_ids, lane_ids == layer_ids + BS - 1], axis=1)
    picker = picker.astype(jnp.float32)

    def side_faces(field):
        picked = jnp.dot(
            field.reshape(slot_count * BS, face_size), picker, precision=lax.Precision.HIGHEST
        )
        z = picked.reshape(slot_count, BS, 2, BS).transpose(2, 0, 1, 3)
        xy = jnp.concatenate(
            [
                field[:, 0, :],
                field[:, BS - 1, :],
                field[0, :, :BS].reshape(1, face_size),
                field[slot_count - 1, :, face_size - BS :].reshape(1, face_size),
            ]
        )
        return xy, z.reshape(2 * slot_count, face_size)

    def pick(landed, holder, fill):
        offset = lax.rem(brick_index - holder + brick_count, brick_count)
        got = lax.dynamic_index_in_dim(landed, offset, keepdims=False)
        return jnp.where(holder >= 0, got, fill)

    def halo(field, xy_land, z_land, fill):
        xplus = pick(xy_land, wanted[0], fill)
        xminus = pick(xy_land, wanted[1], fill)
        yplus = pick(xy_land, wanted[2], fill)
        yminus = pick(xy_land, wanted[3], fill)
        rows = jnp.stack([xplus[:slot_count], xminus[slot_count : 2 * slot_count]])[:, :, None, :]
        beyond_yplus = jnp.stack([field[1, :, :BS], yplus[2 * slot_count].reshape(BS, BS)])
        beyond_yminus = jnp.stack(
            [yminus[2 * slot_count + 1].reshape(BS, BS), field[0, :, face_size - BS :]]
        )
        above = jnp.where(slab_index < grp_count - 1, z_land[1, :slot_count], fill)
        below = jnp.where(slab_index > 0, z_land[0, slot_count:], fill)
        faces = jnp.stack(
            [
                beyond_yplus,
                beyond_yminus,
                above.reshape(slot_count, BS, BS),
                below.reshape(slot_count, BS, BS),
            ]
        )
        return rows, faces

    slot_ids = jnp.arange(slot_count)
    brick_first = slot_ids // PATCH_Y
    brick_second = slot_ids % PATCH_Y
    inside = [
        (brick_first < PATCH_X - 1).astype(jnp.float32),
        (brick_first > 0).astype(jnp.float32),
        (brick_second < PATCH_Y - 1).astype(jnp.float32),
        (brick_second > 0).astype(jnp.float32),
    ]
    face_sums = [
        jnp.sum(effective[0][:, BS - 1, :], axis=1),
        jnp.sum(effective[1][:, 0, :], axis=1),
        jnp.sum(effective[2][:, :, face_size - BS :], axis=(1, 2)),
        jnp.sum(effective[3][:, :, :BS], axis=(1, 2)),
        jnp.sum(jnp.where(borders[4], effective[4], 0.0), axis=(1, 2)),
        jnp.sum(jnp.where(borders[5], effective[5], 0.0), axis=(1, 2)),
    ]
    coarse_diag = jnp.sum(absorb, axis=(1, 2))
    for direction in range(4):
        coarse_diag = coarse_diag + face_sums[direction] * inside[direction]
    coarse_diag = coarse_diag + face_sums[4] + face_sums[5]
    grp_count = lax.axis_size("grp")
    grp_ids = jnp.arange(grp_count, dtype=jnp.int32)

    def slab_slot(values):
        here = (grp_ids == slab_index).astype(jnp.float32)
        return here[:, None, None] * values[None]

    forcing = source[0, 0] * live_here

    def as_tile(values):
        rows = -(-values.shape[0] // 128)
        rows = -(-rows // 8) * 8
        return jnp.pad(values, (0, rows * 128 - values.shape[0])).reshape(rows, 128)

    record = jnp.stack(
        [
            coarse_diag,
            face_sums[0] * inside[0],
            face_sums[2] * inside[2],
            face_sums[4],
            jnp.sum(forcing, axis=(1, 2)),
        ]
    )
    brick_here = (peer_ids == brick_index).astype(jnp.float32)
    spread = (brick_here[:, None, None, None] * slab_slot(record)[None]).reshape(-1)
    forcing_xy, forcing_z = side_faces(forcing)
    diagonal_xy, diagonal_z = side_faces(diagonal)
    summed, xy_land, z_land = exchange(
        as_tile(spread),
        jnp.concatenate([forcing_xy, diagonal_xy]),
        jnp.concatenate([forcing_z, diagonal_z]),
        2,
    )
    summed = summed.reshape(-1)[: spread.shape[0]]
    xy_rows = forcing_xy.shape[0]
    z_rows = forcing_z.shape[0]
    residual_halo = halo(forcing, xy_land[:, :xy_rows], z_land[:, :z_rows], 0.0)
    diagonal_halo = halo(diagonal, xy_land[:, xy_rows:], z_land[:, z_rows:], 1.0)
    gathered = lax.dynamic_index_in_dim(
        summed.reshape(brick_count, grp_count, 5, slot_count), brick_index, keepdims=False
    )
    columns = jnp.transpose(gathered, (1, 0, 2)).reshape(5, -1)
    matrix = assemble(columns[0], (columns[1], columns[2], columns[3]), (PATCH_Y, 1, slot_count))
    factor = jnp.linalg.cholesky(matrix)

    def coarse_solve(terms):
        middle = lax.linalg.triangular_solve(factor, terms[:, None], left_side=True, lower=True)
        result = lax.linalg.triangular_solve(
            factor, middle, left_side=True, lower=True, transpose_a=True
        )
        return lax.dynamic_slice_in_dim(result[:, 0], slab_index * slot_count, slot_count)

    def precondition(residual_field, field_halo, terms):
        smoothed_halo = [OMEGA * part / scale for part, scale in zip(field_halo, diagonal_halo)]
        return stencil(
            residual_field, bonds, masks, diagonal, *smoothed_halo, coef=coarse_solve(terms)
        )

    def sum_and_share(part, field, xy, z, with_sums):
        values = [part[:1]]
        if with_sums:
            sums = slab_slot(part[1:][None])[:, 0]
            values.append((brick_here[:, None, None] * sums[None]).reshape(-1))
        packed = jnp.concatenate(values)
        total, xy_land, z_land = exchange(as_tile(packed), xy, z, 1)
        total = total.reshape(-1)[: packed.shape[0]]
        field_halo = halo(field, xy_land, z_land, 0.0)
        if not with_sums:
            return total[0], None, field_halo
        mine = lax.dynamic_index_in_dim(
            total[1:].reshape(brick_count, -1), brick_index, keepdims=False
        )
        return total[0], mine, field_halo

    terms = columns[4]
    solution_field = jnp.zeros_like(forcing)
    residual = forcing
    search, part, xy, z = precondition(residual, residual_halo, terms)
    energy, _, search_halo = sum_and_share(part, search, xy, z, False)
    for iteration in range(ITERS):
        mapped, part, xy, z = stencil(search, bonds, masks, diagonal, *search_halo)
        curvature, mapped_terms, mapped_halo = sum_and_share(part, mapped, xy, z, True)
        step_size = energy / curvature
        solution_field = solution_field + step_size * search
        residual = residual - step_size * mapped
        if iteration + 1 < ITERS:
            residual_halo = [
                part - step_size * change for part, change in zip(residual_halo, mapped_halo)
            ]
            terms = terms - step_size * mapped_terms
            smoothed, part, xy, z = precondition(residual, residual_halo, terms)
            renewed, _, smoothed_halo = sum_and_share(part, smoothed, xy, z, False)
            search = smoothed + renewed / energy * search
            search_halo = [
                part + renewed / energy * old for part, old in zip(smoothed_halo, search_halo)
            ]
            energy = renewed
    return (solution_field[None, None], residual[None, None])


def solution(mesh):
    return jax.shard_map(
        on_device,
        mesh=mesh,
        in_specs=(
            P("grp", "brick", None, None, None),
            P("grp", "brick", None, None, None),
            P("grp", "brick", None, None, None, None),
            P(),
            P(),
        ),
        out_specs=(P("grp", "brick", None, None, None), P("grp", "brick", None, None, None)),
        check_vma=False,
    )
```

```python
import functools

import jax
import jax.numpy as jnp
from jax import lax
from jax.experimental import pallas as pl
from jax.experimental.pallas import tpu as pltpu
from jax.sharding import PartitionSpec as P

MESH_IDS = pl.DeviceIdType.MESH

BS = 32
PATCH_X = 1
PATCH_Y = 2
ITERS = 3


OMEGA = 0.6


def share(
    x_ref, xy_ref, z_ref, o_ref, xy_out, z_out, landed_b, landed_g, landed_xy, landed_z,
    send_b, recv_b, send_g, recv_g, send_xy, recv_xy, send_z, recv_z, brick_peers, grp_peers,
):
    here_brick = lax.axis_index("brick")
    here_grp = lax.axis_index("grp")
    n_brick = landed_b.shape[0]
    n_grp = landed_g.shape[0]

    def send(src, dst, sends, recvs, index, peer):
        copy = pltpu.make_async_remote_copy(
            src_ref=src,
            dst_ref=dst.at[index],
            send_sem=sends.at[index],
            recv_sem=recvs.at[index],
            device_id=peer,
            device_id_type=MESH_IDS,
        )
        copy.start()
        return copy

    face_copies = [
        send(z_ref, landed_z, send_z, recv_z, 0, grp_peers[0]),
        send(z_ref, landed_z, send_z, recv_z, 1, grp_peers[-1]),
    ]
    face_copies += [
        send(xy_ref, landed_xy, send_xy, recv_xy, k, peer)
        for k, peer in enumerate(brick_peers, start=1)
    ]
    copies = [
        send(x_ref, landed_b, send_b, recv_b, k, peer)
        for k, peer in enumerate(brick_peers, start=1)
    ]
    landed_b[0] = x_ref[...]
    for copy in copies:
        copy.wait()
    total = landed_b[lax.rem(here_brick, n_brick)]
    for j in range(1, n_brick):
        total = total + landed_b[lax.rem(here_brick + n_brick - j, n_brick)]
    o_ref[...] = total
    landed_g[0] = total
    copies = [
        send(o_ref, landed_g, send_g, recv_g, k, peer)
        for k, peer in enumerate(grp_peers, start=1)
    ]
    for copy in copies:
        copy.wait()
    total = landed_g[lax.rem(here_grp, n_grp)]
    for j in range(1, n_grp):
        total = total + landed_g[lax.rem(here_grp + n_grp - j, n_grp)]
    o_ref[...] = total
    for copy in face_copies:
        copy.wait()
    landed_xy[0] = xy_ref[...]
    xy_out[...] = landed_xy[...]
    z_out[...] = landed_z[...]


def exchange_kernel(
    x_ref, xy_ref, z_ref, o_ref, xy_out, z_out,
    landed_b, landed_g, landed_xy, landed_z,
    send_b, recv_b, send_g, recv_g, send_xy, recv_xy, send_z, recv_z,
):
    here_brick = lax.axis_index("brick")
    here_grp = lax.axis_index("grp")
    n_brick = landed_b.shape[0]
    n_grp = landed_g.shape[0]
    brick_peers = [(lax.rem(here_brick + k, n_brick), here_grp) for k in range(1, n_brick)]
    grp_peers = [(here_brick, lax.rem(here_grp + k, n_grp)) for k in range(1, n_grp)]
    barrier = pltpu.get_barrier_semaphore()
    for peer in brick_peers + grp_peers:
        pl.semaphore_signal(barrier, inc=1, device_id=peer, device_id_type=MESH_IDS)
    pl.semaphore_wait(barrier, len(brick_peers) + len(grp_peers))

    share(
        x_ref, xy_ref, z_ref, o_ref, xy_out, z_out, landed_b, landed_g, landed_xy, landed_z,
        send_b, recv_b, send_g, recv_g, send_xy, recv_xy, send_z, recv_z, brick_peers, grp_peers,
    )


def exchange(tile, xy, z, kernel_id):
    n_brick = lax.axis_size("brick")
    n_grp = lax.axis_size("grp")
    vmem = pl.BlockSpec(memory_space=pltpu.VMEM)
    dma = pltpu.SemaphoreType.DMA
    return pl.pallas_call(
        exchange_kernel,
        out_shape=(
            jax.ShapeDtypeStruct(tile.shape, jnp.float32),
            jax.ShapeDtypeStruct((n_brick,) + xy.shape, jnp.float32),
            jax.ShapeDtypeStruct((2,) + z.shape, jnp.float32),
        ),
        in_specs=[vmem] * 3,
        out_specs=(vmem, vmem, vmem),
        scratch_shapes=[
            pltpu.VMEM((n_brick,) + tile.shape, jnp.float32),
            pltpu.VMEM((n_grp,) + tile.shape, jnp.float32),
            pltpu.VMEM((n_brick,) + xy.shape, jnp.float32),
            pltpu.VMEM((2,) + z.shape, jnp.float32),
            dma((n_brick,)),
            dma((n_brick,)),
            dma((n_grp,)),
            dma((n_grp,)),
            dma((n_brick,)),
            dma((n_brick,)),
            dma((2,)),
            dma((2,)),
        ],
        compiler_params=pltpu.CompilerParams(collective_id=kernel_id, has_side_effects=True),
    )(tile, xy, z)


def stencil_body(
    coef_ref, f_ref, bonds_ref, masks_ref, diag_ref, rows_ref, faces_ref, o_ref, xy_ref, z_ref, smooth
):
    slots, width, lanes = f_ref.shape
    row = lax.broadcasted_iota(jnp.int32, (width, lanes), 0)
    lane = lax.broadcasted_iota(jnp.int32, (width, lanes), 1)
    pick = lax.broadcasted_iota(jnp.int32, (BS, lanes), 0)
    spot = lax.broadcasted_iota(jnp.int32, (BS, lanes), 1)
    spread_z = (spot // BS == pick).astype(jnp.float32)
    spread_y = (spot % BS == pick).astype(jnp.float32)

    def spread(face, table):
        return jnp.dot(face, table, precision=lax.Precision.HIGHEST, preferred_element_type=jnp.float32)

    borders = [
        row == width - 1,
        row == 0,
        lane >= lanes - BS,
        lane < BS,
        lane % BS == BS - 1,
        lane % BS == 0,
    ]
    source_lane = lax.broadcasted_iota(jnp.int32, (lanes, BS), 0)
    place = lax.broadcasted_iota(jnp.int32, (lanes, BS), 1)
    layers = [
        (source_lane == offset + step * place).astype(jnp.float32)
        for offset, step in ((0, 1), (lanes - BS, 1), (0, BS), (BS - 1, BS))
    ]
    flat_mask = spot // BS == pick

    def flatten(layer):
        spread_out = jnp.where(flat_mask, spread(layer, spread_y), 0.0)
        return jnp.sum(spread_out, axis=0, keepdims=True)

    dot = jnp.float32(0.0)
    sums = []
    for s in range(slots):
        ds = diag_ref[s]
        if smooth:
            rs = f_ref[s]
            fs = OMEGA * rs / ds
        else:
            fs = f_ref[s]
        xp = jnp.where(row == width - 1, rows_ref[0, s], pltpu.roll(fs, width - 1, 0))
        xm = jnp.where(row == 0, rows_ref[1, s], pltpu.roll(fs, 1, 0))
        yp = jnp.where(lane >= lanes - BS, spread(faces_ref[0, s], spread_y), pltpu.roll(fs, lanes - BS, 1))
        ym = jnp.where(lane < BS, spread(faces_ref[1, s], spread_y), pltpu.roll(fs, BS, 1))
        zp = jnp.where(lane % BS == BS - 1, spread(faces_ref[2, s], spread_z), pltpu.roll(fs, lanes - 1, 1))
        zm = jnp.where(lane % BS == 0, spread(faces_ref[3, s], spread_z), pltpu.roll(fs, 1, 1))
        total = ds * fs
        for d, beyond in enumerate([xp, xm, yp, ym, zp, zm]):
            base = 2 * (d * slots + s)
            active = jnp.where(borders[d], masks_ref[base + 1], masks_ref[base])
            total = total - bonds_ref[d, s] * active * beyond
        if smooth:
            total = fs + OMEGA * (rs - total) / ds
            total = total + coef_ref[s]
            dot = dot + jnp.sum(rs * total)
        else:
            dot = dot + jnp.sum(fs * total)
            sums.append(jnp.sum(total))
        o_ref[s] = total
        xy_ref[pl.ds(s, 1), :] = total[0:1, :]
        xy_ref[pl.ds(slots + s, 1), :] = total[width - 1 : width, :]
        if s == 0:
            xy_ref[pl.ds(2 * slots, 1), :] = flatten(spread(total, layers[0]))
        if s == slots - 1:
            xy_ref[pl.ds(2 * slots + 1, 1), :] = flatten(spread(total, layers[1]))
        z_ref[pl.ds(s, 1), :] = flatten(spread(total, layers[2]))
        z_ref[pl.ds(slots + s, 1), :] = flatten(spread(total, layers[3]))
    return dot, sums


def round_kernel(
    coef_ref, f_ref, bonds_ref, masks_ref, diag_ref, rows_ref, faces_ref,
    o_ref, total_ref, xy_out, z_out,
    xy_buf, z_buf, tile_buf, landed_b, landed_g, landed_xy, landed_z,
    send_b, recv_b, send_g, recv_g, send_xy, recv_xy, send_z, recv_z, *, smooth
):
    here_brick = lax.axis_index("brick")
    here_grp = lax.axis_index("grp")
    n_brick = landed_b.shape[0]
    n_grp = landed_g.shape[0]
    brick_peers = [(lax.rem(here_brick + k, n_brick), here_grp) for k in range(1, n_brick)]
    grp_peers = [(here_brick, lax.rem(here_grp + k, n_grp)) for k in range(1, n_grp)]
    barrier = pltpu.get_barrier_semaphore()
    for peer in brick_peers + grp_peers:
        pl.semaphore_signal(barrier, inc=1, device_id=peer, device_id_type=MESH_IDS)
    dot, sums = stencil_body(
        coef_ref, f_ref, bonds_ref, masks_ref, diag_ref, rows_ref, faces_ref, o_ref, xy_buf, z_buf,
        smooth,
    )
    tile_rows, tile_lanes = tile_buf.shape
    flat = lax.broadcasted_iota(jnp.int32, (tile_rows, tile_lanes), 0) * tile_lanes
    flat = flat + lax.broadcasted_iota(jnp.int32, (tile_rows, tile_lanes), 1)
    tile = jnp.where(flat == 0, dot, 0.0)
    slots = f_ref.shape[0]
    for s, value in enumerate(sums):
        position = 1 + (here_brick * n_grp + here_grp) * slots + s
        tile = jnp.where(flat == position, value, tile)
    tile_buf[...] = tile
    pl.semaphore_wait(barrier, len(brick_peers) + len(grp_peers))
    share(
        tile_buf, xy_buf, z_buf, total_ref, xy_out, z_out, landed_b, landed_g, landed_xy, landed_z,
        send_b, recv_b, send_g, recv_g, send_xy, recv_xy, send_z, recv_z, brick_peers, grp_peers,
    )


def one_round(field, bonds, masks, diag, rows, faces, coef, smooth):
    slots, _, lanes = field.shape
    n_brick = lax.axis_size("brick")
    n_grp = lax.axis_size("grp")
    tile = (8, 128)
    xy = (2 * slots + 2, lanes)
    z = (2 * slots, lanes)
    vmem = pl.BlockSpec(memory_space=pltpu.VMEM)
    smem = pl.BlockSpec(memory_space=pltpu.SMEM)
    dma = pltpu.SemaphoreType.DMA
    return pl.pallas_call(
        functools.partial(round_kernel, smooth=smooth),
        out_shape=(
            jax.ShapeDtypeStruct(field.shape, jnp.float32),
            jax.ShapeDtypeStruct(tile, jnp.float32),
            jax.ShapeDtypeStruct((n_brick,) + xy, jnp.float32),
            jax.ShapeDtypeStruct((2,) + z, jnp.float32),
        ),
        in_specs=[smem, vmem, vmem, smem, vmem, vmem, vmem],
        out_specs=(vmem, vmem, vmem, vmem),
        scratch_shapes=[
            pltpu.VMEM(xy, jnp.float32),
            pltpu.VMEM(z, jnp.float32),
            pltpu.VMEM(tile, jnp.float32),
            pltpu.VMEM((n_brick,) + tile, jnp.float32),
            pltpu.VMEM((n_grp,) + tile, jnp.float32),
            pltpu.VMEM((n_brick,) + xy, jnp.float32),
            pltpu.VMEM((2,) + z, jnp.float32),
            dma((n_brick,)),
            dma((n_brick,)),
            dma((n_grp,)),
            dma((n_grp,)),
            dma((n_brick,)),
            dma((n_brick,)),
            dma((2,)),
            dma((2,)),
        ],
        compiler_params=pltpu.CompilerParams(
            collective_id=3 if smooth else 1, has_side_effects=True
        ),
    )(coef, field, bonds, masks, diag, rows, faces)


def assemble(coarse_diag, couplings, strides):
    extent = coarse_diag.shape[0]
    matrix = jnp.diag(coarse_diag)
    for coupling, stride in zip(couplings, strides):
        banded = coupling[: extent - stride]
        matrix = matrix - jnp.diag(banded, stride) - jnp.diag(banded, -stride)
    return matrix


def on_device(source, uptake, conductance, occupancy, assignment):
    face_size = BS * BS
    slot_count = PATCH_X * PATCH_Y
    slab_index = lax.axis_index("grp")
    brick_index = lax.axis_index("brick")
    brick_count = lax.axis_size("brick")
    across = brick_count // 2
    peer_ids = jnp.arange(brick_count, dtype=jnp.int32)
    patch_index = assignment[brick_index]
    patch_row = patch_index // across
    patch_column = patch_index % across

    def owner_of(row_shift, column_shift):
        row_target = patch_row + row_shift
        column_target = patch_column + column_shift
        inside = (
            (row_target >= 0) & (row_target < 2) & (column_target >= 0) & (column_target < across)
        )
        holder = jnp.sum(jnp.where(assignment == row_target * across + column_target, peer_ids, 0))
        return jnp.where(inside, holder, -1)

    wanted = jnp.stack([owner_of(1, 0), owner_of(-1, 0), owner_of(0, 1), owner_of(0, -1)])
    padded = jnp.pad(occupancy, 1)
    window = lax.dynamic_slice(
        padded,
        (slab_index, patch_row * PATCH_X, patch_column * PATCH_Y),
        (3, PATCH_X + 2, PATCH_Y + 2),
    ).astype(jnp.float32)
    centre = window[1, 1:-1, 1:-1].reshape(slot_count)
    toward = [
        window[1, 2:, 1:-1],
        window[1, :-2, 1:-1],
        window[1, 1:-1, 2:],
        window[1, 1:-1, :-2],
        window[2, 1:-1, 1:-1],
        window[0, 1:-1, 1:-1],
    ]
    first_axis = lax.broadcasted_iota(jnp.int32, (1, BS, face_size), 1)
    flat_axis = lax.broadcasted_iota(jnp.int32, (1, BS, face_size), 2)
    second_axis = flat_axis // BS
    third_axis = flat_axis % BS
    cube_third = lax.broadcasted_iota(jnp.int32, (1, BS, BS, BS), 3)
    borders = [
        first_axis == BS - 1,
        first_axis == 0,
        second_axis == BS - 1,
        second_axis == 0,
        third_axis == BS - 1,
        third_axis == 0,
    ]
    bonds = conductance[0, 0]
    live_here = centre[:, None, None]
    effective = []
    for direction in range(6):
        neighbour_live = toward[direction].reshape(slot_count)[:, None, None]
        active = jnp.where(borders[direction], live_here * neighbour_live, live_here)
        effective.append(bonds[direction] * active)
    absorb = uptake[0, 0]
    diagonal = absorb
    for direction in range(6):
        diagonal = diagonal + effective[direction]

    masks = jnp.stack(
        [
            jnp.stack([centre, centre * toward[direction].reshape(slot_count)], axis=1)
            for direction in range(6)
        ]
    ).reshape(-1)

    lane_ids = jnp.arange(face_size, dtype=jnp.int32)[:, None]
    layer_ids = BS * jnp.arange(BS, dtype=jnp.int32)[None, :]
    picker = jnp.concatenate([lane_ids == layer_ids, lane_ids == layer_ids + BS - 1], axis=1)
    picker = picker.astype(jnp.float32)

    def side_faces(field):
        picked = jnp.dot(
            field.reshape(slot_count * BS, face_size), picker, precision=lax.Precision.HIGHEST
        )
        z = picked.reshape(slot_count, BS, 2, BS).transpose(2, 0, 1, 3)
        xy = jnp.concatenate(
            [
                field[:, 0, :],
                field[:, BS - 1, :],
                field[0, :, :BS].reshape(1, face_size),
                field[slot_count - 1, :, face_size - BS :].reshape(1, face_size),
            ]
        )
        return xy, z.reshape(2 * slot_count, face_size)

    def pick(landed, holder, fill):
        offset = lax.rem(brick_index - holder + brick_count, brick_count)
        got = lax.dynamic_index_in_dim(landed, offset, keepdims=False)
        return jnp.where(holder >= 0, got, fill)

    def halo(field, xy_land, z_land, fill):
        xplus = pick(xy_land, wanted[0], fill)
        xminus = pick(xy_land, wanted[1], fill)
        yplus = pick(xy_land, wanted[2], fill)
        yminus = pick(xy_land, wanted[3], fill)
        rows = jnp.stack([xplus[:slot_count], xminus[slot_count : 2 * slot_count]])[:, :, None, :]
        beyond_yplus = jnp.stack([field[1, :, :BS], yplus[2 * slot_count].reshape(BS, BS)])
        beyond_yminus = jnp.stack(
            [yminus[2 * slot_count + 1].reshape(BS, BS), field[0, :, face_size - BS :]]
        )
        above = jnp.where(slab_index < grp_count - 1, z_land[1, :slot_count], fill)
        below = jnp.where(slab_index > 0, z_land[0, slot_count:], fill)
        faces = jnp.stack(
            [
                beyond_yplus,
                beyond_yminus,
                above.reshape(slot_count, BS, BS),
                below.reshape(slot_count, BS, BS),
            ]
        )
        return rows, faces

    slot_ids = jnp.arange(slot_count)
    brick_first = slot_ids // PATCH_Y
    brick_second = slot_ids % PATCH_Y
    inside = [
        (brick_first < PATCH_X - 1).astype(jnp.float32),
        (brick_first > 0).astype(jnp.float32),
        (brick_second < PATCH_Y - 1).astype(jnp.float32),
        (brick_second > 0).astype(jnp.float32),
    ]
    face_sums = [
        jnp.sum(effective[0][:, BS - 1, :], axis=1),
        jnp.sum(effective[1][:, 0, :], axis=1),
        jnp.sum(effective[2][:, :, face_size - BS :], axis=(1, 2)),
        jnp.sum(effective[3][:, :, :BS], axis=(1, 2)),
        jnp.sum(jnp.where(borders[4], effective[4], 0.0), axis=(1, 2)),
        jnp.sum(jnp.where(borders[5], effective[5], 0.0), axis=(1, 2)),
    ]
    coarse_diag = jnp.sum(absorb, axis=(1, 2))
    for direction in range(4):
        coarse_diag = coarse_diag + face_sums[direction] * inside[direction]
    coarse_diag = coarse_diag + face_sums[4] + face_sums[5]
    grp_count = lax.axis_size("grp")
    grp_ids = jnp.arange(grp_count, dtype=jnp.int32)

    def slab_slot(values):
        here = (grp_ids == slab_index).astype(jnp.float32)
        return here[:, None, None] * values[None]

    forcing = source[0, 0] * live_here

    def as_tile(values):
        rows = -(-values.shape[0] // 128)
        rows = -(-rows // 8) * 8
        return jnp.pad(values, (0, rows * 128 - values.shape[0])).reshape(rows, 128)

    record = jnp.stack(
        [
            coarse_diag,
            face_sums[0] * inside[0],
            face_sums[2] * inside[2],
            face_sums[4],
            jnp.sum(forcing, axis=(1, 2)),
        ]
    )
    brick_here = (peer_ids == brick_index).astype(jnp.float32)
    spread = (brick_here[:, None, None, None] * slab_slot(record)[None]).reshape(-1)
    forcing_xy, forcing_z = side_faces(forcing)
    diagonal_xy, diagonal_z = side_faces(diagonal)
    summed, xy_land, z_land = exchange(
        as_tile(spread),
        jnp.concatenate([forcing_xy, diagonal_xy]),
        jnp.concatenate([forcing_z, diagonal_z]),
        2,
    )
    summed = summed.reshape(-1)[: spread.shape[0]]
    xy_rows = forcing_xy.shape[0]
    z_rows = forcing_z.shape[0]
    residual_halo = halo(forcing, xy_land[:, :xy_rows], z_land[:, :z_rows], 0.0)
    diagonal_halo = halo(diagonal, xy_land[:, xy_rows:], z_land[:, z_rows:], 1.0)
    gathered = lax.dynamic_index_in_dim(
        summed.reshape(brick_count, grp_count, 5, slot_count), brick_index, keepdims=False
    )
    columns = jnp.transpose(gathered, (1, 0, 2)).reshape(5, -1)
    matrix = assemble(columns[0], (columns[1], columns[2], columns[3]), (PATCH_Y, 1, slot_count))
    factor = jnp.linalg.cholesky(matrix)

    def coarse_solve(terms):
        middle = lax.linalg.triangular_solve(factor, terms[:, None], left_side=True, lower=True)
        result = lax.linalg.triangular_solve(
            factor, middle, left_side=True, lower=True, transpose_a=True
        )
        return lax.dynamic_slice_in_dim(result[:, 0], slab_index * slot_count, slot_count)

    def round_trip(field, field_halo, coef, smooth):
        out, total, xy_land, z_land = one_round(
            field, bonds, masks, diagonal, *field_halo, coef, smooth
        )
        total = total.reshape(-1)
        out_halo = halo(out, xy_land, z_land, 0.0)
        if smooth:
            return out, total[0], None, out_halo
        count = brick_count * grp_count * slot_count
        mine = lax.dynamic_index_in_dim(
            total[1 : 1 + count].reshape(brick_count, -1), brick_index, keepdims=False
        )
        return out, total[0], mine, out_halo

    def precondition(residual_field, field_halo, terms):
        smoothed_halo = [OMEGA * part / scale for part, scale in zip(field_halo, diagonal_halo)]
        return round_trip(residual_field, smoothed_halo, coarse_solve(terms), True)

    no_coarse = jnp.zeros((slot_count,), jnp.float32)
    terms = columns[4]
    solution_field = jnp.zeros_like(forcing)
    residual = forcing
    search, energy, _, search_halo = precondition(residual, residual_halo, terms)
    for iteration in range(ITERS):
        mapped, curvature, mapped_terms, mapped_halo = round_trip(
            search, search_halo, no_coarse, False
        )
        step_size = energy / curvature
        solution_field = solution_field + step_size * search
        residual = residual - step_size * mapped
        if iteration + 1 < ITERS:
            residual_halo = [
                part - step_size * change for part, change in zip(residual_halo, mapped_halo)
            ]
            terms = terms - step_size * mapped_terms
            smoothed, renewed, _, smoothed_halo = precondition(residual, residual_halo, terms)
            search = smoothed + renewed / energy * search
            search_halo = [
                part + renewed / energy * old for part, old in zip(smoothed_halo, search_halo)
            ]
            energy = renewed
    return (solution_field[None, None], residual[None, None])


def solution(mesh):
    return jax.shard_map(
        on_device,
        mesh=mesh,
        in_specs=(
            P("grp", "brick", None, None, None),
            P("grp", "brick", None, None, None),
            P("grp", "brick", None, None, None, None),
            P(),
            P(),
        ),
        out_specs=(P("grp", "brick", None, None, None), P("grp", "brick", None, None, None)),
        check_vma=False,
    )
```

```python
import functools

import jax
import jax.numpy as jnp
from jax import lax
from jax.experimental import pallas as pl
from jax.experimental.pallas import tpu as pltpu
from jax.sharding import PartitionSpec as P

MESH_IDS = pl.DeviceIdType.MESH

BS = 32
PATCH_X = 1
PATCH_Y = 2
ITERS = 3


OMEGA = 0.6


def share(
    x_ref, xy_ref, z_ref, o_ref, xy_out, z_out, landed_b, landed_g, landed_xy, landed_z,
    send_b, recv_b, send_g, recv_g, send_xy, recv_xy, send_z, recv_z, brick_peers, grp_peers,
):
    here_brick = lax.axis_index("brick")
    here_grp = lax.axis_index("grp")
    n_brick = landed_b.shape[0]
    n_grp = landed_g.shape[0]

    def send(src, dst, sends, recvs, index, peer):
        copy = pltpu.make_async_remote_copy(
            src_ref=src,
            dst_ref=dst.at[index],
            send_sem=sends.at[index],
            recv_sem=recvs.at[index],
            device_id=peer,
            device_id_type=MESH_IDS,
        )
        copy.start()
        return copy

    face_copies = [
        send(z_ref, landed_z, send_z, recv_z, 0, grp_peers[0]),
        send(z_ref, landed_z, send_z, recv_z, 1, grp_peers[-1]),
    ]
    face_copies += [
        send(xy_ref, landed_xy, send_xy, recv_xy, k, peer)
        for k, peer in enumerate(brick_peers, start=1)
    ]
    copies = [
        send(x_ref, landed_b, send_b, recv_b, k, peer)
        for k, peer in enumerate(brick_peers, start=1)
    ]
    landed_b[0] = x_ref[...]
    for copy in copies:
        copy.wait()
    total = landed_b[lax.rem(here_brick, n_brick)]
    for j in range(1, n_brick):
        total = total + landed_b[lax.rem(here_brick + n_brick - j, n_brick)]
    o_ref[...] = total
    landed_g[0] = total
    copies = [
        send(o_ref, landed_g, send_g, recv_g, k, peer)
        for k, peer in enumerate(grp_peers, start=1)
    ]
    for copy in copies:
        copy.wait()
    total = landed_g[lax.rem(here_grp, n_grp)]
    for j in range(1, n_grp):
        total = total + landed_g[lax.rem(here_grp + n_grp - j, n_grp)]
    o_ref[...] = total
    for copy in face_copies:
        copy.wait()
    landed_xy[0] = xy_ref[...]
    xy_out[...] = landed_xy[...]
    z_out[...] = landed_z[...]


def exchange_kernel(
    x_ref, xy_ref, z_ref, o_ref, xy_out, z_out,
    landed_b, landed_g, landed_xy, landed_z,
    send_b, recv_b, send_g, recv_g, send_xy, recv_xy, send_z, recv_z,
):
    here_brick = lax.axis_index("brick")
    here_grp = lax.axis_index("grp")
    n_brick = landed_b.shape[0]
    n_grp = landed_g.shape[0]
    brick_peers = [(lax.rem(here_brick + k, n_brick), here_grp) for k in range(1, n_brick)]
    grp_peers = [(here_brick, lax.rem(here_grp + k, n_grp)) for k in range(1, n_grp)]
    barrier = pltpu.get_barrier_semaphore()
    for peer in brick_peers + grp_peers:
        pl.semaphore_signal(barrier, inc=1, device_id=peer, device_id_type=MESH_IDS)
    pl.semaphore_wait(barrier, len(brick_peers) + len(grp_peers))

    share(
        x_ref, xy_ref, z_ref, o_ref, xy_out, z_out, landed_b, landed_g, landed_xy, landed_z,
        send_b, recv_b, send_g, recv_g, send_xy, recv_xy, send_z, recv_z, brick_peers, grp_peers,
    )


def exchange(tile, xy, z, kernel_id):
    n_brick = lax.axis_size("brick")
    n_grp = lax.axis_size("grp")
    vmem = pl.BlockSpec(memory_space=pltpu.VMEM)
    dma = pltpu.SemaphoreType.DMA
    return pl.pallas_call(
        exchange_kernel,
        out_shape=(
            jax.ShapeDtypeStruct(tile.shape, jnp.float32),
            jax.ShapeDtypeStruct((n_brick,) + xy.shape, jnp.float32),
            jax.ShapeDtypeStruct((2,) + z.shape, jnp.float32),
        ),
        in_specs=[vmem] * 3,
        out_specs=(vmem, vmem, vmem),
        scratch_shapes=[
            pltpu.VMEM((n_brick,) + tile.shape, jnp.float32),
            pltpu.VMEM((n_grp,) + tile.shape, jnp.float32),
            pltpu.VMEM((n_brick,) + xy.shape, jnp.float32),
            pltpu.VMEM((2,) + z.shape, jnp.float32),
            dma((n_brick,)),
            dma((n_brick,)),
            dma((n_grp,)),
            dma((n_grp,)),
            dma((n_brick,)),
            dma((n_brick,)),
            dma((2,)),
            dma((2,)),
        ],
        compiler_params=pltpu.CompilerParams(collective_id=kernel_id, has_side_effects=True),
    )(tile, xy, z)


def stencil_body(
    coef_ref, f_ref, bonds_ref, masks_ref, diag_ref, rows_ref, faces_ref, o_ref, xy_ref, z_ref, smooth
):
    slots, width, lanes = f_ref.shape
    row = lax.broadcasted_iota(jnp.int32, (width, lanes), 0)
    lane = lax.broadcasted_iota(jnp.int32, (width, lanes), 1)
    pick = lax.broadcasted_iota(jnp.int32, (BS, lanes), 0)
    spot = lax.broadcasted_iota(jnp.int32, (BS, lanes), 1)
    spread_z = (spot // BS == pick).astype(jnp.float32)
    spread_y = (spot % BS == pick).astype(jnp.float32)

    def spread(face, table):
        high = face.astype(jnp.bfloat16)
        rest = face - high.astype(jnp.float32)
        middle = rest.astype(jnp.bfloat16)
        low = (rest - middle.astype(jnp.float32)).astype(jnp.bfloat16)
        table = table.astype(jnp.bfloat16)
        parts = [
            jnp.dot(part, table, preferred_element_type=jnp.float32) for part in (high, middle, low)
        ]
        return (parts[0] + parts[1]) + parts[2]

    borders = [
        row == width - 1,
        row == 0,
        lane >= lanes - BS,
        lane < BS,
        lane % BS == BS - 1,
        lane % BS == 0,
    ]
    source_lane = lax.broadcasted_iota(jnp.int32, (lanes, BS), 0)
    place = lax.broadcasted_iota(jnp.int32, (lanes, BS), 1)
    layers = [
        (source_lane == offset + step * place).astype(jnp.float32)
        for offset, step in ((0, 1), (lanes - BS, 1), (0, BS), (BS - 1, BS))
    ]
    flat_mask = spot // BS == pick

    def flatten(layer):
        spread_out = jnp.where(flat_mask, spread(layer, spread_y), 0.0)
        return jnp.sum(spread_out, axis=0, keepdims=True)

    dot = jnp.float32(0.0)
    sums = []
    for s in range(slots):
        ds = diag_ref[s]
        if smooth:
            rs = f_ref[s]
            fs = OMEGA * rs / ds
        else:
            fs = f_ref[s]
        xp = jnp.where(row == width - 1, rows_ref[0, s], pltpu.roll(fs, width - 1, 0))
        xm = jnp.where(row == 0, rows_ref[1, s], pltpu.roll(fs, 1, 0))
        yp = jnp.where(lane >= lanes - BS, spread(faces_ref[0, s], spread_y), pltpu.roll(fs, lanes - BS, 1))
        ym = jnp.where(lane < BS, spread(faces_ref[1, s], spread_y), pltpu.roll(fs, BS, 1))
        zp = jnp.where(lane % BS == BS - 1, spread(faces_ref[2, s], spread_z), pltpu.roll(fs, lanes - 1, 1))
        zm = jnp.where(lane % BS == 0, spread(faces_ref[3, s], spread_z), pltpu.roll(fs, 1, 1))
        total = ds * fs
        for d, beyond in enumerate([xp, xm, yp, ym, zp, zm]):
            base = 2 * (d * slots + s)
            active = jnp.where(borders[d], masks_ref[base + 1], masks_ref[base])
            total = total - bonds_ref[d, s] * active * beyond
        if smooth:
            total = fs + OMEGA * (rs - total) / ds
            total = total + coef_ref[s]
            dot = dot + jnp.sum(rs * total)
        else:
            dot = dot + jnp.sum(fs * total)
            sums.append(jnp.sum(total))
        o_ref[s] = total
        xy_ref[pl.ds(s, 1), :] = total[0:1, :]
        xy_ref[pl.ds(slots + s, 1), :] = total[width - 1 : width, :]
        if s == 0:
            xy_ref[pl.ds(2 * slots, 1), :] = flatten(spread(total, layers[0]))
        if s == slots - 1:
            xy_ref[pl.ds(2 * slots + 1, 1), :] = flatten(spread(total, layers[1]))
        z_ref[pl.ds(s, 1), :] = flatten(spread(total, layers[2]))
        z_ref[pl.ds(slots + s, 1), :] = flatten(spread(total, layers[3]))
    return dot, sums


def round_kernel(
    coef_ref, f_ref, bonds_ref, masks_ref, diag_ref, rows_ref, faces_ref,
    o_ref, total_ref, xy_out, z_out,
    xy_buf, z_buf, tile_buf, landed_b, landed_g, landed_xy, landed_z,
    send_b, recv_b, send_g, recv_g, send_xy, recv_xy, send_z, recv_z, *, smooth
):
    here_brick = lax.axis_index("brick")
    here_grp = lax.axis_index("grp")
    n_brick = landed_b.shape[0]
    n_grp = landed_g.shape[0]
    brick_peers = [(lax.rem(here_brick + k, n_brick), here_grp) for k in range(1, n_brick)]
    grp_peers = [(here_brick, lax.rem(here_grp + k, n_grp)) for k in range(1, n_grp)]
    barrier = pltpu.get_barrier_semaphore()
    for peer in brick_peers + grp_peers:
        pl.semaphore_signal(barrier, inc=1, device_id=peer, device_id_type=MESH_IDS)
    dot, sums = stencil_body(
        coef_ref, f_ref, bonds_ref, masks_ref, diag_ref, rows_ref, faces_ref, o_ref, xy_buf, z_buf,
        smooth,
    )
    tile_rows, tile_lanes = tile_buf.shape
    flat = lax.broadcasted_iota(jnp.int32, (tile_rows, tile_lanes), 0) * tile_lanes
    flat = flat + lax.broadcasted_iota(jnp.int32, (tile_rows, tile_lanes), 1)
    tile = jnp.where(flat == 0, dot, 0.0)
    slots = f_ref.shape[0]
    for s, value in enumerate(sums):
        position = 1 + (here_brick * n_grp + here_grp) * slots + s
        tile = jnp.where(flat == position, value, tile)
    tile_buf[...] = tile
    pl.semaphore_wait(barrier, len(brick_peers) + len(grp_peers))
    share(
        tile_buf, xy_buf, z_buf, total_ref, xy_out, z_out, landed_b, landed_g, landed_xy, landed_z,
        send_b, recv_b, send_g, recv_g, send_xy, recv_xy, send_z, recv_z, brick_peers, grp_peers,
    )


def one_round(field, bonds, masks, diag, rows, faces, coef, smooth):
    slots, _, lanes = field.shape
    n_brick = lax.axis_size("brick")
    n_grp = lax.axis_size("grp")
    tile = (8, 128)
    xy = (2 * slots + 2, lanes)
    z = (2 * slots, lanes)
    vmem = pl.BlockSpec(memory_space=pltpu.VMEM)
    smem = pl.BlockSpec(memory_space=pltpu.SMEM)
    dma = pltpu.SemaphoreType.DMA
    return pl.pallas_call(
        functools.partial(round_kernel, smooth=smooth),
        out_shape=(
            jax.ShapeDtypeStruct(field.shape, jnp.float32),
            jax.ShapeDtypeStruct(tile, jnp.float32),
            jax.ShapeDtypeStruct((n_brick,) + xy, jnp.float32),
            jax.ShapeDtypeStruct((2,) + z, jnp.float32),
        ),
        in_specs=[smem, vmem, vmem, smem, vmem, vmem, vmem],
        out_specs=(vmem, vmem, vmem, vmem),
        scratch_shapes=[
            pltpu.VMEM(xy, jnp.float32),
            pltpu.VMEM(z, jnp.float32),
            pltpu.VMEM(tile, jnp.float32),
            pltpu.VMEM((n_brick,) + tile, jnp.float32),
            pltpu.VMEM((n_grp,) + tile, jnp.float32),
            pltpu.VMEM((n_brick,) + xy, jnp.float32),
            pltpu.VMEM((2,) + z, jnp.float32),
            dma((n_brick,)),
            dma((n_brick,)),
            dma((n_grp,)),
            dma((n_grp,)),
            dma((n_brick,)),
            dma((n_brick,)),
            dma((2,)),
            dma((2,)),
        ],
        compiler_params=pltpu.CompilerParams(
            collective_id=3 if smooth else 1, has_side_effects=True
        ),
    )(coef, field, bonds, masks, diag, rows, faces)


def assemble(coarse_diag, couplings, strides):
    extent = coarse_diag.shape[0]
    matrix = jnp.diag(coarse_diag)
    for coupling, stride in zip(couplings, strides):
        banded = coupling[: extent - stride]
        matrix = matrix - jnp.diag(banded, stride) - jnp.diag(banded, -stride)
    return matrix


def on_device(source, uptake, conductance, occupancy, assignment):
    face_size = BS * BS
    slot_count = PATCH_X * PATCH_Y
    slab_index = lax.axis_index("grp")
    brick_index = lax.axis_index("brick")
    brick_count = lax.axis_size("brick")
    across = brick_count // 2
    peer_ids = jnp.arange(brick_count, dtype=jnp.int32)
    patch_index = assignment[brick_index]
    patch_row = patch_index // across
    patch_column = patch_index % across

    def owner_of(row_shift, column_shift):
        row_target = patch_row + row_shift
        column_target = patch_column + column_shift
        inside = (
            (row_target >= 0) & (row_target < 2) & (column_target >= 0) & (column_target < across)
        )
        holder = jnp.sum(jnp.where(assignment == row_target * across + column_target, peer_ids, 0))
        return jnp.where(inside, holder, -1)

    wanted = jnp.stack([owner_of(1, 0), owner_of(-1, 0), owner_of(0, 1), owner_of(0, -1)])
    padded = jnp.pad(occupancy, 1)
    window = lax.dynamic_slice(
        padded,
        (slab_index, patch_row * PATCH_X, patch_column * PATCH_Y),
        (3, PATCH_X + 2, PATCH_Y + 2),
    ).astype(jnp.float32)
    centre = window[1, 1:-1, 1:-1].reshape(slot_count)
    toward = [
        window[1, 2:, 1:-1],
        window[1, :-2, 1:-1],
        window[1, 1:-1, 2:],
        window[1, 1:-1, :-2],
        window[2, 1:-1, 1:-1],
        window[0, 1:-1, 1:-1],
    ]
    first_axis = lax.broadcasted_iota(jnp.int32, (1, BS, face_size), 1)
    flat_axis = lax.broadcasted_iota(jnp.int32, (1, BS, face_size), 2)
    second_axis = flat_axis // BS
    third_axis = flat_axis % BS
    cube_third = lax.broadcasted_iota(jnp.int32, (1, BS, BS, BS), 3)
    borders = [
        first_axis == BS - 1,
        first_axis == 0,
        second_axis == BS - 1,
        second_axis == 0,
        third_axis == BS - 1,
        third_axis == 0,
    ]
    bonds = conductance[0, 0]
    live_here = centre[:, None, None]
    effective = []
    for direction in range(6):
        neighbour_live = toward[direction].reshape(slot_count)[:, None, None]
        active = jnp.where(borders[direction], live_here * neighbour_live, live_here)
        effective.append(bonds[direction] * active)
    absorb = uptake[0, 0]
    diagonal = absorb
    for direction in range(6):
        diagonal = diagonal + effective[direction]

    masks = jnp.stack(
        [
            jnp.stack([centre, centre * toward[direction].reshape(slot_count)], axis=1)
            for direction in range(6)
        ]
    ).reshape(-1)

    lane_ids = jnp.arange(face_size, dtype=jnp.int32)[:, None]
    layer_ids = BS * jnp.arange(BS, dtype=jnp.int32)[None, :]
    picker = jnp.concatenate([lane_ids == layer_ids, lane_ids == layer_ids + BS - 1], axis=1)
    picker = picker.astype(jnp.float32)

    def side_faces(field):
        picked = jnp.dot(
            field.reshape(slot_count * BS, face_size), picker, precision=lax.Precision.HIGHEST
        )
        z = picked.reshape(slot_count, BS, 2, BS).transpose(2, 0, 1, 3)
        xy = jnp.concatenate(
            [
                field[:, 0, :],
                field[:, BS - 1, :],
                field[0, :, :BS].reshape(1, face_size),
                field[slot_count - 1, :, face_size - BS :].reshape(1, face_size),
            ]
        )
        return xy, z.reshape(2 * slot_count, face_size)

    def pick(landed, holder, fill):
        offset = lax.rem(brick_index - holder + brick_count, brick_count)
        got = lax.dynamic_index_in_dim(landed, offset, keepdims=False)
        return jnp.where(holder >= 0, got, fill)

    def halo(field, xy_land, z_land, fill):
        xplus = pick(xy_land, wanted[0], fill)
        xminus = pick(xy_land, wanted[1], fill)
        yplus = pick(xy_land, wanted[2], fill)
        yminus = pick(xy_land, wanted[3], fill)
        rows = jnp.stack([xplus[:slot_count], xminus[slot_count : 2 * slot_count]])[:, :, None, :]
        beyond_yplus = jnp.stack([field[1, :, :BS], yplus[2 * slot_count].reshape(BS, BS)])
        beyond_yminus = jnp.stack(
            [yminus[2 * slot_count + 1].reshape(BS, BS), field[0, :, face_size - BS :]]
        )
        above = jnp.where(slab_index < grp_count - 1, z_land[1, :slot_count], fill)
        below = jnp.where(slab_index > 0, z_land[0, slot_count:], fill)
        faces = jnp.stack(
            [
                beyond_yplus,
                beyond_yminus,
                above.reshape(slot_count, BS, BS),
                below.reshape(slot_count, BS, BS),
            ]
        )
        return rows, faces

    slot_ids = jnp.arange(slot_count)
    brick_first = slot_ids // PATCH_Y
    brick_second = slot_ids % PATCH_Y
    inside = [
        (brick_first < PATCH_X - 1).astype(jnp.float32),
        (brick_first > 0).astype(jnp.float32),
        (brick_second < PATCH_Y - 1).astype(jnp.float32),
        (brick_second > 0).astype(jnp.float32),
    ]
    face_sums = [
        jnp.sum(effective[0][:, BS - 1, :], axis=1),
        jnp.sum(effective[1][:, 0, :], axis=1),
        jnp.sum(effective[2][:, :, face_size - BS :], axis=(1, 2)),
        jnp.sum(effective[3][:, :, :BS], axis=(1, 2)),
        jnp.sum(jnp.where(borders[4], effective[4], 0.0), axis=(1, 2)),
        jnp.sum(jnp.where(borders[5], effective[5], 0.0), axis=(1, 2)),
    ]
    coarse_diag = jnp.sum(absorb, axis=(1, 2))
    for direction in range(4):
        coarse_diag = coarse_diag + face_sums[direction] * inside[direction]
    coarse_diag = coarse_diag + face_sums[4] + face_sums[5]
    grp_count = lax.axis_size("grp")
    grp_ids = jnp.arange(grp_count, dtype=jnp.int32)

    def slab_slot(values):
        here = (grp_ids == slab_index).astype(jnp.float32)
        return here[:, None, None] * values[None]

    forcing = source[0, 0] * live_here

    def as_tile(values):
        rows = -(-values.shape[0] // 128)
        rows = -(-rows // 8) * 8
        return jnp.pad(values, (0, rows * 128 - values.shape[0])).reshape(rows, 128)

    record = jnp.stack(
        [
            coarse_diag,
            face_sums[0] * inside[0],
            face_sums[2] * inside[2],
            face_sums[4],
            jnp.sum(forcing, axis=(1, 2)),
        ]
    )
    brick_here = (peer_ids == brick_index).astype(jnp.float32)
    spread = (brick_here[:, None, None, None] * slab_slot(record)[None]).reshape(-1)
    forcing_xy, forcing_z = side_faces(forcing)
    diagonal_xy, diagonal_z = side_faces(diagonal)
    summed, xy_land, z_land = exchange(
        as_tile(spread),
        jnp.concatenate([forcing_xy, diagonal_xy]),
        jnp.concatenate([forcing_z, diagonal_z]),
        2,
    )
    summed = summed.reshape(-1)[: spread.shape[0]]
    xy_rows = forcing_xy.shape[0]
    z_rows = forcing_z.shape[0]
    residual_halo = halo(forcing, xy_land[:, :xy_rows], z_land[:, :z_rows], 0.0)
    diagonal_halo = halo(diagonal, xy_land[:, xy_rows:], z_land[:, z_rows:], 1.0)
    gathered = lax.dynamic_index_in_dim(
        summed.reshape(brick_count, grp_count, 5, slot_count), brick_index, keepdims=False
    )
    columns = jnp.transpose(gathered, (1, 0, 2)).reshape(5, -1)
    matrix = assemble(columns[0], (columns[1], columns[2], columns[3]), (PATCH_Y, 1, slot_count))
    factor = jnp.linalg.cholesky(matrix)

    def coarse_solve(terms):
        middle = lax.linalg.triangular_solve(factor, terms[:, None], left_side=True, lower=True)
        result = lax.linalg.triangular_solve(
            factor, middle, left_side=True, lower=True, transpose_a=True
        )
        return lax.dynamic_slice_in_dim(result[:, 0], slab_index * slot_count, slot_count)

    def round_trip(field, field_halo, coef, smooth):
        out, total, xy_land, z_land = one_round(
            field, bonds, masks, diagonal, *field_halo, coef, smooth
        )
        total = total.reshape(-1)
        out_halo = halo(out, xy_land, z_land, 0.0)
        if smooth:
            return out, total[0], None, out_halo
        count = brick_count * grp_count * slot_count
        mine = lax.dynamic_index_in_dim(
            total[1 : 1 + count].reshape(brick_count, -1), brick_index, keepdims=False
        )
        return out, total[0], mine, out_halo

    def precondition(residual_field, field_halo, terms):
        smoothed_halo = [OMEGA * part / scale for part, scale in zip(field_halo, diagonal_halo)]
        return round_trip(residual_field, smoothed_halo, coarse_solve(terms), True)

    no_coarse = jnp.zeros((slot_count,), jnp.float32)
    terms = columns[4]
    solution_field = jnp.zeros_like(forcing)
    residual = forcing
    search, energy, _, search_halo = precondition(residual, residual_halo, terms)
    for iteration in range(ITERS):
        mapped, curvature, mapped_terms, mapped_halo = round_trip(
            search, search_halo, no_coarse, False
        )
        step_size = energy / curvature
        solution_field = solution_field + step_size * search
        residual = residual - step_size * mapped
        if iteration + 1 < ITERS:
            residual_halo = [
                part - step_size * change for part, change in zip(residual_halo, mapped_halo)
            ]
            terms = terms - step_size * mapped_terms
            smoothed, renewed, _, smoothed_halo = precondition(residual, residual_halo, terms)
            search = smoothed + renewed / energy * search
            search_halo = [
                part + renewed / energy * old for part, old in zip(smoothed_halo, search_halo)
            ]
            energy = renewed
    return (solution_field[None, None], residual[None, None])


def solution(mesh):
    return jax.shard_map(
        on_device,
        mesh=mesh,
        in_specs=(
            P("grp", "brick", None, None, None),
            P("grp", "brick", None, None, None),
            P("grp", "brick", None, None, None, None),
            P(),
            P(),
        ),
        out_specs=(P("grp", "brick", None, None, None), P("grp", "brick", None, None, None)),
        check_vma=False,
    )
```

```python
import functools

import jax
import jax.numpy as jnp
from jax import lax
from jax.experimental import pallas as pl
from jax.experimental.pallas import tpu as pltpu
from jax.sharding import PartitionSpec as P

MESH_IDS = pl.DeviceIdType.MESH

BS = 32
PATCH_X = 1
PATCH_Y = 2
ITERS = 3


OMEGA = 0.6


def share(
    x_ref, xy_ref, z_ref, o_ref, xy_out, z_out, landed_b, landed_g, landed_xy, landed_z,
    send_b, recv_b, send_g, recv_g, send_xy, recv_xy, send_z, recv_z, brick_peers, grp_peers,
    dot_ref=None,
):
    here_brick = lax.axis_index("brick")
    here_grp = lax.axis_index("grp")
    n_brick = landed_b.shape[0]
    n_grp = landed_g.shape[0]

    def send(src, dst, sends, recvs, index, peer):
        copy = pltpu.make_async_remote_copy(
            src_ref=src,
            dst_ref=dst.at[index],
            send_sem=sends.at[index],
            recv_sem=recvs.at[index],
            device_id=peer,
            device_id_type=MESH_IDS,
        )
        copy.start()
        return copy

    face_copies = [
        send(z_ref, landed_z, send_z, recv_z, 0, grp_peers[0]),
        send(z_ref, landed_z, send_z, recv_z, 1, grp_peers[-1]),
    ]
    face_copies += [
        send(xy_ref, landed_xy, send_xy, recv_xy, k, peer)
        for k, peer in enumerate(brick_peers, start=1)
    ]
    copies = [
        send(x_ref, landed_b, send_b, recv_b, k, peer)
        for k, peer in enumerate(brick_peers, start=1)
    ]
    landed_b[0] = x_ref[...]
    for copy in copies:
        copy.wait()
    total = landed_b[lax.rem(here_brick, n_brick)]
    for j in range(1, n_brick):
        total = total + landed_b[lax.rem(here_brick + n_brick - j, n_brick)]
    o_ref[...] = total
    landed_g[0] = total
    copies = [
        send(o_ref, landed_g, send_g, recv_g, k, peer)
        for k, peer in enumerate(grp_peers, start=1)
    ]
    for copy in copies:
        copy.wait()
    total = landed_g[lax.rem(here_grp, n_grp)]
    for j in range(1, n_grp):
        total = total + landed_g[lax.rem(here_grp + n_grp - j, n_grp)]
    o_ref[...] = total
    for copy in face_copies:
        copy.wait()
    landed_xy[0] = xy_ref[...]
    xy_out[...] = landed_xy[...]
    z_out[...] = landed_z[...]
    if dot_ref is not None:
        tile_rows, tile_lanes = o_ref.shape
        first = lax.broadcasted_iota(jnp.int32, (tile_rows, tile_lanes), 0) * tile_lanes
        first = first + lax.broadcasted_iota(jnp.int32, (tile_rows, tile_lanes), 1)
        dot_ref[0] = jnp.sum(jnp.where(first == 0, total, 0.0))


def exchange_kernel(
    x_ref, xy_ref, z_ref, o_ref, xy_out, z_out,
    landed_b, landed_g, landed_xy, landed_z,
    send_b, recv_b, send_g, recv_g, send_xy, recv_xy, send_z, recv_z,
):
    here_brick = lax.axis_index("brick")
    here_grp = lax.axis_index("grp")
    n_brick = landed_b.shape[0]
    n_grp = landed_g.shape[0]
    brick_peers = [(lax.rem(here_brick + k, n_brick), here_grp) for k in range(1, n_brick)]
    grp_peers = [(here_brick, lax.rem(here_grp + k, n_grp)) for k in range(1, n_grp)]
    barrier = pltpu.get_barrier_semaphore()
    for peer in brick_peers + grp_peers:
        pl.semaphore_signal(barrier, inc=1, device_id=peer, device_id_type=MESH_IDS)
    pl.semaphore_wait(barrier, len(brick_peers) + len(grp_peers))

    share(
        x_ref, xy_ref, z_ref, o_ref, xy_out, z_out, landed_b, landed_g, landed_xy, landed_z,
        send_b, recv_b, send_g, recv_g, send_xy, recv_xy, send_z, recv_z, brick_peers, grp_peers,
    )


def exchange(tile, xy, z, kernel_id):
    n_brick = lax.axis_size("brick")
    n_grp = lax.axis_size("grp")
    vmem = pl.BlockSpec(memory_space=pltpu.VMEM)
    dma = pltpu.SemaphoreType.DMA
    return pl.pallas_call(
        exchange_kernel,
        out_shape=(
            jax.ShapeDtypeStruct(tile.shape, jnp.float32),
            jax.ShapeDtypeStruct((n_brick,) + xy.shape, jnp.float32),
            jax.ShapeDtypeStruct((2,) + z.shape, jnp.float32),
        ),
        in_specs=[vmem] * 3,
        out_specs=(vmem, vmem, vmem),
        scratch_shapes=[
            pltpu.VMEM((n_brick,) + tile.shape, jnp.float32),
            pltpu.VMEM((n_grp,) + tile.shape, jnp.float32),
            pltpu.VMEM((n_brick,) + xy.shape, jnp.float32),
            pltpu.VMEM((2,) + z.shape, jnp.float32),
            dma((n_brick,)),
            dma((n_brick,)),
            dma((n_grp,)),
            dma((n_grp,)),
            dma((n_brick,)),
            dma((n_brick,)),
            dma((2,)),
            dma((2,)),
        ],
        compiler_params=pltpu.CompilerParams(collective_id=kernel_id, has_side_effects=True),
    )(tile, xy, z)


def stencil_body(
    coef_ref, f_ref, bonds_ref, masks_ref, diag_ref, rows_ref, faces_ref, o_ref, xy_ref, z_ref, smooth
):
    slots, width, lanes = f_ref.shape
    row = lax.broadcasted_iota(jnp.int32, (width, lanes), 0)
    lane = lax.broadcasted_iota(jnp.int32, (width, lanes), 1)
    pick = lax.broadcasted_iota(jnp.int32, (BS, lanes), 0)
    spot = lax.broadcasted_iota(jnp.int32, (BS, lanes), 1)
    spread_z = (spot // BS == pick).astype(jnp.float32)
    spread_y = (spot % BS == pick).astype(jnp.float32)

    def spread(face, table):
        high = face.astype(jnp.bfloat16)
        rest = face - high.astype(jnp.float32)
        middle = rest.astype(jnp.bfloat16)
        low = (rest - middle.astype(jnp.float32)).astype(jnp.bfloat16)
        table = table.astype(jnp.bfloat16)
        parts = [
            jnp.dot(part, table, preferred_element_type=jnp.float32) for part in (high, middle, low)
        ]
        return (parts[0] + parts[1]) + parts[2]

    borders = [
        row == width - 1,
        row == 0,
        lane >= lanes - BS,
        lane < BS,
        lane % BS == BS - 1,
        lane % BS == 0,
    ]
    source_lane = lax.broadcasted_iota(jnp.int32, (lanes, BS), 0)
    place = lax.broadcasted_iota(jnp.int32, (lanes, BS), 1)
    layers = [
        (source_lane == offset + step * place).astype(jnp.float32)
        for offset, step in ((0, 1), (lanes - BS, 1), (0, BS), (BS - 1, BS))
    ]
    flat_mask = spot // BS == pick

    def flatten(layer):
        spread_out = jnp.where(flat_mask, spread(layer, spread_y), 0.0)
        return jnp.sum(spread_out, axis=0, keepdims=True)

    dot = jnp.float32(0.0)
    sums = []
    for s in range(slots):
        ds = diag_ref[s]
        if smooth:
            rs = f_ref[s]
            fs = OMEGA * rs / ds
        else:
            fs = f_ref[s]
        xp = jnp.where(row == width - 1, rows_ref[0, s], pltpu.roll(fs, width - 1, 0))
        xm = jnp.where(row == 0, rows_ref[1, s], pltpu.roll(fs, 1, 0))
        yp = jnp.where(lane >= lanes - BS, spread(faces_ref[0, s], spread_y), pltpu.roll(fs, lanes - BS, 1))
        ym = jnp.where(lane < BS, spread(faces_ref[1, s], spread_y), pltpu.roll(fs, BS, 1))
        zp = jnp.where(lane % BS == BS - 1, spread(faces_ref[2, s], spread_z), pltpu.roll(fs, lanes - 1, 1))
        zm = jnp.where(lane % BS == 0, spread(faces_ref[3, s], spread_z), pltpu.roll(fs, 1, 1))
        total = ds * fs
        for d, beyond in enumerate([xp, xm, yp, ym, zp, zm]):
            base = 2 * (d * slots + s)
            active = jnp.where(borders[d], masks_ref[base + 1], masks_ref[base])
            total = total - bonds_ref[d, s] * active * beyond
        if smooth:
            total = fs + OMEGA * (rs - total) / ds
            total = total + coef_ref[s]
            dot = dot + jnp.sum(rs * total)
        else:
            dot = dot + jnp.sum(fs * total)
            sums.append(jnp.sum(total))
        o_ref[s] = total
        xy_ref[pl.ds(s, 1), :] = total[0:1, :]
        xy_ref[pl.ds(slots + s, 1), :] = total[width - 1 : width, :]
        if s == 0:
            xy_ref[pl.ds(2 * slots, 1), :] = flatten(spread(total, layers[0]))
        if s == slots - 1:
            xy_ref[pl.ds(2 * slots + 1, 1), :] = flatten(spread(total, layers[1]))
        z_ref[pl.ds(s, 1), :] = flatten(spread(total, layers[2]))
        z_ref[pl.ds(slots + s, 1), :] = flatten(spread(total, layers[3]))
    return dot, sums


def round_kernel(
    coef_ref, f_ref, bonds_ref, masks_ref, diag_ref, rows_ref, faces_ref,
    o_ref, total_ref, xy_out, z_out, dot_ref,
    xy_buf, z_buf, tile_buf, landed_b, landed_g, landed_xy, landed_z,
    send_b, recv_b, send_g, recv_g, send_xy, recv_xy, send_z, recv_z, *, smooth
):
    here_brick = lax.axis_index("brick")
    here_grp = lax.axis_index("grp")
    n_brick = landed_b.shape[0]
    n_grp = landed_g.shape[0]
    brick_peers = [(lax.rem(here_brick + k, n_brick), here_grp) for k in range(1, n_brick)]
    grp_peers = [(here_brick, lax.rem(here_grp + k, n_grp)) for k in range(1, n_grp)]
    barrier = pltpu.get_barrier_semaphore()
    for peer in brick_peers + grp_peers:
        pl.semaphore_signal(barrier, inc=1, device_id=peer, device_id_type=MESH_IDS)
    dot, sums = stencil_body(
        coef_ref, f_ref, bonds_ref, masks_ref, diag_ref, rows_ref, faces_ref, o_ref, xy_buf, z_buf,
        smooth,
    )
    tile_rows, tile_lanes = tile_buf.shape
    flat = lax.broadcasted_iota(jnp.int32, (tile_rows, tile_lanes), 0) * tile_lanes
    flat = flat + lax.broadcasted_iota(jnp.int32, (tile_rows, tile_lanes), 1)
    tile = jnp.where(flat == 0, dot, 0.0)
    slots = f_ref.shape[0]
    for s, value in enumerate(sums):
        position = 1 + (here_brick * n_grp + here_grp) * slots + s
        tile = jnp.where(flat == position, value, tile)
    tile_buf[...] = tile
    pl.semaphore_wait(barrier, len(brick_peers) + len(grp_peers))
    share(
        tile_buf, xy_buf, z_buf, total_ref, xy_out, z_out, landed_b, landed_g, landed_xy, landed_z,
        send_b, recv_b, send_g, recv_g, send_xy, recv_xy, send_z, recv_z, brick_peers, grp_peers,
        dot_ref=dot_ref,
    )


def one_round(field, bonds, masks, diag, rows, faces, coef, smooth):
    slots, _, lanes = field.shape
    n_brick = lax.axis_size("brick")
    n_grp = lax.axis_size("grp")
    tile = (8, 128)
    xy = (2 * slots + 2, lanes)
    z = (2 * slots, lanes)
    vmem = pl.BlockSpec(memory_space=pltpu.VMEM)
    smem = pl.BlockSpec(memory_space=pltpu.SMEM)
    dma = pltpu.SemaphoreType.DMA
    return pl.pallas_call(
        functools.partial(round_kernel, smooth=smooth),
        out_shape=(
            jax.ShapeDtypeStruct(field.shape, jnp.float32),
            jax.ShapeDtypeStruct(tile, jnp.float32),
            jax.ShapeDtypeStruct((n_brick,) + xy, jnp.float32),
            jax.ShapeDtypeStruct((2,) + z, jnp.float32),
            jax.ShapeDtypeStruct((1,), jnp.float32),
        ),
        in_specs=[smem, vmem, vmem, smem, vmem, vmem, vmem],
        out_specs=(vmem, vmem, vmem, vmem, smem),
        scratch_shapes=[
            pltpu.VMEM(xy, jnp.float32),
            pltpu.VMEM(z, jnp.float32),
            pltpu.VMEM(tile, jnp.float32),
            pltpu.VMEM((n_brick,) + tile, jnp.float32),
            pltpu.VMEM((n_grp,) + tile, jnp.float32),
            pltpu.VMEM((n_brick,) + xy, jnp.float32),
            pltpu.VMEM((2,) + z, jnp.float32),
            dma((n_brick,)),
            dma((n_brick,)),
            dma((n_grp,)),
            dma((n_grp,)),
            dma((n_brick,)),
            dma((n_brick,)),
            dma((2,)),
            dma((2,)),
        ],
        compiler_params=pltpu.CompilerParams(
            collective_id=3 if smooth else 1, has_side_effects=True
        ),
    )(coef, field, bonds, masks, diag, rows, faces)


def assemble(coarse_diag, couplings, strides):
    extent = coarse_diag.shape[0]
    matrix = jnp.diag(coarse_diag)
    for coupling, stride in zip(couplings, strides):
        banded = coupling[: extent - stride]
        matrix = matrix - jnp.diag(banded, stride) - jnp.diag(banded, -stride)
    return matrix


def on_device(source, uptake, conductance, occupancy, assignment):
    face_size = BS * BS
    slot_count = PATCH_X * PATCH_Y
    slab_index = lax.axis_index("grp")
    brick_index = lax.axis_index("brick")
    brick_count = lax.axis_size("brick")
    across = brick_count // 2
    peer_ids = jnp.arange(brick_count, dtype=jnp.int32)
    patch_index = assignment[brick_index]
    patch_row = patch_index // across
    patch_column = patch_index % across

    def owner_of(row_shift, column_shift):
        row_target = patch_row + row_shift
        column_target = patch_column + column_shift
        inside = (
            (row_target >= 0) & (row_target < 2) & (column_target >= 0) & (column_target < across)
        )
        holder = jnp.sum(jnp.where(assignment == row_target * across + column_target, peer_ids, 0))
        return jnp.where(inside, holder, -1)

    wanted = jnp.stack([owner_of(1, 0), owner_of(-1, 0), owner_of(0, 1), owner_of(0, -1)])
    padded = jnp.pad(occupancy, 1)
    window = lax.dynamic_slice(
        padded,
        (slab_index, patch_row * PATCH_X, patch_column * PATCH_Y),
        (3, PATCH_X + 2, PATCH_Y + 2),
    ).astype(jnp.float32)
    centre = window[1, 1:-1, 1:-1].reshape(slot_count)
    toward = [
        window[1, 2:, 1:-1],
        window[1, :-2, 1:-1],
        window[1, 1:-1, 2:],
        window[1, 1:-1, :-2],
        window[2, 1:-1, 1:-1],
        window[0, 1:-1, 1:-1],
    ]
    first_axis = lax.broadcasted_iota(jnp.int32, (1, BS, face_size), 1)
    flat_axis = lax.broadcasted_iota(jnp.int32, (1, BS, face_size), 2)
    second_axis = flat_axis // BS
    third_axis = flat_axis % BS
    cube_third = lax.broadcasted_iota(jnp.int32, (1, BS, BS, BS), 3)
    borders = [
        first_axis == BS - 1,
        first_axis == 0,
        second_axis == BS - 1,
        second_axis == 0,
        third_axis == BS - 1,
        third_axis == 0,
    ]
    bonds = conductance[0, 0]
    live_here = centre[:, None, None]
    effective = []
    for direction in range(6):
        neighbour_live = toward[direction].reshape(slot_count)[:, None, None]
        active = jnp.where(borders[direction], live_here * neighbour_live, live_here)
        effective.append(bonds[direction] * active)
    absorb = uptake[0, 0]
    diagonal = absorb
    for direction in range(6):
        diagonal = diagonal + effective[direction]

    masks = jnp.stack(
        [
            jnp.stack([centre, centre * toward[direction].reshape(slot_count)], axis=1)
            for direction in range(6)
        ]
    ).reshape(-1)

    lane_ids = jnp.arange(face_size, dtype=jnp.int32)[:, None]
    layer_ids = BS * jnp.arange(BS, dtype=jnp.int32)[None, :]
    picker = jnp.concatenate([lane_ids == layer_ids, lane_ids == layer_ids + BS - 1], axis=1)
    picker = picker.astype(jnp.float32)

    def side_faces(field):
        picked = jnp.dot(
            field.reshape(slot_count * BS, face_size), picker, precision=lax.Precision.HIGHEST
        )
        z = picked.reshape(slot_count, BS, 2, BS).transpose(2, 0, 1, 3)
        xy = jnp.concatenate(
            [
                field[:, 0, :],
                field[:, BS - 1, :],
                field[0, :, :BS].reshape(1, face_size),
                field[slot_count - 1, :, face_size - BS :].reshape(1, face_size),
            ]
        )
        return xy, z.reshape(2 * slot_count, face_size)

    def pick(landed, holder, fill):
        offset = lax.rem(brick_index - holder + brick_count, brick_count)
        got = lax.dynamic_index_in_dim(landed, offset, keepdims=False)
        return jnp.where(holder >= 0, got, fill)

    def halo(field, xy_land, z_land, fill):
        xplus = pick(xy_land, wanted[0], fill)
        xminus = pick(xy_land, wanted[1], fill)
        yplus = pick(xy_land, wanted[2], fill)
        yminus = pick(xy_land, wanted[3], fill)
        rows = jnp.stack([xplus[:slot_count], xminus[slot_count : 2 * slot_count]])[:, :, None, :]
        beyond_yplus = jnp.stack([field[1, :, :BS], yplus[2 * slot_count].reshape(BS, BS)])
        beyond_yminus = jnp.stack(
            [yminus[2 * slot_count + 1].reshape(BS, BS), field[0, :, face_size - BS :]]
        )
        above = jnp.where(slab_index < grp_count - 1, z_land[1, :slot_count], fill)
        below = jnp.where(slab_index > 0, z_land[0, slot_count:], fill)
        faces = jnp.stack(
            [
                beyond_yplus,
                beyond_yminus,
                above.reshape(slot_count, BS, BS),
                below.reshape(slot_count, BS, BS),
            ]
        )
        return rows, faces

    slot_ids = jnp.arange(slot_count)
    brick_first = slot_ids // PATCH_Y
    brick_second = slot_ids % PATCH_Y
    inside = [
        (brick_first < PATCH_X - 1).astype(jnp.float32),
        (brick_first > 0).astype(jnp.float32),
        (brick_second < PATCH_Y - 1).astype(jnp.float32),
        (brick_second > 0).astype(jnp.float32),
    ]
    face_sums = [
        jnp.sum(effective[0][:, BS - 1, :], axis=1),
        jnp.sum(effective[1][:, 0, :], axis=1),
        jnp.sum(effective[2][:, :, face_size - BS :], axis=(1, 2)),
        jnp.sum(effective[3][:, :, :BS], axis=(1, 2)),
        jnp.sum(jnp.where(borders[4], effective[4], 0.0), axis=(1, 2)),
        jnp.sum(jnp.where(borders[5], effective[5], 0.0), axis=(1, 2)),
    ]
    coarse_diag = jnp.sum(absorb, axis=(1, 2))
    for direction in range(4):
        coarse_diag = coarse_diag + face_sums[direction] * inside[direction]
    coarse_diag = coarse_diag + face_sums[4] + face_sums[5]
    grp_count = lax.axis_size("grp")
    grp_ids = jnp.arange(grp_count, dtype=jnp.int32)

    def slab_slot(values):
        here = (grp_ids == slab_index).astype(jnp.float32)
        return here[:, None, None] * values[None]

    forcing = source[0, 0] * live_here

    def as_tile(values):
        rows = -(-values.shape[0] // 128)
        rows = -(-rows // 8) * 8
        return jnp.pad(values, (0, rows * 128 - values.shape[0])).reshape(rows, 128)

    record = jnp.stack(
        [
            coarse_diag,
            face_sums[0] * inside[0],
            face_sums[2] * inside[2],
            face_sums[4],
            jnp.sum(forcing, axis=(1, 2)),
        ]
    )
    brick_here = (peer_ids == brick_index).astype(jnp.float32)
    spread = (brick_here[:, None, None, None] * slab_slot(record)[None]).reshape(-1)
    forcing_xy, forcing_z = side_faces(forcing)
    diagonal_xy, diagonal_z = side_faces(diagonal)
    summed, xy_land, z_land = exchange(
        as_tile(spread),
        jnp.concatenate([forcing_xy, diagonal_xy]),
        jnp.concatenate([forcing_z, diagonal_z]),
        2,
    )
    summed = summed.reshape(-1)[: spread.shape[0]]
    xy_rows = forcing_xy.shape[0]
    z_rows = forcing_z.shape[0]
    residual_halo = halo(forcing, xy_land[:, :xy_rows], z_land[:, :z_rows], 0.0)
    diagonal_halo = halo(diagonal, xy_land[:, xy_rows:], z_land[:, z_rows:], 1.0)
    gathered = lax.dynamic_index_in_dim(
        summed.reshape(brick_count, grp_count, 5, slot_count), brick_index, keepdims=False
    )
    columns = jnp.transpose(gathered, (1, 0, 2)).reshape(5, -1)
    matrix = assemble(columns[0], (columns[1], columns[2], columns[3]), (PATCH_Y, 1, slot_count))
    factor = jnp.linalg.cholesky(matrix)

    def coarse_solve(terms):
        middle = lax.linalg.triangular_solve(factor, terms[:, None], left_side=True, lower=True)
        result = lax.linalg.triangular_solve(
            factor, middle, left_side=True, lower=True, transpose_a=True
        )
        return lax.dynamic_slice_in_dim(result[:, 0], slab_index * slot_count, slot_count)

    def round_trip(field, field_halo, coef, smooth):
        out, total, xy_land, z_land, dot = one_round(
            field, bonds, masks, diagonal, *field_halo, coef, smooth
        )
        total = total.reshape(-1)
        out_halo = halo(out, xy_land, z_land, 0.0)
        if smooth:
            return out, dot[0], None, out_halo
        count = brick_count * grp_count * slot_count
        mine = lax.dynamic_index_in_dim(
            total[1 : 1 + count].reshape(brick_count, -1), brick_index, keepdims=False
        )
        return out, dot[0], mine, out_halo

    def precondition(residual_field, field_halo, terms):
        smoothed_halo = [OMEGA * part / scale for part, scale in zip(field_halo, diagonal_halo)]
        return round_trip(residual_field, smoothed_halo, coarse_solve(terms), True)

    no_coarse = jnp.zeros((slot_count,), jnp.float32)
    terms = columns[4]
    solution_field = jnp.zeros_like(forcing)
    residual = forcing
    search, energy, _, search_halo = precondition(residual, residual_halo, terms)
    for iteration in range(ITERS):
        mapped, curvature, mapped_terms, mapped_halo = round_trip(
            search, search_halo, no_coarse, False
        )
        step_size = energy / curvature
        solution_field = solution_field + step_size * search
        residual = residual - step_size * mapped
        if iteration + 1 < ITERS:
            residual_halo = [
                part - step_size * change for part, change in zip(residual_halo, mapped_halo)
            ]
            terms = terms - step_size * mapped_terms
            smoothed, renewed, _, smoothed_halo = precondition(residual, residual_halo, terms)
            search = smoothed + renewed / energy * search
            search_halo = [
                part + renewed / energy * old for part, old in zip(smoothed_halo, search_halo)
            ]
            energy = renewed
    return (solution_field[None, None], residual[None, None])


def solution(mesh):
    return jax.shard_map(
        on_device,
        mesh=mesh,
        in_specs=(
            P("grp", "brick", None, None, None),
            P("grp", "brick", None, None, None),
            P("grp", "brick", None, None, None, None),
            P(),
            P(),
        ),
        out_specs=(P("grp", "brick", None, None, None), P("grp", "brick", None, None, None)),
        check_vma=False,
    )
```

```python
import functools

import jax
import jax.numpy as jnp
from jax import lax
from jax.experimental import pallas as pl
from jax.experimental.pallas import tpu as pltpu
from jax.sharding import PartitionSpec as P

MESH_IDS = pl.DeviceIdType.MESH

BS = 32
PATCH_X = 1
PATCH_Y = 2
ITERS = 3


OMEGA = 0.6


def share(
    x_ref, xy_ref, z_ref, o_ref, xy_out, z_out, landed_b, landed_g, landed_xy, landed_z,
    send_b, recv_b, send_g, recv_g, send_xy, recv_xy, send_z, recv_z, brick_peers, grp_peers,
    dot_ref=None,
):
    here_brick = lax.axis_index("brick")
    here_grp = lax.axis_index("grp")
    n_brick = landed_b.shape[0]
    n_grp = landed_g.shape[0]

    def send(src, dst, sends, recvs, index, peer):
        copy = pltpu.make_async_remote_copy(
            src_ref=src,
            dst_ref=dst.at[index],
            send_sem=sends.at[index],
            recv_sem=recvs.at[index],
            device_id=peer,
            device_id_type=MESH_IDS,
        )
        copy.start()
        return copy

    face_copies = [
        send(z_ref, landed_z, send_z, recv_z, 0, grp_peers[0]),
        send(z_ref, landed_z, send_z, recv_z, 1, grp_peers[-1]),
    ]
    face_copies += [
        send(xy_ref, landed_xy, send_xy, recv_xy, k, peer)
        for k, peer in enumerate(brick_peers, start=1)
    ]
    copies = [
        send(x_ref, landed_b, send_b, recv_b, k, peer)
        for k, peer in enumerate(brick_peers, start=1)
    ]
    landed_b[0] = x_ref[...]
    for copy in copies:
        copy.wait()
    total = landed_b[lax.rem(here_brick, n_brick)]
    for j in range(1, n_brick):
        total = total + landed_b[lax.rem(here_brick + n_brick - j, n_brick)]
    o_ref[...] = total
    landed_g[0] = total
    copies = [
        send(o_ref, landed_g, send_g, recv_g, k, peer)
        for k, peer in enumerate(grp_peers, start=1)
    ]
    for copy in copies:
        copy.wait()
    total = landed_g[lax.rem(here_grp, n_grp)]
    for j in range(1, n_grp):
        total = total + landed_g[lax.rem(here_grp + n_grp - j, n_grp)]
    o_ref[...] = total
    for copy in face_copies:
        copy.wait()
    landed_xy[0] = xy_ref[...]
    xy_out[...] = landed_xy[...]
    z_out[...] = landed_z[...]
    if dot_ref is not None:
        tile_rows, tile_lanes = o_ref.shape
        first = lax.broadcasted_iota(jnp.int32, (tile_rows, tile_lanes), 0) * tile_lanes
        first = first + lax.broadcasted_iota(jnp.int32, (tile_rows, tile_lanes), 1)
        dot_ref[0] = jnp.sum(jnp.where(first == 0, total, 0.0))


def exchange_kernel(
    x_ref, xy_ref, z_ref, o_ref, xy_out, z_out,
    landed_b, landed_g, landed_xy, landed_z,
    send_b, recv_b, send_g, recv_g, send_xy, recv_xy, send_z, recv_z,
):
    here_brick = lax.axis_index("brick")
    here_grp = lax.axis_index("grp")
    n_brick = landed_b.shape[0]
    n_grp = landed_g.shape[0]
    brick_peers = [(lax.rem(here_brick + k, n_brick), here_grp) for k in range(1, n_brick)]
    grp_peers = [(here_brick, lax.rem(here_grp + k, n_grp)) for k in range(1, n_grp)]
    barrier = pltpu.get_barrier_semaphore()
    for peer in brick_peers + grp_peers:
        pl.semaphore_signal(barrier, inc=1, device_id=peer, device_id_type=MESH_IDS)
    pl.semaphore_wait(barrier, len(brick_peers) + len(grp_peers))

    share(
        x_ref, xy_ref, z_ref, o_ref, xy_out, z_out, landed_b, landed_g, landed_xy, landed_z,
        send_b, recv_b, send_g, recv_g, send_xy, recv_xy, send_z, recv_z, brick_peers, grp_peers,
    )


def exchange(tile, xy, z, kernel_id):
    n_brick = lax.axis_size("brick")
    n_grp = lax.axis_size("grp")
    vmem = pl.BlockSpec(memory_space=pltpu.VMEM)
    dma = pltpu.SemaphoreType.DMA
    return pl.pallas_call(
        exchange_kernel,
        out_shape=(
            jax.ShapeDtypeStruct(tile.shape, jnp.float32),
            jax.ShapeDtypeStruct((n_brick,) + xy.shape, jnp.float32),
            jax.ShapeDtypeStruct((2,) + z.shape, jnp.float32),
        ),
        in_specs=[vmem] * 3,
        out_specs=(vmem, vmem, vmem),
        scratch_shapes=[
            pltpu.VMEM((n_brick,) + tile.shape, jnp.float32),
            pltpu.VMEM((n_grp,) + tile.shape, jnp.float32),
            pltpu.VMEM((n_brick,) + xy.shape, jnp.float32),
            pltpu.VMEM((2,) + z.shape, jnp.float32),
            dma((n_brick,)),
            dma((n_brick,)),
            dma((n_grp,)),
            dma((n_grp,)),
            dma((n_brick,)),
            dma((n_brick,)),
            dma((2,)),
            dma((2,)),
        ],
        compiler_params=pltpu.CompilerParams(collective_id=kernel_id, has_side_effects=True),
    )(tile, xy, z)


def stencil_body(
    coef_ref, f_ref, bonds_ref, masks_ref, diag_ref, rows_ref, faces_ref, o_ref, xy_ref, z_ref, smooth
):
    slots, width, lanes = f_ref.shape
    row = lax.broadcasted_iota(jnp.int32, (width, lanes), 0)
    lane = lax.broadcasted_iota(jnp.int32, (width, lanes), 1)
    pick = lax.broadcasted_iota(jnp.int32, (BS, lanes), 0)
    spot = lax.broadcasted_iota(jnp.int32, (BS, lanes), 1)
    spread_z = (spot // BS == pick).astype(jnp.float32)
    spread_y = (spot % BS == pick).astype(jnp.float32)

    def spread(face, table):
        high = face.astype(jnp.bfloat16)
        rest = face - high.astype(jnp.float32)
        middle = rest.astype(jnp.bfloat16)
        low = (rest - middle.astype(jnp.float32)).astype(jnp.bfloat16)
        table = table.astype(jnp.bfloat16)
        parts = [
            jnp.dot(part, table, preferred_element_type=jnp.float32) for part in (high, middle, low)
        ]
        return (parts[0] + parts[1]) + parts[2]

    borders = [
        row == width - 1,
        row == 0,
        lane >= lanes - BS,
        lane < BS,
        lane % BS == BS - 1,
        lane % BS == 0,
    ]
    source_lane = lax.broadcasted_iota(jnp.int32, (lanes, BS), 0)
    place = lax.broadcasted_iota(jnp.int32, (lanes, BS), 1)
    layers = [
        (source_lane == offset + step * place).astype(jnp.float32)
        for offset, step in ((0, 1), (lanes - BS, 1), (0, BS), (BS - 1, BS))
    ]
    flat_mask = spot // BS == pick

    def flatten(layer):
        spread_out = jnp.where(flat_mask, spread(layer, spread_y), 0.0)
        return jnp.sum(spread_out, axis=0, keepdims=True)

    dot = jnp.float32(0.0)
    sums = []
    for s in range(slots):
        ds = diag_ref[s]
        if smooth:
            rs = f_ref[s]
            fs = OMEGA * rs / ds
        else:
            fs = f_ref[s]
        xp = jnp.where(row == width - 1, rows_ref[0, s], pltpu.roll(fs, width - 1, 0))
        xm = jnp.where(row == 0, rows_ref[1, s], pltpu.roll(fs, 1, 0))
        yp = jnp.where(lane >= lanes - BS, spread(faces_ref[0, s], spread_y), pltpu.roll(fs, lanes - BS, 1))
        ym = jnp.where(lane < BS, spread(faces_ref[1, s], spread_y), pltpu.roll(fs, BS, 1))
        zp = jnp.where(lane % BS == BS - 1, spread(faces_ref[2, s], spread_z), pltpu.roll(fs, lanes - 1, 1))
        zm = jnp.where(lane % BS == 0, spread(faces_ref[3, s], spread_z), pltpu.roll(fs, 1, 1))
        total = ds * fs
        for d, beyond in enumerate([xp, xm, yp, ym, zp, zm]):
            base = 2 * (d * slots + s)
            active = jnp.where(borders[d], masks_ref[base + 1], masks_ref[base])
            total = total - bonds_ref[d, s] * active * beyond
        if smooth:
            total = fs + OMEGA * (rs - total) / ds
            total = total + coef_ref[s]
            dot = dot + jnp.sum(rs * total)
        else:
            dot = dot + jnp.sum(fs * total)
            sums.append(jnp.sum(total))
        o_ref[s] = total
        xy_ref[pl.ds(s, 1), :] = total[0:1, :]
        xy_ref[pl.ds(slots + s, 1), :] = total[width - 1 : width, :]
        if s == 0:
            xy_ref[pl.ds(2 * slots, 1), :] = flatten(spread(total, layers[0]))
        if s == slots - 1:
            xy_ref[pl.ds(2 * slots + 1, 1), :] = flatten(spread(total, layers[1]))
        z_ref[pl.ds(s, 1), :] = flatten(spread(total, layers[2]))
        z_ref[pl.ds(slots + s, 1), :] = flatten(spread(total, layers[3]))
    return dot, sums


def round_kernel(
    coef_ref, f_ref, bonds_ref, masks_ref, diag_ref, rows_ref, faces_ref,
    o_ref, total_ref, xy_out, z_out, dot_ref,
    xy_buf, z_buf, tile_buf, landed_b, landed_g, landed_xy, landed_z,
    send_b, recv_b, send_g, recv_g, send_xy, recv_xy, send_z, recv_z, *, smooth
):
    here_brick = lax.axis_index("brick")
    here_grp = lax.axis_index("grp")
    n_brick = landed_b.shape[0]
    n_grp = landed_g.shape[0]
    brick_peers = [(lax.rem(here_brick + k, n_brick), here_grp) for k in range(1, n_brick)]
    grp_peers = [(here_brick, lax.rem(here_grp + k, n_grp)) for k in range(1, n_grp)]
    barrier = pltpu.get_barrier_semaphore()
    for peer in brick_peers + grp_peers:
        pl.semaphore_signal(barrier, inc=1, device_id=peer, device_id_type=MESH_IDS)
    dot, sums = stencil_body(
        coef_ref, f_ref, bonds_ref, masks_ref, diag_ref, rows_ref, faces_ref, o_ref, xy_buf, z_buf,
        smooth,
    )
    tile_rows, tile_lanes = tile_buf.shape
    flat = lax.broadcasted_iota(jnp.int32, (tile_rows, tile_lanes), 0) * tile_lanes
    flat = flat + lax.broadcasted_iota(jnp.int32, (tile_rows, tile_lanes), 1)
    tile = jnp.where(flat == 0, dot, 0.0)
    slots = f_ref.shape[0]
    for s, value in enumerate(sums):
        position = 1 + (here_brick * n_grp + here_grp) * slots + s
        tile = jnp.where(flat == position, value, tile)
    tile_buf[...] = tile
    pl.semaphore_wait(barrier, len(brick_peers) + len(grp_peers))
    share(
        tile_buf, xy_buf, z_buf, total_ref, xy_out, z_out, landed_b, landed_g, landed_xy, landed_z,
        send_b, recv_b, send_g, recv_g, send_xy, recv_xy, send_z, recv_z, brick_peers, grp_peers,
        dot_ref=dot_ref,
    )


def one_round(field, bonds, masks, diag, rows, faces, coef, smooth):
    slots, _, lanes = field.shape
    n_brick = lax.axis_size("brick")
    n_grp = lax.axis_size("grp")
    tile = (8, 128)
    xy = (2 * slots + 2, lanes)
    z = (2 * slots, lanes)
    vmem = pl.BlockSpec(memory_space=pltpu.VMEM)
    smem = pl.BlockSpec(memory_space=pltpu.SMEM)
    dma = pltpu.SemaphoreType.DMA
    return pl.pallas_call(
        functools.partial(round_kernel, smooth=smooth),
        out_shape=(
            jax.ShapeDtypeStruct(field.shape, jnp.float32),
            jax.ShapeDtypeStruct(tile, jnp.float32),
            jax.ShapeDtypeStruct((n_brick,) + xy, jnp.float32),
            jax.ShapeDtypeStruct((2,) + z, jnp.float32),
            jax.ShapeDtypeStruct((1,), jnp.float32),
        ),
        in_specs=[smem, vmem, vmem, smem, vmem, vmem, vmem],
        out_specs=(vmem, vmem, vmem, vmem, smem),
        scratch_shapes=[
            pltpu.VMEM(xy, jnp.float32),
            pltpu.VMEM(z, jnp.float32),
            pltpu.VMEM(tile, jnp.float32),
            pltpu.VMEM((n_brick,) + tile, jnp.float32),
            pltpu.VMEM((n_grp,) + tile, jnp.float32),
            pltpu.VMEM((n_brick,) + xy, jnp.float32),
            pltpu.VMEM((2,) + z, jnp.float32),
            dma((n_brick,)),
            dma((n_brick,)),
            dma((n_grp,)),
            dma((n_grp,)),
            dma((n_brick,)),
            dma((n_brick,)),
            dma((2,)),
            dma((2,)),
        ],
        compiler_params=pltpu.CompilerParams(
            collective_id=3 if smooth else 1, has_side_effects=True
        ),
    )(coef, field, bonds, masks, diag, rows, faces)


def assemble(coarse_diag, couplings, strides):
    extent = coarse_diag.shape[0]
    matrix = jnp.diag(coarse_diag)
    for coupling, stride in zip(couplings, strides):
        banded = coupling[: extent - stride]
        matrix = matrix - jnp.diag(banded, stride) - jnp.diag(banded, -stride)
    return matrix


def on_device(source, uptake, conductance, occupancy, assignment):
    face_size = BS * BS
    slot_count = PATCH_X * PATCH_Y
    slab_index = lax.axis_index("grp")
    brick_index = lax.axis_index("brick")
    brick_count = lax.axis_size("brick")
    across = brick_count // 2
    peer_ids = jnp.arange(brick_count, dtype=jnp.int32)
    patch_index = assignment[brick_index]
    patch_row = patch_index // across
    patch_column = patch_index % across

    def owner_of(row_shift, column_shift):
        row_target = patch_row + row_shift
        column_target = patch_column + column_shift
        inside = (
            (row_target >= 0) & (row_target < 2) & (column_target >= 0) & (column_target < across)
        )
        holder = jnp.sum(jnp.where(assignment == row_target * across + column_target, peer_ids, 0))
        return jnp.where(inside, holder, -1)

    wanted = jnp.stack([owner_of(1, 0), owner_of(-1, 0), owner_of(0, 1), owner_of(0, -1)])
    padded = jnp.pad(occupancy, 1)
    window = lax.dynamic_slice(
        padded,
        (slab_index, patch_row * PATCH_X, patch_column * PATCH_Y),
        (3, PATCH_X + 2, PATCH_Y + 2),
    ).astype(jnp.float32)
    centre = window[1, 1:-1, 1:-1].reshape(slot_count)
    toward = [
        window[1, 2:, 1:-1],
        window[1, :-2, 1:-1],
        window[1, 1:-1, 2:],
        window[1, 1:-1, :-2],
        window[2, 1:-1, 1:-1],
        window[0, 1:-1, 1:-1],
    ]
    first_axis = lax.broadcasted_iota(jnp.int32, (1, BS, face_size), 1)
    flat_axis = lax.broadcasted_iota(jnp.int32, (1, BS, face_size), 2)
    second_axis = flat_axis // BS
    third_axis = flat_axis % BS
    cube_third = lax.broadcasted_iota(jnp.int32, (1, BS, BS, BS), 3)
    borders = [
        first_axis == BS - 1,
        first_axis == 0,
        second_axis == BS - 1,
        second_axis == 0,
        third_axis == BS - 1,
        third_axis == 0,
    ]
    bonds = conductance[0, 0]
    live_here = centre[:, None, None]
    effective = []
    for direction in range(6):
        neighbour_live = toward[direction].reshape(slot_count)[:, None, None]
        active = jnp.where(borders[direction], live_here * neighbour_live, live_here)
        effective.append(bonds[direction] * active)
    absorb = uptake[0, 0]
    diagonal = absorb
    for direction in range(6):
        diagonal = diagonal + effective[direction]

    masks = jnp.stack(
        [
            jnp.stack([centre, centre * toward[direction].reshape(slot_count)], axis=1)
            for direction in range(6)
        ]
    ).reshape(-1)

    lane_ids = jnp.arange(face_size, dtype=jnp.int32)[:, None]
    layer_ids = BS * jnp.arange(BS, dtype=jnp.int32)[None, :]
    picker = jnp.concatenate([lane_ids == layer_ids, lane_ids == layer_ids + BS - 1], axis=1)
    picker = picker.astype(jnp.float32)

    def side_faces(field):
        rows_of = field.reshape(slot_count * BS, face_size)
        high = rows_of.astype(jnp.bfloat16)
        rest = rows_of - high.astype(jnp.float32)
        middle = rest.astype(jnp.bfloat16)
        low = (rest - middle.astype(jnp.float32)).astype(jnp.bfloat16)
        table = picker.astype(jnp.bfloat16)
        parts = [
            jnp.dot(part, table, preferred_element_type=jnp.float32) for part in (high, middle, low)
        ]
        picked = (parts[0] + parts[1]) + parts[2]
        z = picked.reshape(slot_count, BS, 2, BS).transpose(2, 0, 1, 3)
        xy = jnp.concatenate(
            [
                field[:, 0, :],
                field[:, BS - 1, :],
                field[0, :, :BS].reshape(1, face_size),
                field[slot_count - 1, :, face_size - BS :].reshape(1, face_size),
            ]
        )
        return xy, z.reshape(2 * slot_count, face_size)

    def pick(landed, holder, fill):
        offset = lax.rem(brick_index - holder + brick_count, brick_count)
        got = lax.dynamic_index_in_dim(landed, offset, keepdims=False)
        return jnp.where(holder >= 0, got, fill)

    def halo(field, xy_land, z_land, fill):
        xplus = pick(xy_land, wanted[0], fill)
        xminus = pick(xy_land, wanted[1], fill)
        yplus = pick(xy_land, wanted[2], fill)
        yminus = pick(xy_land, wanted[3], fill)
        rows = jnp.stack([xplus[:slot_count], xminus[slot_count : 2 * slot_count]])[:, :, None, :]
        beyond_yplus = jnp.stack([field[1, :, :BS], yplus[2 * slot_count].reshape(BS, BS)])
        beyond_yminus = jnp.stack(
            [yminus[2 * slot_count + 1].reshape(BS, BS), field[0, :, face_size - BS :]]
        )
        above = jnp.where(slab_index < grp_count - 1, z_land[1, :slot_count], fill)
        below = jnp.where(slab_index > 0, z_land[0, slot_count:], fill)
        faces = jnp.stack(
            [
                beyond_yplus,
                beyond_yminus,
                above.reshape(slot_count, BS, BS),
                below.reshape(slot_count, BS, BS),
            ]
        )
        return rows, faces

    slot_ids = jnp.arange(slot_count)
    brick_first = slot_ids // PATCH_Y
    brick_second = slot_ids % PATCH_Y
    inside = [
        (brick_first < PATCH_X - 1).astype(jnp.float32),
        (brick_first > 0).astype(jnp.float32),
        (brick_second < PATCH_Y - 1).astype(jnp.float32),
        (brick_second > 0).astype(jnp.float32),
    ]
    face_sums = [
        jnp.sum(effective[0][:, BS - 1, :], axis=1),
        jnp.sum(effective[1][:, 0, :], axis=1),
        jnp.sum(effective[2][:, :, face_size - BS :], axis=(1, 2)),
        jnp.sum(effective[3][:, :, :BS], axis=(1, 2)),
        jnp.sum(jnp.where(borders[4], effective[4], 0.0), axis=(1, 2)),
        jnp.sum(jnp.where(borders[5], effective[5], 0.0), axis=(1, 2)),
    ]
    coarse_diag = jnp.sum(absorb, axis=(1, 2))
    for direction in range(4):
        coarse_diag = coarse_diag + face_sums[direction] * inside[direction]
    coarse_diag = coarse_diag + face_sums[4] + face_sums[5]
    grp_count = lax.axis_size("grp")
    grp_ids = jnp.arange(grp_count, dtype=jnp.int32)

    def slab_slot(values):
        here = (grp_ids == slab_index).astype(jnp.float32)
        return here[:, None, None] * values[None]

    forcing = source[0, 0] * live_here

    def as_tile(values):
        rows = -(-values.shape[0] // 128)
        rows = -(-rows // 8) * 8
        return jnp.pad(values, (0, rows * 128 - values.shape[0])).reshape(rows, 128)

    record = jnp.stack(
        [
            coarse_diag,
            face_sums[0] * inside[0],
            face_sums[2] * inside[2],
            face_sums[4],
            jnp.sum(forcing, axis=(1, 2)),
        ]
    )
    brick_here = (peer_ids == brick_index).astype(jnp.float32)
    spread = (brick_here[:, None, None, None] * slab_slot(record)[None]).reshape(-1)
    forcing_xy, forcing_z = side_faces(forcing)
    diagonal_xy, diagonal_z = side_faces(diagonal)
    summed, xy_land, z_land = exchange(
        as_tile(spread),
        jnp.concatenate([forcing_xy, diagonal_xy]),
        jnp.concatenate([forcing_z, diagonal_z]),
        2,
    )
    summed = summed.reshape(-1)[: spread.shape[0]]
    xy_rows = forcing_xy.shape[0]
    z_rows = forcing_z.shape[0]
    residual_halo = halo(forcing, xy_land[:, :xy_rows], z_land[:, :z_rows], 0.0)
    diagonal_halo = halo(diagonal, xy_land[:, xy_rows:], z_land[:, z_rows:], 1.0)
    gathered = lax.dynamic_index_in_dim(
        summed.reshape(brick_count, grp_count, 5, slot_count), brick_index, keepdims=False
    )
    columns = jnp.transpose(gathered, (1, 0, 2)).reshape(5, -1)
    matrix = assemble(columns[0], (columns[1], columns[2], columns[3]), (PATCH_Y, 1, slot_count))
    factor = jnp.linalg.cholesky(matrix)

    def coarse_solve(terms):
        middle = lax.linalg.triangular_solve(factor, terms[:, None], left_side=True, lower=True)
        result = lax.linalg.triangular_solve(
            factor, middle, left_side=True, lower=True, transpose_a=True
        )
        return lax.dynamic_slice_in_dim(result[:, 0], slab_index * slot_count, slot_count)

    def round_trip(field, field_halo, coef, smooth):
        out, total, xy_land, z_land, dot = one_round(
            field, bonds, masks, diagonal, *field_halo, coef, smooth
        )
        total = total.reshape(-1)
        out_halo = halo(out, xy_land, z_land, 0.0)
        if smooth:
            return out, dot[0], None, out_halo
        count = brick_count * grp_count * slot_count
        mine = lax.dynamic_index_in_dim(
            total[1 : 1 + count].reshape(brick_count, -1), brick_index, keepdims=False
        )
        return out, dot[0], mine, out_halo

    def precondition(residual_field, field_halo, terms):
        smoothed_halo = [OMEGA * part / scale for part, scale in zip(field_halo, diagonal_halo)]
        return round_trip(residual_field, smoothed_halo, coarse_solve(terms), True)

    no_coarse = jnp.zeros((slot_count,), jnp.float32)
    terms = columns[4]
    solution_field = jnp.zeros_like(forcing)
    residual = forcing
    search, energy, _, search_halo = precondition(residual, residual_halo, terms)
    for iteration in range(ITERS):
        mapped, curvature, mapped_terms, mapped_halo = round_trip(
            search, search_halo, no_coarse, False
        )
        step_size = energy / curvature
        solution_field = solution_field + step_size * search
        residual = residual - step_size * mapped
        if iteration + 1 < ITERS:
            residual_halo = [
                part - step_size * change for part, change in zip(residual_halo, mapped_halo)
            ]
            terms = terms - step_size * mapped_terms
            smoothed, renewed, _, smoothed_halo = precondition(residual, residual_halo, terms)
            search = smoothed + renewed / energy * search
            search_halo = [
                part + renewed / energy * old for part, old in zip(smoothed_halo, search_halo)
            ]
            energy = renewed
    return (solution_field[None, None], residual[None, None])


def solution(mesh):
    return jax.shard_map(
        on_device,
        mesh=mesh,
        in_specs=(
            P("grp", "brick", None, None, None),
            P("grp", "brick", None, None, None),
            P("grp", "brick", None, None, None, None),
            P(),
            P(),
        ),
        out_specs=(P("grp", "brick", None, None, None), P("grp", "brick", None, None, None)),
        check_vma=False,
    )
```

```python
import functools

import jax
import jax.numpy as jnp
from jax import lax
from jax.experimental import pallas as pl
from jax.experimental.pallas import tpu as pltpu
from jax.sharding import PartitionSpec as P

MESH_IDS = pl.DeviceIdType.MESH

BS = 32
PATCH_X = 1
PATCH_Y = 2
ITERS = 3


OMEGA = 0.6


def share(
    x_ref, xy_ref, z_ref, o_ref, xy_out, z_out, landed_b, landed_g, landed_xy, landed_z,
    send_b, recv_b, send_g, recv_g, send_xy, recv_xy, send_z, recv_z, brick_peers, grp_peers,
    dot_ref=None, with_faces=True,
):
    here_brick = lax.axis_index("brick")
    here_grp = lax.axis_index("grp")
    n_brick = landed_b.shape[0]
    n_grp = landed_g.shape[0]

    def send(src, dst, sends, recvs, index, peer):
        copy = pltpu.make_async_remote_copy(
            src_ref=src,
            dst_ref=dst.at[index],
            send_sem=sends.at[index],
            recv_sem=recvs.at[index],
            device_id=peer,
            device_id_type=MESH_IDS,
        )
        copy.start()
        return copy

    face_copies = []
    if with_faces:
        face_copies = [
            send(z_ref, landed_z, send_z, recv_z, 0, grp_peers[0]),
            send(z_ref, landed_z, send_z, recv_z, 1, grp_peers[-1]),
        ]
        face_copies += [
            send(xy_ref, landed_xy, send_xy, recv_xy, k, peer)
            for k, peer in enumerate(brick_peers, start=1)
        ]
    copies = [
        send(x_ref, landed_b, send_b, recv_b, k, peer)
        for k, peer in enumerate(brick_peers, start=1)
    ]
    landed_b[0] = x_ref[...]
    for copy in copies:
        copy.wait()
    total = landed_b[lax.rem(here_brick, n_brick)]
    for j in range(1, n_brick):
        total = total + landed_b[lax.rem(here_brick + n_brick - j, n_brick)]
    o_ref[...] = total
    landed_g[0] = total
    copies = [
        send(o_ref, landed_g, send_g, recv_g, k, peer)
        for k, peer in enumerate(grp_peers, start=1)
    ]
    for copy in copies:
        copy.wait()
    total = landed_g[lax.rem(here_grp, n_grp)]
    for j in range(1, n_grp):
        total = total + landed_g[lax.rem(here_grp + n_grp - j, n_grp)]
    o_ref[...] = total
    for copy in face_copies:
        copy.wait()
    if with_faces:
        landed_xy[0] = xy_ref[...]
        xy_out[...] = landed_xy[...]
        z_out[...] = landed_z[...]
    else:
        xy_out[...] = jnp.zeros(xy_out.shape, jnp.float32)
        z_out[...] = jnp.zeros(z_out.shape, jnp.float32)
    if dot_ref is not None:
        tile_rows, tile_lanes = o_ref.shape
        first = lax.broadcasted_iota(jnp.int32, (tile_rows, tile_lanes), 0) * tile_lanes
        first = first + lax.broadcasted_iota(jnp.int32, (tile_rows, tile_lanes), 1)
        dot_ref[0] = jnp.sum(jnp.where(first == 0, total, 0.0))


def exchange_kernel(
    x_ref, xy_ref, z_ref, o_ref, xy_out, z_out,
    landed_b, landed_g, landed_xy, landed_z,
    send_b, recv_b, send_g, recv_g, send_xy, recv_xy, send_z, recv_z,
):
    here_brick = lax.axis_index("brick")
    here_grp = lax.axis_index("grp")
    n_brick = landed_b.shape[0]
    n_grp = landed_g.shape[0]
    brick_peers = [(lax.rem(here_brick + k, n_brick), here_grp) for k in range(1, n_brick)]
    grp_peers = [(here_brick, lax.rem(here_grp + k, n_grp)) for k in range(1, n_grp)]
    barrier = pltpu.get_barrier_semaphore()
    for peer in brick_peers + grp_peers:
        pl.semaphore_signal(barrier, inc=1, device_id=peer, device_id_type=MESH_IDS)
    pl.semaphore_wait(barrier, len(brick_peers) + len(grp_peers))

    share(
        x_ref, xy_ref, z_ref, o_ref, xy_out, z_out, landed_b, landed_g, landed_xy, landed_z,
        send_b, recv_b, send_g, recv_g, send_xy, recv_xy, send_z, recv_z, brick_peers, grp_peers,
    )


def exchange(tile, xy, z, kernel_id):
    n_brick = lax.axis_size("brick")
    n_grp = lax.axis_size("grp")
    vmem = pl.BlockSpec(memory_space=pltpu.VMEM)
    dma = pltpu.SemaphoreType.DMA
    return pl.pallas_call(
        exchange_kernel,
        out_shape=(
            jax.ShapeDtypeStruct(tile.shape, jnp.float32),
            jax.ShapeDtypeStruct((n_brick,) + xy.shape, jnp.float32),
            jax.ShapeDtypeStruct((2,) + z.shape, jnp.float32),
        ),
        in_specs=[vmem] * 3,
        out_specs=(vmem, vmem, vmem),
        scratch_shapes=[
            pltpu.VMEM((n_brick,) + tile.shape, jnp.float32),
            pltpu.VMEM((n_grp,) + tile.shape, jnp.float32),
            pltpu.VMEM((n_brick,) + xy.shape, jnp.float32),
            pltpu.VMEM((2,) + z.shape, jnp.float32),
            dma((n_brick,)),
            dma((n_brick,)),
            dma((n_grp,)),
            dma((n_grp,)),
            dma((n_brick,)),
            dma((n_brick,)),
            dma((2,)),
            dma((2,)),
        ],
        compiler_params=pltpu.CompilerParams(collective_id=kernel_id, has_side_effects=True),
    )(tile, xy, z)


def stencil_body(
    coef_ref, f_ref, bonds_ref, masks_ref, diag_ref, rows_ref, faces_ref, o_ref, xy_ref, z_ref, smooth,
    with_faces=True,
):
    slots, width, lanes = f_ref.shape
    row = lax.broadcasted_iota(jnp.int32, (width, lanes), 0)
    lane = lax.broadcasted_iota(jnp.int32, (width, lanes), 1)
    pick = lax.broadcasted_iota(jnp.int32, (BS, lanes), 0)
    spot = lax.broadcasted_iota(jnp.int32, (BS, lanes), 1)
    spread_z = (spot // BS == pick).astype(jnp.float32)
    spread_y = (spot % BS == pick).astype(jnp.float32)

    def spread(face, table):
        high = face.astype(jnp.bfloat16)
        rest = face - high.astype(jnp.float32)
        middle = rest.astype(jnp.bfloat16)
        low = (rest - middle.astype(jnp.float32)).astype(jnp.bfloat16)
        table = table.astype(jnp.bfloat16)
        parts = [
            jnp.dot(part, table, preferred_element_type=jnp.float32) for part in (high, middle, low)
        ]
        return (parts[0] + parts[1]) + parts[2]

    borders = [
        row == width - 1,
        row == 0,
        lane >= lanes - BS,
        lane < BS,
        lane % BS == BS - 1,
        lane % BS == 0,
    ]
    source_lane = lax.broadcasted_iota(jnp.int32, (lanes, BS), 0)
    place = lax.broadcasted_iota(jnp.int32, (lanes, BS), 1)
    layers = [
        (source_lane == offset + step * place).astype(jnp.float32)
        for offset, step in ((0, 1), (lanes - BS, 1), (0, BS), (BS - 1, BS))
    ]
    flat_mask = spot // BS == pick

    def flatten(layer):
        spread_out = jnp.where(flat_mask, spread(layer, spread_y), 0.0)
        return jnp.sum(spread_out, axis=0, keepdims=True)

    dot = jnp.float32(0.0)
    sums = []
    for s in range(slots):
        ds = diag_ref[s]
        if smooth:
            rs = f_ref[s]
            fs = OMEGA * rs / ds
        else:
            fs = f_ref[s]
        xp = jnp.where(row == width - 1, rows_ref[0, s], pltpu.roll(fs, width - 1, 0))
        xm = jnp.where(row == 0, rows_ref[1, s], pltpu.roll(fs, 1, 0))
        yp = jnp.where(lane >= lanes - BS, spread(faces_ref[0, s], spread_y), pltpu.roll(fs, lanes - BS, 1))
        ym = jnp.where(lane < BS, spread(faces_ref[1, s], spread_y), pltpu.roll(fs, BS, 1))
        zp = jnp.where(lane % BS == BS - 1, spread(faces_ref[2, s], spread_z), pltpu.roll(fs, lanes - 1, 1))
        zm = jnp.where(lane % BS == 0, spread(faces_ref[3, s], spread_z), pltpu.roll(fs, 1, 1))
        total = ds * fs
        for d, beyond in enumerate([xp, xm, yp, ym, zp, zm]):
            base = 2 * (d * slots + s)
            active = jnp.where(borders[d], masks_ref[base + 1], masks_ref[base])
            total = total - bonds_ref[d, s] * active * beyond
        if smooth:
            total = fs + OMEGA * (rs - total) / ds
            total = total + coef_ref[s]
            dot = dot + jnp.sum(rs * total)
        else:
            dot = dot + jnp.sum(fs * total)
            sums.append(jnp.sum(total))
        o_ref[s] = total
        if not with_faces:
            continue
        xy_ref[pl.ds(s, 1), :] = total[0:1, :]
        xy_ref[pl.ds(slots + s, 1), :] = total[width - 1 : width, :]
        if s == 0:
            xy_ref[pl.ds(2 * slots, 1), :] = flatten(spread(total, layers[0]))
        if s == slots - 1:
            xy_ref[pl.ds(2 * slots + 1, 1), :] = flatten(spread(total, layers[1]))
        z_ref[pl.ds(s, 1), :] = flatten(spread(total, layers[2]))
        z_ref[pl.ds(slots + s, 1), :] = flatten(spread(total, layers[3]))
    return dot, sums


def round_kernel(
    coef_ref, f_ref, bonds_ref, masks_ref, diag_ref, rows_ref, faces_ref,
    o_ref, total_ref, xy_out, z_out, dot_ref,
    xy_buf, z_buf, tile_buf, landed_b, landed_g, landed_xy, landed_z,
    send_b, recv_b, send_g, recv_g, send_xy, recv_xy, send_z, recv_z, *, smooth, with_faces
):
    here_brick = lax.axis_index("brick")
    here_grp = lax.axis_index("grp")
    n_brick = landed_b.shape[0]
    n_grp = landed_g.shape[0]
    brick_peers = [(lax.rem(here_brick + k, n_brick), here_grp) for k in range(1, n_brick)]
    grp_peers = [(here_brick, lax.rem(here_grp + k, n_grp)) for k in range(1, n_grp)]
    barrier = pltpu.get_barrier_semaphore()
    for peer in brick_peers + grp_peers:
        pl.semaphore_signal(barrier, inc=1, device_id=peer, device_id_type=MESH_IDS)
    dot, sums = stencil_body(
        coef_ref, f_ref, bonds_ref, masks_ref, diag_ref, rows_ref, faces_ref, o_ref, xy_buf, z_buf,
        smooth, with_faces,
    )
    tile_rows, tile_lanes = tile_buf.shape
    flat = lax.broadcasted_iota(jnp.int32, (tile_rows, tile_lanes), 0) * tile_lanes
    flat = flat + lax.broadcasted_iota(jnp.int32, (tile_rows, tile_lanes), 1)
    tile = jnp.where(flat == 0, dot, 0.0)
    slots = f_ref.shape[0]
    for s, value in enumerate(sums):
        position = 1 + (here_brick * n_grp + here_grp) * slots + s
        tile = jnp.where(flat == position, value, tile)
    tile_buf[...] = tile
    pl.semaphore_wait(barrier, len(brick_peers) + len(grp_peers))
    share(
        tile_buf, xy_buf, z_buf, total_ref, xy_out, z_out, landed_b, landed_g, landed_xy, landed_z,
        send_b, recv_b, send_g, recv_g, send_xy, recv_xy, send_z, recv_z, brick_peers, grp_peers,
        dot_ref=dot_ref, with_faces=with_faces,
    )


def one_round(field, bonds, masks, diag, rows, faces, coef, smooth, with_faces=True):
    slots, _, lanes = field.shape
    n_brick = lax.axis_size("brick")
    n_grp = lax.axis_size("grp")
    tile = (8, 128)
    xy = (2 * slots + 2, lanes)
    z = (2 * slots, lanes)
    vmem = pl.BlockSpec(memory_space=pltpu.VMEM)
    smem = pl.BlockSpec(memory_space=pltpu.SMEM)
    dma = pltpu.SemaphoreType.DMA
    return pl.pallas_call(
        functools.partial(round_kernel, smooth=smooth, with_faces=with_faces),
        out_shape=(
            jax.ShapeDtypeStruct(field.shape, jnp.float32),
            jax.ShapeDtypeStruct(tile, jnp.float32),
            jax.ShapeDtypeStruct((n_brick,) + xy, jnp.float32),
            jax.ShapeDtypeStruct((2,) + z, jnp.float32),
            jax.ShapeDtypeStruct((1,), jnp.float32),
        ),
        in_specs=[smem, vmem, vmem, smem, vmem, vmem, vmem],
        out_specs=(vmem, vmem, vmem, vmem, smem),
        scratch_shapes=[
            pltpu.VMEM(xy, jnp.float32),
            pltpu.VMEM(z, jnp.float32),
            pltpu.VMEM(tile, jnp.float32),
            pltpu.VMEM((n_brick,) + tile, jnp.float32),
            pltpu.VMEM((n_grp,) + tile, jnp.float32),
            pltpu.VMEM((n_brick,) + xy, jnp.float32),
            pltpu.VMEM((2,) + z, jnp.float32),
            dma((n_brick,)),
            dma((n_brick,)),
            dma((n_grp,)),
            dma((n_grp,)),
            dma((n_brick,)),
            dma((n_brick,)),
            dma((2,)),
            dma((2,)),
        ],
        compiler_params=pltpu.CompilerParams(
            collective_id=(3 if smooth else 1) if with_faces else 4, has_side_effects=True
        ),
    )(coef, field, bonds, masks, diag, rows, faces)


def assemble(coarse_diag, couplings, strides):
    extent = coarse_diag.shape[0]
    matrix = jnp.diag(coarse_diag)
    for coupling, stride in zip(couplings, strides):
        banded = coupling[: extent - stride]
        matrix = matrix - jnp.diag(banded, stride) - jnp.diag(banded, -stride)
    return matrix


def on_device(source, uptake, conductance, occupancy, assignment):
    face_size = BS * BS
    slot_count = PATCH_X * PATCH_Y
    slab_index = lax.axis_index("grp")
    brick_index = lax.axis_index("brick")
    brick_count = lax.axis_size("brick")
    across = brick_count // 2
    peer_ids = jnp.arange(brick_count, dtype=jnp.int32)
    patch_index = assignment[brick_index]
    patch_row = patch_index // across
    patch_column = patch_index % across

    def owner_of(row_shift, column_shift):
        row_target = patch_row + row_shift
        column_target = patch_column + column_shift
        inside = (
            (row_target >= 0) & (row_target < 2) & (column_target >= 0) & (column_target < across)
        )
        holder = jnp.sum(jnp.where(assignment == row_target * across + column_target, peer_ids, 0))
        return jnp.where(inside, holder, -1)

    wanted = jnp.stack([owner_of(1, 0), owner_of(-1, 0), owner_of(0, 1), owner_of(0, -1)])
    padded = jnp.pad(occupancy, 1)
    window = lax.dynamic_slice(
        padded,
        (slab_index, patch_row * PATCH_X, patch_column * PATCH_Y),
        (3, PATCH_X + 2, PATCH_Y + 2),
    ).astype(jnp.float32)
    centre = window[1, 1:-1, 1:-1].reshape(slot_count)
    toward = [
        window[1, 2:, 1:-1],
        window[1, :-2, 1:-1],
        window[1, 1:-1, 2:],
        window[1, 1:-1, :-2],
        window[2, 1:-1, 1:-1],
        window[0, 1:-1, 1:-1],
    ]
    first_axis = lax.broadcasted_iota(jnp.int32, (1, BS, face_size), 1)
    flat_axis = lax.broadcasted_iota(jnp.int32, (1, BS, face_size), 2)
    second_axis = flat_axis // BS
    third_axis = flat_axis % BS
    cube_third = lax.broadcasted_iota(jnp.int32, (1, BS, BS, BS), 3)
    borders = [
        first_axis == BS - 1,
        first_axis == 0,
        second_axis == BS - 1,
        second_axis == 0,
        third_axis == BS - 1,
        third_axis == 0,
    ]
    bonds = conductance[0, 0]
    live_here = centre[:, None, None]
    effective = []
    for direction in range(6):
        neighbour_live = toward[direction].reshape(slot_count)[:, None, None]
        active = jnp.where(borders[direction], live_here * neighbour_live, live_here)
        effective.append(bonds[direction] * active)
    absorb = uptake[0, 0]
    diagonal = absorb
    for direction in range(6):
        diagonal = diagonal + effective[direction]

    masks = jnp.stack(
        [
            jnp.stack([centre, centre * toward[direction].reshape(slot_count)], axis=1)
            for direction in range(6)
        ]
    ).reshape(-1)

    lane_ids = jnp.arange(face_size, dtype=jnp.int32)[:, None]
    layer_ids = BS * jnp.arange(BS, dtype=jnp.int32)[None, :]
    picker = jnp.concatenate([lane_ids == layer_ids, lane_ids == layer_ids + BS - 1], axis=1)
    picker = picker.astype(jnp.float32)

    def side_faces(field):
        picked = jnp.dot(
            field.reshape(slot_count * BS, face_size), picker, precision=lax.Precision.HIGHEST
        )
        z = picked.reshape(slot_count, BS, 2, BS).transpose(2, 0, 1, 3)
        xy = jnp.concatenate(
            [
                field[:, 0, :],
                field[:, BS - 1, :],
                field[0, :, :BS].reshape(1, face_size),
                field[slot_count - 1, :, face_size - BS :].reshape(1, face_size),
            ]
        )
        return xy, z.reshape(2 * slot_count, face_size)

    def pick(landed, holder, fill):
        offset = lax.rem(brick_index - holder + brick_count, brick_count)
        got = lax.dynamic_index_in_dim(landed, offset, keepdims=False)
        return jnp.where(holder >= 0, got, fill)

    def halo(field, xy_land, z_land, fill):
        xplus = pick(xy_land, wanted[0], fill)
        xminus = pick(xy_land, wanted[1], fill)
        yplus = pick(xy_land, wanted[2], fill)
        yminus = pick(xy_land, wanted[3], fill)
        rows = jnp.stack([xplus[:slot_count], xminus[slot_count : 2 * slot_count]])[:, :, None, :]
        beyond_yplus = jnp.stack([field[1, :, :BS], yplus[2 * slot_count].reshape(BS, BS)])
        beyond_yminus = jnp.stack(
            [yminus[2 * slot_count + 1].reshape(BS, BS), field[0, :, face_size - BS :]]
        )
        above = jnp.where(slab_index < grp_count - 1, z_land[1, :slot_count], fill)
        below = jnp.where(slab_index > 0, z_land[0, slot_count:], fill)
        faces = jnp.stack(
            [
                beyond_yplus,
                beyond_yminus,
                above.reshape(slot_count, BS, BS),
                below.reshape(slot_count, BS, BS),
            ]
        )
        return rows, faces

    slot_ids = jnp.arange(slot_count)
    brick_first = slot_ids // PATCH_Y
    brick_second = slot_ids % PATCH_Y
    inside = [
        (brick_first < PATCH_X - 1).astype(jnp.float32),
        (brick_first > 0).astype(jnp.float32),
        (brick_second < PATCH_Y - 1).astype(jnp.float32),
        (brick_second > 0).astype(jnp.float32),
    ]
    face_sums = [
        jnp.sum(effective[0][:, BS - 1, :], axis=1),
        jnp.sum(effective[1][:, 0, :], axis=1),
        jnp.sum(effective[2][:, :, face_size - BS :], axis=(1, 2)),
        jnp.sum(effective[3][:, :, :BS], axis=(1, 2)),
        jnp.sum(jnp.where(borders[4], effective[4], 0.0), axis=(1, 2)),
        jnp.sum(jnp.where(borders[5], effective[5], 0.0), axis=(1, 2)),
    ]
    coarse_diag = jnp.sum(absorb, axis=(1, 2))
    for direction in range(4):
        coarse_diag = coarse_diag + face_sums[direction] * inside[direction]
    coarse_diag = coarse_diag + face_sums[4] + face_sums[5]
    grp_count = lax.axis_size("grp")
    grp_ids = jnp.arange(grp_count, dtype=jnp.int32)

    def slab_slot(values):
        here = (grp_ids == slab_index).astype(jnp.float32)
        return here[:, None, None] * values[None]

    forcing = source[0, 0] * live_here

    def as_tile(values):
        rows = -(-values.shape[0] // 128)
        rows = -(-rows // 8) * 8
        return jnp.pad(values, (0, rows * 128 - values.shape[0])).reshape(rows, 128)

    record = jnp.stack(
        [
            coarse_diag,
            face_sums[0] * inside[0],
            face_sums[2] * inside[2],
            face_sums[4],
            jnp.sum(forcing, axis=(1, 2)),
        ]
    )
    brick_here = (peer_ids == brick_index).astype(jnp.float32)
    spread = (brick_here[:, None, None, None] * slab_slot(record)[None]).reshape(-1)
    forcing_xy, forcing_z = side_faces(forcing)
    diagonal_xy, diagonal_z = side_faces(diagonal)
    summed, xy_land, z_land = exchange(
        as_tile(spread),
        jnp.concatenate([forcing_xy, diagonal_xy]),
        jnp.concatenate([forcing_z, diagonal_z]),
        2,
    )
    summed = summed.reshape(-1)[: spread.shape[0]]
    xy_rows = forcing_xy.shape[0]
    z_rows = forcing_z.shape[0]
    residual_halo = halo(forcing, xy_land[:, :xy_rows], z_land[:, :z_rows], 0.0)
    diagonal_halo = halo(diagonal, xy_land[:, xy_rows:], z_land[:, z_rows:], 1.0)
    gathered = lax.dynamic_index_in_dim(
        summed.reshape(brick_count, grp_count, 5, slot_count), brick_index, keepdims=False
    )
    columns = jnp.transpose(gathered, (1, 0, 2)).reshape(5, -1)
    matrix = assemble(columns[0], (columns[1], columns[2], columns[3]), (PATCH_Y, 1, slot_count))
    factor = jnp.linalg.cholesky(matrix)

    def coarse_solve(terms):
        middle = lax.linalg.triangular_solve(factor, terms[:, None], left_side=True, lower=True)
        result = lax.linalg.triangular_solve(
            factor, middle, left_side=True, lower=True, transpose_a=True
        )
        return lax.dynamic_slice_in_dim(result[:, 0], slab_index * slot_count, slot_count)

    def round_trip(field, field_halo, coef, smooth, with_faces=True):
        out, total, xy_land, z_land, dot = one_round(
            field, bonds, masks, diagonal, *field_halo, coef, smooth, with_faces
        )
        total = total.reshape(-1)
        out_halo = halo(out, xy_land, z_land, 0.0) if with_faces else None
        if smooth:
            return out, dot[0], None, out_halo
        count = brick_count * grp_count * slot_count
        mine = lax.dynamic_index_in_dim(
            total[1 : 1 + count].reshape(brick_count, -1), brick_index, keepdims=False
        )
        return out, dot[0], mine, out_halo

    def precondition(residual_field, field_halo, terms):
        smoothed_halo = [OMEGA * part / scale for part, scale in zip(field_halo, diagonal_halo)]
        return round_trip(residual_field, smoothed_halo, coarse_solve(terms), True)

    no_coarse = jnp.zeros((slot_count,), jnp.float32)
    terms = columns[4]
    solution_field = jnp.zeros_like(forcing)
    residual = forcing
    search, energy, _, search_halo = precondition(residual, residual_halo, terms)
    for iteration in range(ITERS):
        mapped, curvature, mapped_terms, mapped_halo = round_trip(
            search, search_halo, no_coarse, False, iteration + 1 < ITERS
        )
        step_size = energy / curvature
        solution_field = solution_field + step_size * search
        residual = residual - step_size * mapped
        if iteration + 1 < ITERS:
            residual_halo = [
                part - step_size * change for part, change in zip(residual_halo, mapped_halo)
            ]
            terms = terms - step_size * mapped_terms
            smoothed, renewed, _, smoothed_halo = precondition(residual, residual_halo, terms)
            search = smoothed + renewed / energy * search
            search_halo = [
                part + renewed / energy * old for part, old in zip(smoothed_halo, search_halo)
            ]
            energy = renewed
    return (solution_field[None, None], residual[None, None])


def solution(mesh):
    return jax.shard_map(
        on_device,
        mesh=mesh,
        in_specs=(
            P("grp", "brick", None, None, None),
            P("grp", "brick", None, None, None),
            P("grp", "brick", None, None, None, None),
            P(),
            P(),
        ),
        out_specs=(P("grp", "brick", None, None, None), P("grp", "brick", None, None, None)),
        check_vma=False,
    )
```

```python
import functools

import jax
import jax.numpy as jnp
from jax import lax
from jax.experimental import pallas as pl
from jax.experimental.pallas import tpu as pltpu
from jax.sharding import PartitionSpec as P

MESH_IDS = pl.DeviceIdType.MESH

BS = 32
PATCH_X = 1
PATCH_Y = 2
ITERS = 3


OMEGA = 0.6


def share(
    x_ref, xy_ref, z_ref, o_ref, xy_out, z_out, landed_b, landed_g, landed_xy, landed_z,
    send_b, recv_b, send_g, recv_g, send_xy, recv_xy, send_z, recv_z, brick_peers, grp_peers,
    dot_ref=None, with_faces=True,
):
    here_brick = lax.axis_index("brick")
    here_grp = lax.axis_index("grp")
    n_brick = landed_b.shape[0]
    n_grp = landed_g.shape[0]

    def send(src, dst, sends, recvs, index, peer):
        copy = pltpu.make_async_remote_copy(
            src_ref=src,
            dst_ref=dst.at[index],
            send_sem=sends.at[index],
            recv_sem=recvs.at[index],
            device_id=peer,
            device_id_type=MESH_IDS,
        )
        copy.start()
        return copy

    face_copies = []
    if with_faces:
        face_copies = [
            send(z_ref, landed_z, send_z, recv_z, 0, grp_peers[0]),
            send(z_ref, landed_z, send_z, recv_z, 1, grp_peers[-1]),
        ]
        face_copies += [
            send(xy_ref, landed_xy, send_xy, recv_xy, k, peer)
            for k, peer in enumerate(brick_peers, start=1)
        ]
    copies = [
        send(x_ref, landed_b, send_b, recv_b, k, peer)
        for k, peer in enumerate(brick_peers, start=1)
    ]
    landed_b[0] = x_ref[...]
    for copy in copies:
        copy.wait()
    total = landed_b[lax.rem(here_brick, n_brick)]
    for j in range(1, n_brick):
        total = total + landed_b[lax.rem(here_brick + n_brick - j, n_brick)]
    o_ref[...] = total
    landed_g[0] = total
    copies = [
        send(o_ref, landed_g, send_g, recv_g, k, peer)
        for k, peer in enumerate(grp_peers, start=1)
    ]
    for copy in copies:
        copy.wait()
    total = landed_g[lax.rem(here_grp, n_grp)]
    for j in range(1, n_grp):
        total = total + landed_g[lax.rem(here_grp + n_grp - j, n_grp)]
    o_ref[...] = total
    for copy in face_copies:
        copy.wait()
    if with_faces:
        landed_xy[0] = xy_ref[...]
        for k in range(landed_xy.shape[0]):
            xy_out[:, k, :] = landed_xy[k]
        z_out[...] = landed_z[...]
    else:
        xy_out[...] = jnp.zeros(xy_out.shape, jnp.float32)
        z_out[...] = jnp.zeros(z_out.shape, jnp.float32)
    if dot_ref is not None:
        tile_rows, tile_lanes = o_ref.shape
        first = lax.broadcasted_iota(jnp.int32, (tile_rows, tile_lanes), 0) * tile_lanes
        first = first + lax.broadcasted_iota(jnp.int32, (tile_rows, tile_lanes), 1)
        dot_ref[0] = jnp.sum(jnp.where(first == 0, total, 0.0))


def exchange_kernel(
    x_ref, xy_ref, z_ref, o_ref, xy_out, z_out,
    landed_b, landed_g, landed_xy, landed_z,
    send_b, recv_b, send_g, recv_g, send_xy, recv_xy, send_z, recv_z,
):
    here_brick = lax.axis_index("brick")
    here_grp = lax.axis_index("grp")
    n_brick = landed_b.shape[0]
    n_grp = landed_g.shape[0]
    brick_peers = [(lax.rem(here_brick + k, n_brick), here_grp) for k in range(1, n_brick)]
    grp_peers = [(here_brick, lax.rem(here_grp + k, n_grp)) for k in range(1, n_grp)]
    barrier = pltpu.get_barrier_semaphore()
    for peer in brick_peers + grp_peers:
        pl.semaphore_signal(barrier, inc=1, device_id=peer, device_id_type=MESH_IDS)
    pl.semaphore_wait(barrier, len(brick_peers) + len(grp_peers))

    share(
        x_ref, xy_ref, z_ref, o_ref, xy_out, z_out, landed_b, landed_g, landed_xy, landed_z,
        send_b, recv_b, send_g, recv_g, send_xy, recv_xy, send_z, recv_z, brick_peers, grp_peers,
    )


def exchange(tile, xy, z, kernel_id):
    n_brick = lax.axis_size("brick")
    n_grp = lax.axis_size("grp")
    vmem = pl.BlockSpec(memory_space=pltpu.VMEM)
    dma = pltpu.SemaphoreType.DMA
    return pl.pallas_call(
        exchange_kernel,
        out_shape=(
            jax.ShapeDtypeStruct(tile.shape, jnp.float32),
            jax.ShapeDtypeStruct((xy.shape[0], n_brick, xy.shape[1]), jnp.float32),
            jax.ShapeDtypeStruct((2,) + z.shape, jnp.float32),
        ),
        in_specs=[vmem] * 3,
        out_specs=(vmem, vmem, vmem),
        scratch_shapes=[
            pltpu.VMEM((n_brick,) + tile.shape, jnp.float32),
            pltpu.VMEM((n_grp,) + tile.shape, jnp.float32),
            pltpu.VMEM((n_brick,) + xy.shape, jnp.float32),
            pltpu.VMEM((2,) + z.shape, jnp.float32),
            dma((n_brick,)),
            dma((n_brick,)),
            dma((n_grp,)),
            dma((n_grp,)),
            dma((n_brick,)),
            dma((n_brick,)),
            dma((2,)),
            dma((2,)),
        ],
        compiler_params=pltpu.CompilerParams(collective_id=kernel_id, has_side_effects=True),
    )(tile, xy, z)


def stencil_body(
    coef_ref, f_ref, bonds_ref, masks_ref, diag_ref, rows_ref, faces_ref, o_ref, xy_ref, z_ref, smooth,
    with_faces=True,
):
    slots, width, lanes = f_ref.shape
    row = lax.broadcasted_iota(jnp.int32, (width, lanes), 0)
    lane = lax.broadcasted_iota(jnp.int32, (width, lanes), 1)
    pick = lax.broadcasted_iota(jnp.int32, (BS, lanes), 0)
    spot = lax.broadcasted_iota(jnp.int32, (BS, lanes), 1)
    spread_z = (spot // BS == pick).astype(jnp.float32)
    spread_y = (spot % BS == pick).astype(jnp.float32)

    def spread(face, table):
        high = face.astype(jnp.bfloat16)
        rest = face - high.astype(jnp.float32)
        middle = rest.astype(jnp.bfloat16)
        low = (rest - middle.astype(jnp.float32)).astype(jnp.bfloat16)
        table = table.astype(jnp.bfloat16)
        parts = [
            jnp.dot(part, table, preferred_element_type=jnp.float32) for part in (high, middle, low)
        ]
        return (parts[0] + parts[1]) + parts[2]

    borders = [
        row == width - 1,
        row == 0,
        lane >= lanes - BS,
        lane < BS,
        lane % BS == BS - 1,
        lane % BS == 0,
    ]
    source_lane = lax.broadcasted_iota(jnp.int32, (lanes, BS), 0)
    place = lax.broadcasted_iota(jnp.int32, (lanes, BS), 1)
    layers = [
        (source_lane == offset + step * place).astype(jnp.float32)
        for offset, step in ((0, 1), (lanes - BS, 1), (0, BS), (BS - 1, BS))
    ]
    flat_mask = spot // BS == pick

    def flatten(layer):
        spread_out = jnp.where(flat_mask, spread(layer, spread_y), 0.0)
        return jnp.sum(spread_out, axis=0, keepdims=True)

    dot = jnp.float32(0.0)
    sums = []
    for s in range(slots):
        ds = diag_ref[s]
        if smooth:
            rs = f_ref[s]
            fs = OMEGA * rs / ds
        else:
            fs = f_ref[s]
        xp = jnp.where(row == width - 1, rows_ref[0, s], pltpu.roll(fs, width - 1, 0))
        xm = jnp.where(row == 0, rows_ref[1, s], pltpu.roll(fs, 1, 0))
        yp = jnp.where(lane >= lanes - BS, spread(faces_ref[0, s], spread_y), pltpu.roll(fs, lanes - BS, 1))
        ym = jnp.where(lane < BS, spread(faces_ref[1, s], spread_y), pltpu.roll(fs, BS, 1))
        zp = jnp.where(lane % BS == BS - 1, spread(faces_ref[2, s], spread_z), pltpu.roll(fs, lanes - 1, 1))
        zm = jnp.where(lane % BS == 0, spread(faces_ref[3, s], spread_z), pltpu.roll(fs, 1, 1))
        total = ds * fs
        for d, beyond in enumerate([xp, xm, yp, ym, zp, zm]):
            base = 2 * (d * slots + s)
            active = jnp.where(borders[d], masks_ref[base + 1], masks_ref[base])
            total = total - bonds_ref[d, s] * active * beyond
        if smooth:
            total = fs + OMEGA * (rs - total) / ds
            total = total + coef_ref[s]
            dot = dot + jnp.sum(rs * total)
        else:
            dot = dot + jnp.sum(fs * total)
            sums.append(jnp.sum(total))
        o_ref[s] = total
        if not with_faces:
            continue
        xy_ref[pl.ds(s, 1), :] = total[0:1, :]
        xy_ref[pl.ds(slots + s, 1), :] = total[width - 1 : width, :]
        if s == 0:
            xy_ref[pl.ds(2 * slots, 1), :] = flatten(spread(total, layers[0]))
        if s == slots - 1:
            xy_ref[pl.ds(2 * slots + 1, 1), :] = flatten(spread(total, layers[1]))
        z_ref[pl.ds(s, 1), :] = flatten(spread(total, layers[2]))
        z_ref[pl.ds(slots + s, 1), :] = flatten(spread(total, layers[3]))
    return dot, sums


def round_kernel(
    coef_ref, f_ref, bonds_ref, masks_ref, diag_ref, rows_ref, faces_ref,
    o_ref, total_ref, xy_out, z_out, dot_ref,
    xy_buf, z_buf, tile_buf, landed_b, landed_g, landed_xy, landed_z,
    send_b, recv_b, send_g, recv_g, send_xy, recv_xy, send_z, recv_z, *, smooth, with_faces
):
    here_brick = lax.axis_index("brick")
    here_grp = lax.axis_index("grp")
    n_brick = landed_b.shape[0]
    n_grp = landed_g.shape[0]
    brick_peers = [(lax.rem(here_brick + k, n_brick), here_grp) for k in range(1, n_brick)]
    grp_peers = [(here_brick, lax.rem(here_grp + k, n_grp)) for k in range(1, n_grp)]
    barrier = pltpu.get_barrier_semaphore()
    for peer in brick_peers + grp_peers:
        pl.semaphore_signal(barrier, inc=1, device_id=peer, device_id_type=MESH_IDS)
    dot, sums = stencil_body(
        coef_ref, f_ref, bonds_ref, masks_ref, diag_ref, rows_ref, faces_ref, o_ref, xy_buf, z_buf,
        smooth, with_faces,
    )
    tile_rows, tile_lanes = tile_buf.shape
    flat = lax.broadcasted_iota(jnp.int32, (tile_rows, tile_lanes), 0) * tile_lanes
    flat = flat + lax.broadcasted_iota(jnp.int32, (tile_rows, tile_lanes), 1)
    tile = jnp.where(flat == 0, dot, 0.0)
    slots = f_ref.shape[0]
    for s, value in enumerate(sums):
        position = 1 + (here_brick * n_grp + here_grp) * slots + s
        tile = jnp.where(flat == position, value, tile)
    tile_buf[...] = tile
    pl.semaphore_wait(barrier, len(brick_peers) + len(grp_peers))
    share(
        tile_buf, xy_buf, z_buf, total_ref, xy_out, z_out, landed_b, landed_g, landed_xy, landed_z,
        send_b, recv_b, send_g, recv_g, send_xy, recv_xy, send_z, recv_z, brick_peers, grp_peers,
        dot_ref=dot_ref, with_faces=with_faces,
    )


def one_round(field, bonds, masks, diag, rows, faces, coef, smooth, with_faces=True):
    slots, _, lanes = field.shape
    n_brick = lax.axis_size("brick")
    n_grp = lax.axis_size("grp")
    tile = (8, 128)
    xy = (2 * slots + 2, lanes)
    z = (2 * slots, lanes)
    vmem = pl.BlockSpec(memory_space=pltpu.VMEM)
    smem = pl.BlockSpec(memory_space=pltpu.SMEM)
    dma = pltpu.SemaphoreType.DMA
    return pl.pallas_call(
        functools.partial(round_kernel, smooth=smooth, with_faces=with_faces),
        out_shape=(
            jax.ShapeDtypeStruct(field.shape, jnp.float32),
            jax.ShapeDtypeStruct(tile, jnp.float32),
            jax.ShapeDtypeStruct((xy[0], n_brick, xy[1]), jnp.float32),
            jax.ShapeDtypeStruct((2,) + z, jnp.float32),
            jax.ShapeDtypeStruct((1,), jnp.float32),
        ),
        in_specs=[smem, vmem, vmem, smem, vmem, vmem, vmem],
        out_specs=(vmem, vmem, vmem, vmem, smem),
        scratch_shapes=[
            pltpu.VMEM(xy, jnp.float32),
            pltpu.VMEM(z, jnp.float32),
            pltpu.VMEM(tile, jnp.float32),
            pltpu.VMEM((n_brick,) + tile, jnp.float32),
            pltpu.VMEM((n_grp,) + tile, jnp.float32),
            pltpu.VMEM((n_brick,) + xy, jnp.float32),
            pltpu.VMEM((2,) + z, jnp.float32),
            dma((n_brick,)),
            dma((n_brick,)),
            dma((n_grp,)),
            dma((n_grp,)),
            dma((n_brick,)),
            dma((n_brick,)),
            dma((2,)),
            dma((2,)),
        ],
        compiler_params=pltpu.CompilerParams(
            collective_id=(3 if smooth else 1) if with_faces else 4, has_side_effects=True
        ),
    )(coef, field, bonds, masks, diag, rows, faces)


def assemble(coarse_diag, couplings, strides):
    extent = coarse_diag.shape[0]
    matrix = jnp.diag(coarse_diag)
    for coupling, stride in zip(couplings, strides):
        banded = coupling[: extent - stride]
        matrix = matrix - jnp.diag(banded, stride) - jnp.diag(banded, -stride)
    return matrix


def on_device(source, uptake, conductance, occupancy, assignment):
    face_size = BS * BS
    slot_count = PATCH_X * PATCH_Y
    slab_index = lax.axis_index("grp")
    brick_index = lax.axis_index("brick")
    brick_count = lax.axis_size("brick")
    across = brick_count // 2
    peer_ids = jnp.arange(brick_count, dtype=jnp.int32)
    patch_index = assignment[brick_index]
    patch_row = patch_index // across
    patch_column = patch_index % across

    def owner_of(row_shift, column_shift):
        row_target = patch_row + row_shift
        column_target = patch_column + column_shift
        inside = (
            (row_target >= 0) & (row_target < 2) & (column_target >= 0) & (column_target < across)
        )
        holder = jnp.sum(jnp.where(assignment == row_target * across + column_target, peer_ids, 0))
        return jnp.where(inside, holder, -1)

    wanted = jnp.stack([owner_of(1, 0), owner_of(-1, 0), owner_of(0, 1), owner_of(0, -1)])
    padded = jnp.pad(occupancy, 1)
    window = lax.dynamic_slice(
        padded,
        (slab_index, patch_row * PATCH_X, patch_column * PATCH_Y),
        (3, PATCH_X + 2, PATCH_Y + 2),
    ).astype(jnp.float32)
    centre = window[1, 1:-1, 1:-1].reshape(slot_count)
    toward = [
        window[1, 2:, 1:-1],
        window[1, :-2, 1:-1],
        window[1, 1:-1, 2:],
        window[1, 1:-1, :-2],
        window[2, 1:-1, 1:-1],
        window[0, 1:-1, 1:-1],
    ]
    first_axis = lax.broadcasted_iota(jnp.int32, (1, BS, face_size), 1)
    flat_axis = lax.broadcasted_iota(jnp.int32, (1, BS, face_size), 2)
    second_axis = flat_axis // BS
    third_axis = flat_axis % BS
    cube_third = lax.broadcasted_iota(jnp.int32, (1, BS, BS, BS), 3)
    borders = [
        first_axis == BS - 1,
        first_axis == 0,
        second_axis == BS - 1,
        second_axis == 0,
        third_axis == BS - 1,
        third_axis == 0,
    ]
    bonds = conductance[0, 0]
    live_here = centre[:, None, None]
    effective = []
    for direction in range(6):
        neighbour_live = toward[direction].reshape(slot_count)[:, None, None]
        active = jnp.where(borders[direction], live_here * neighbour_live, live_here)
        effective.append(bonds[direction] * active)
    absorb = uptake[0, 0]
    diagonal = absorb
    for direction in range(6):
        diagonal = diagonal + effective[direction]

    masks = jnp.stack(
        [
            jnp.stack([centre, centre * toward[direction].reshape(slot_count)], axis=1)
            for direction in range(6)
        ]
    ).reshape(-1)

    lane_ids = jnp.arange(face_size, dtype=jnp.int32)[:, None]
    layer_ids = BS * jnp.arange(BS, dtype=jnp.int32)[None, :]
    picker = jnp.concatenate([lane_ids == layer_ids, lane_ids == layer_ids + BS - 1], axis=1)
    picker = picker.astype(jnp.float32)

    def side_faces(field):
        picked = jnp.dot(
            field.reshape(slot_count * BS, face_size), picker, precision=lax.Precision.HIGHEST
        )
        z = picked.reshape(slot_count, BS, 2, BS).transpose(2, 0, 1, 3)
        xy = jnp.concatenate(
            [
                field[:, 0, :],
                field[:, BS - 1, :],
                field[0, :, :BS].reshape(1, face_size),
                field[slot_count - 1, :, face_size - BS :].reshape(1, face_size),
            ]
        )
        return xy, z.reshape(2 * slot_count, face_size)

    def pick(landed, holder, fill):
        offset = lax.rem(brick_index - holder + brick_count, brick_count)
        got = lax.dynamic_index_in_dim(landed, offset, axis=1, keepdims=False)
        return jnp.where(holder >= 0, got, fill)

    def halo(field, xy_land, z_land, fill):
        xplus = pick(xy_land, wanted[0], fill)
        xminus = pick(xy_land, wanted[1], fill)
        yplus = pick(xy_land, wanted[2], fill)
        yminus = pick(xy_land, wanted[3], fill)
        rows = jnp.stack([xplus[:slot_count], xminus[slot_count : 2 * slot_count]])[:, :, None, :]
        beyond_yplus = jnp.stack([field[1, :, :BS], yplus[2 * slot_count].reshape(BS, BS)])
        beyond_yminus = jnp.stack(
            [yminus[2 * slot_count + 1].reshape(BS, BS), field[0, :, face_size - BS :]]
        )
        above = jnp.where(slab_index < grp_count - 1, z_land[1, :slot_count], fill)
        below = jnp.where(slab_index > 0, z_land[0, slot_count:], fill)
        faces = jnp.stack(
            [
                beyond_yplus,
                beyond_yminus,
                above.reshape(slot_count, BS, BS),
                below.reshape(slot_count, BS, BS),
            ]
        )
        return rows, faces

    slot_ids = jnp.arange(slot_count)
    brick_first = slot_ids // PATCH_Y
    brick_second = slot_ids % PATCH_Y
    inside = [
        (brick_first < PATCH_X - 1).astype(jnp.float32),
        (brick_first > 0).astype(jnp.float32),
        (brick_second < PATCH_Y - 1).astype(jnp.float32),
        (brick_second > 0).astype(jnp.float32),
    ]
    face_sums = [
        jnp.sum(effective[0][:, BS - 1, :], axis=1),
        jnp.sum(effective[1][:, 0, :], axis=1),
        jnp.sum(effective[2][:, :, face_size - BS :], axis=(1, 2)),
        jnp.sum(effective[3][:, :, :BS], axis=(1, 2)),
        jnp.sum(jnp.where(borders[4], effective[4], 0.0), axis=(1, 2)),
        jnp.sum(jnp.where(borders[5], effective[5], 0.0), axis=(1, 2)),
    ]
    coarse_diag = jnp.sum(absorb, axis=(1, 2))
    for direction in range(4):
        coarse_diag = coarse_diag + face_sums[direction] * inside[direction]
    coarse_diag = coarse_diag + face_sums[4] + face_sums[5]
    grp_count = lax.axis_size("grp")
    grp_ids = jnp.arange(grp_count, dtype=jnp.int32)

    def slab_slot(values):
        here = (grp_ids == slab_index).astype(jnp.float32)
        return here[:, None, None] * values[None]

    forcing = source[0, 0] * live_here

    def as_tile(values):
        rows = -(-values.shape[0] // 128)
        rows = -(-rows // 8) * 8
        return jnp.pad(values, (0, rows * 128 - values.shape[0])).reshape(rows, 128)

    record = jnp.stack(
        [
            coarse_diag,
            face_sums[0] * inside[0],
            face_sums[2] * inside[2],
            face_sums[4],
            jnp.sum(forcing, axis=(1, 2)),
        ]
    )
    brick_here = (peer_ids == brick_index).astype(jnp.float32)
    spread = (brick_here[:, None, None, None] * slab_slot(record)[None]).reshape(-1)
    forcing_xy, forcing_z = side_faces(forcing)
    diagonal_xy, diagonal_z = side_faces(diagonal)
    summed, xy_land, z_land = exchange(
        as_tile(spread),
        jnp.concatenate([forcing_xy, diagonal_xy]),
        jnp.concatenate([forcing_z, diagonal_z]),
        2,
    )
    summed = summed.reshape(-1)[: spread.shape[0]]
    xy_rows = forcing_xy.shape[0]
    z_rows = forcing_z.shape[0]
    residual_halo = halo(forcing, xy_land[:xy_rows], z_land[:, :z_rows], 0.0)
    diagonal_halo = halo(diagonal, xy_land[xy_rows:], z_land[:, z_rows:], 1.0)
    gathered = lax.dynamic_index_in_dim(
        summed.reshape(brick_count, grp_count, 5, slot_count), brick_index, keepdims=False
    )
    columns = jnp.transpose(gathered, (1, 0, 2)).reshape(5, -1)
    matrix = assemble(columns[0], (columns[1], columns[2], columns[3]), (PATCH_Y, 1, slot_count))
    factor = jnp.linalg.cholesky(matrix)

    def coarse_solve(terms):
        middle = lax.linalg.triangular_solve(factor, terms[:, None], left_side=True, lower=True)
        result = lax.linalg.triangular_solve(
            factor, middle, left_side=True, lower=True, transpose_a=True
        )
        return lax.dynamic_slice_in_dim(result[:, 0], slab_index * slot_count, slot_count)

    def round_trip(field, field_halo, coef, smooth, with_faces=True):
        out, total, xy_land, z_land, dot = one_round(
            field, bonds, masks, diagonal, *field_halo, coef, smooth, with_faces
        )
        total = total.reshape(-1)
        out_halo = halo(out, xy_land, z_land, 0.0) if with_faces else None
        if smooth:
            return out, dot[0], None, out_halo
        count = brick_count * grp_count * slot_count
        mine = lax.dynamic_index_in_dim(
            total[1 : 1 + count].reshape(brick_count, -1), brick_index, keepdims=False
        )
        return out, dot[0], mine, out_halo

    def precondition(residual_field, field_halo, terms):
        smoothed_halo = [OMEGA * part / scale for part, scale in zip(field_halo, diagonal_halo)]
        return round_trip(residual_field, smoothed_halo, coarse_solve(terms), True)

    no_coarse = jnp.zeros((slot_count,), jnp.float32)
    terms = columns[4]
    solution_field = jnp.zeros_like(forcing)
    residual = forcing
    search, energy, _, search_halo = precondition(residual, residual_halo, terms)
    for iteration in range(ITERS):
        mapped, curvature, mapped_terms, mapped_halo = round_trip(
            search, search_halo, no_coarse, False, iteration + 1 < ITERS
        )
        step_size = energy / curvature
        solution_field = solution_field + step_size * search
        residual = residual - step_size * mapped
        if iteration + 1 < ITERS:
            residual_halo = [
                part - step_size * change for part, change in zip(residual_halo, mapped_halo)
            ]
            terms = terms - step_size * mapped_terms
            smoothed, renewed, _, smoothed_halo = precondition(residual, residual_halo, terms)
            search = smoothed + renewed / energy * search
            search_halo = [
                part + renewed / energy * old for part, old in zip(smoothed_halo, search_halo)
            ]
            energy = renewed
    return (solution_field[None, None], residual[None, None])


def solution(mesh):
    return jax.shard_map(
        on_device,
        mesh=mesh,
        in_specs=(
            P("grp", "brick", None, None, None),
            P("grp", "brick", None, None, None),
            P("grp", "brick", None, None, None, None),
            P(),
            P(),
        ),
        out_specs=(P("grp", "brick", None, None, None), P("grp", "brick", None, None, None)),
        check_vma=False,
    )
```

```python
import functools

import jax
import jax.numpy as jnp
from jax import lax
from jax.experimental import pallas as pl
from jax.experimental.pallas import tpu as pltpu
from jax.sharding import PartitionSpec as P

MESH_IDS = pl.DeviceIdType.MESH

BS = 32
PATCH_X = 1
PATCH_Y = 2
ITERS = 3


OMEGA = 0.6


def share(
    x_ref, xy_ref, z_ref, o_ref, xy_out, z_out, landed_b, landed_g, landed_xy, landed_z,
    send_b, recv_b, send_g, recv_g, send_xy, recv_xy, send_z, recv_z, brick_peers, grp_peers,
    dot_ref=None, with_faces=True,
):
    here_brick = lax.axis_index("brick")
    here_grp = lax.axis_index("grp")
    n_brick = landed_b.shape[0]
    n_grp = landed_g.shape[0]

    def send(src, dst, sends, recvs, index, peer):
        copy = pltpu.make_async_remote_copy(
            src_ref=src,
            dst_ref=dst.at[index],
            send_sem=sends.at[index],
            recv_sem=recvs.at[index],
            device_id=peer,
            device_id_type=MESH_IDS,
        )
        copy.start()
        return copy

    face_copies = []
    if with_faces:
        face_copies = [
            send(z_ref, landed_z, send_z, recv_z, 0, grp_peers[0]),
            send(z_ref, landed_z, send_z, recv_z, 1, grp_peers[-1]),
        ]
        face_copies += [
            send(xy_ref, landed_xy, send_xy, recv_xy, k, peer)
            for k, peer in enumerate(brick_peers, start=1)
        ]
    copies = [
        send(x_ref, landed_b, send_b, recv_b, k, peer)
        for k, peer in enumerate(brick_peers, start=1)
    ]
    landed_b[0] = x_ref[...]
    for copy in copies:
        copy.wait()
    total = landed_b[lax.rem(here_brick, n_brick)]
    for j in range(1, n_brick):
        total = total + landed_b[lax.rem(here_brick + n_brick - j, n_brick)]
    o_ref[...] = total
    landed_g[0] = total
    copies = [
        send(o_ref, landed_g, send_g, recv_g, k, peer)
        for k, peer in enumerate(grp_peers, start=1)
    ]
    for copy in copies:
        copy.wait()
    total = landed_g[lax.rem(here_grp, n_grp)]
    for j in range(1, n_grp):
        total = total + landed_g[lax.rem(here_grp + n_grp - j, n_grp)]
    o_ref[...] = total
    for copy in face_copies:
        copy.wait()
    if with_faces:
        landed_xy[0] = xy_ref[...]
        xy_out[...] = landed_xy[...]
        z_out[...] = landed_z[...]
    else:
        xy_out[...] = jnp.zeros(xy_out.shape, jnp.float32)
        z_out[...] = jnp.zeros(z_out.shape, jnp.float32)
    if dot_ref is not None:
        tile_rows, tile_lanes = o_ref.shape
        first = lax.broadcasted_iota(jnp.int32, (tile_rows, tile_lanes), 0) * tile_lanes
        first = first + lax.broadcasted_iota(jnp.int32, (tile_rows, tile_lanes), 1)
        dot_ref[0] = jnp.sum(jnp.where(first == 0, total, 0.0))


def setup_faces(f_ref, xy_ref, z_ref, xy_base, z_base):
    slots, width, lanes = f_ref.shape
    pick = lax.broadcasted_iota(jnp.int32, (BS, lanes), 0)
    spot = lax.broadcasted_iota(jnp.int32, (BS, lanes), 1)
    spread_y = (spot % BS == pick).astype(jnp.float32)
    flat_mask = spot // BS == pick
    source_lane = lax.broadcasted_iota(jnp.int32, (lanes, BS), 0)
    place = lax.broadcasted_iota(jnp.int32, (lanes, BS), 1)
    layers = [
        (source_lane == offset + step * place).astype(jnp.float32)
        for offset, step in ((0, 1), (lanes - BS, 1), (0, BS), (BS - 1, BS))
    ]

    def spread(face, table):
        high = face.astype(jnp.bfloat16)
        rest = face - high.astype(jnp.float32)
        middle = rest.astype(jnp.bfloat16)
        low = (rest - middle.astype(jnp.float32)).astype(jnp.bfloat16)
        table = table.astype(jnp.bfloat16)
        parts = [
            jnp.dot(part, table, preferred_element_type=jnp.float32) for part in (high, middle, low)
        ]
        return (parts[0] + parts[1]) + parts[2]

    def flatten(layer):
        return jnp.sum(jnp.where(flat_mask, spread(layer, spread_y), 0.0), axis=0, keepdims=True)

    for s in range(slots):
        total = f_ref[s]
        xy_ref[pl.ds(xy_base + s, 1), :] = total[0:1, :]
        xy_ref[pl.ds(xy_base + slots + s, 1), :] = total[width - 1 : width, :]
        if s == 0:
            xy_ref[pl.ds(xy_base + 2 * slots, 1), :] = flatten(spread(total, layers[0]))
        if s == slots - 1:
            xy_ref[pl.ds(xy_base + 2 * slots + 1, 1), :] = flatten(spread(total, layers[1]))
        z_ref[pl.ds(z_base + s, 1), :] = flatten(spread(total, layers[2]))
        z_ref[pl.ds(z_base + slots + s, 1), :] = flatten(spread(total, layers[3]))


def exchange_kernel(
    x_ref, forcing_ref, diag_ref, o_ref, xy_out, z_out,
    xy_ref, z_ref, landed_b, landed_g, landed_xy, landed_z,
    send_b, recv_b, send_g, recv_g, send_xy, recv_xy, send_z, recv_z,
):
    here_brick = lax.axis_index("brick")
    here_grp = lax.axis_index("grp")
    n_brick = landed_b.shape[0]
    n_grp = landed_g.shape[0]
    brick_peers = [(lax.rem(here_brick + k, n_brick), here_grp) for k in range(1, n_brick)]
    grp_peers = [(here_brick, lax.rem(here_grp + k, n_grp)) for k in range(1, n_grp)]
    barrier = pltpu.get_barrier_semaphore()
    for peer in brick_peers + grp_peers:
        pl.semaphore_signal(barrier, inc=1, device_id=peer, device_id_type=MESH_IDS)
    slots = forcing_ref.shape[0]
    setup_faces(forcing_ref, xy_ref, z_ref, 0, 0)
    setup_faces(diag_ref, xy_ref, z_ref, 2 * slots + 2, 2 * slots)
    pl.semaphore_wait(barrier, len(brick_peers) + len(grp_peers))

    share(
        x_ref, xy_ref, z_ref, o_ref, xy_out, z_out, landed_b, landed_g, landed_xy, landed_z,
        send_b, recv_b, send_g, recv_g, send_xy, recv_xy, send_z, recv_z, brick_peers, grp_peers,
    )


def exchange(tile, forcing, diag, kernel_id):
    slots, _, lanes = forcing.shape
    xy = jax.ShapeDtypeStruct((2 * (2 * slots + 2), lanes), jnp.float32)
    z = jax.ShapeDtypeStruct((2 * (2 * slots), lanes), jnp.float32)
    n_brick = lax.axis_size("brick")
    n_grp = lax.axis_size("grp")
    vmem = pl.BlockSpec(memory_space=pltpu.VMEM)
    dma = pltpu.SemaphoreType.DMA
    return pl.pallas_call(
        exchange_kernel,
        out_shape=(
            jax.ShapeDtypeStruct(tile.shape, jnp.float32),
            jax.ShapeDtypeStruct((n_brick,) + xy.shape, jnp.float32),
            jax.ShapeDtypeStruct((2,) + z.shape, jnp.float32),
        ),
        in_specs=[vmem] * 3,
        out_specs=(vmem, vmem, vmem),
        scratch_shapes=[
            pltpu.VMEM(xy.shape, jnp.float32),
            pltpu.VMEM(z.shape, jnp.float32),
            pltpu.VMEM((n_brick,) + tile.shape, jnp.float32),
            pltpu.VMEM((n_grp,) + tile.shape, jnp.float32),
            pltpu.VMEM((n_brick,) + xy.shape, jnp.float32),
            pltpu.VMEM((2,) + z.shape, jnp.float32),
            dma((n_brick,)),
            dma((n_brick,)),
            dma((n_grp,)),
            dma((n_grp,)),
            dma((n_brick,)),
            dma((n_brick,)),
            dma((2,)),
            dma((2,)),
        ],
        compiler_params=pltpu.CompilerParams(collective_id=kernel_id, has_side_effects=True),
    )(tile, forcing, diag)


def stencil_body(
    coef_ref, f_ref, bonds_ref, masks_ref, diag_ref, rows_ref, faces_ref, o_ref, xy_ref, z_ref, smooth,
    with_faces=True,
):
    slots, width, lanes = f_ref.shape
    row = lax.broadcasted_iota(jnp.int32, (width, lanes), 0)
    lane = lax.broadcasted_iota(jnp.int32, (width, lanes), 1)
    pick = lax.broadcasted_iota(jnp.int32, (BS, lanes), 0)
    spot = lax.broadcasted_iota(jnp.int32, (BS, lanes), 1)
    spread_z = (spot // BS == pick).astype(jnp.float32)
    spread_y = (spot % BS == pick).astype(jnp.float32)

    def spread(face, table):
        high = face.astype(jnp.bfloat16)
        rest = face - high.astype(jnp.float32)
        middle = rest.astype(jnp.bfloat16)
        low = (rest - middle.astype(jnp.float32)).astype(jnp.bfloat16)
        table = table.astype(jnp.bfloat16)
        parts = [
            jnp.dot(part, table, preferred_element_type=jnp.float32) for part in (high, middle, low)
        ]
        return (parts[0] + parts[1]) + parts[2]

    borders = [
        row == width - 1,
        row == 0,
        lane >= lanes - BS,
        lane < BS,
        lane % BS == BS - 1,
        lane % BS == 0,
    ]
    source_lane = lax.broadcasted_iota(jnp.int32, (lanes, BS), 0)
    place = lax.broadcasted_iota(jnp.int32, (lanes, BS), 1)
    layers = [
        (source_lane == offset + step * place).astype(jnp.float32)
        for offset, step in ((0, 1), (lanes - BS, 1), (0, BS), (BS - 1, BS))
    ]
    flat_mask = spot // BS == pick

    def flatten(layer):
        spread_out = jnp.where(flat_mask, spread(layer, spread_y), 0.0)
        return jnp.sum(spread_out, axis=0, keepdims=True)

    dot = jnp.float32(0.0)
    sums = []
    for s in range(slots):
        ds = diag_ref[s]
        if smooth:
            rs = f_ref[s]
            fs = OMEGA * rs / ds
        else:
            fs = f_ref[s]
        xp = jnp.where(row == width - 1, rows_ref[0, s], pltpu.roll(fs, width - 1, 0))
        xm = jnp.where(row == 0, rows_ref[1, s], pltpu.roll(fs, 1, 0))
        yp = jnp.where(lane >= lanes - BS, spread(faces_ref[0, s], spread_y), pltpu.roll(fs, lanes - BS, 1))
        ym = jnp.where(lane < BS, spread(faces_ref[1, s], spread_y), pltpu.roll(fs, BS, 1))
        zp = jnp.where(lane % BS == BS - 1, spread(faces_ref[2, s], spread_z), pltpu.roll(fs, lanes - 1, 1))
        zm = jnp.where(lane % BS == 0, spread(faces_ref[3, s], spread_z), pltpu.roll(fs, 1, 1))
        total = ds * fs
        for d, beyond in enumerate([xp, xm, yp, ym, zp, zm]):
            base = 2 * (d * slots + s)
            active = jnp.where(borders[d], masks_ref[base + 1], masks_ref[base])
            total = total - bonds_ref[d, s] * active * beyond
        if smooth:
            total = fs + OMEGA * (rs - total) / ds
            total = total + coef_ref[s]
            dot = dot + jnp.sum(rs * total)
        else:
            dot = dot + jnp.sum(fs * total)
            sums.append(jnp.sum(total))
        o_ref[s] = total
        if not with_faces:
            continue
        xy_ref[pl.ds(s, 1), :] = total[0:1, :]
        xy_ref[pl.ds(slots + s, 1), :] = total[width - 1 : width, :]
        if s == 0:
            xy_ref[pl.ds(2 * slots, 1), :] = flatten(spread(total, layers[0]))
        if s == slots - 1:
            xy_ref[pl.ds(2 * slots + 1, 1), :] = flatten(spread(total, layers[1]))
        z_ref[pl.ds(s, 1), :] = flatten(spread(total, layers[2]))
        z_ref[pl.ds(slots + s, 1), :] = flatten(spread(total, layers[3]))
    return dot, sums


def round_kernel(
    coef_ref, f_ref, bonds_ref, masks_ref, diag_ref, rows_ref, faces_ref,
    o_ref, total_ref, xy_out, z_out, dot_ref,
    xy_buf, z_buf, tile_buf, landed_b, landed_g, landed_xy, landed_z,
    send_b, recv_b, send_g, recv_g, send_xy, recv_xy, send_z, recv_z, *, smooth, with_faces
):
    here_brick = lax.axis_index("brick")
    here_grp = lax.axis_index("grp")
    n_brick = landed_b.shape[0]
    n_grp = landed_g.shape[0]
    brick_peers = [(lax.rem(here_brick + k, n_brick), here_grp) for k in range(1, n_brick)]
    grp_peers = [(here_brick, lax.rem(here_grp + k, n_grp)) for k in range(1, n_grp)]
    barrier = pltpu.get_barrier_semaphore()
    for peer in brick_peers + grp_peers:
        pl.semaphore_signal(barrier, inc=1, device_id=peer, device_id_type=MESH_IDS)
    dot, sums = stencil_body(
        coef_ref, f_ref, bonds_ref, masks_ref, diag_ref, rows_ref, faces_ref, o_ref, xy_buf, z_buf,
        smooth, with_faces,
    )
    tile_rows, tile_lanes = tile_buf.shape
    flat = lax.broadcasted_iota(jnp.int32, (tile_rows, tile_lanes), 0) * tile_lanes
    flat = flat + lax.broadcasted_iota(jnp.int32, (tile_rows, tile_lanes), 1)
    tile = jnp.where(flat == 0, dot, 0.0)
    slots = f_ref.shape[0]
    for s, value in enumerate(sums):
        position = 1 + (here_brick * n_grp + here_grp) * slots + s
        tile = jnp.where(flat == position, value, tile)
    tile_buf[...] = tile
    pl.semaphore_wait(barrier, len(brick_peers) + len(grp_peers))
    share(
        tile_buf, xy_buf, z_buf, total_ref, xy_out, z_out, landed_b, landed_g, landed_xy, landed_z,
        send_b, recv_b, send_g, recv_g, send_xy, recv_xy, send_z, recv_z, brick_peers, grp_peers,
        dot_ref=dot_ref, with_faces=with_faces,
    )


def one_round(field, bonds, masks, diag, rows, faces, coef, smooth, with_faces=True):
    slots, _, lanes = field.shape
    n_brick = lax.axis_size("brick")
    n_grp = lax.axis_size("grp")
    tile = (8, 128)
    xy = (2 * slots + 2, lanes)
    z = (2 * slots, lanes)
    vmem = pl.BlockSpec(memory_space=pltpu.VMEM)
    smem = pl.BlockSpec(memory_space=pltpu.SMEM)
    dma = pltpu.SemaphoreType.DMA
    return pl.pallas_call(
        functools.partial(round_kernel, smooth=smooth, with_faces=with_faces),
        out_shape=(
            jax.ShapeDtypeStruct(field.shape, jnp.float32),
            jax.ShapeDtypeStruct(tile, jnp.float32),
            jax.ShapeDtypeStruct((n_brick,) + xy, jnp.float32),
            jax.ShapeDtypeStruct((2,) + z, jnp.float32),
            jax.ShapeDtypeStruct((1,), jnp.float32),
        ),
        in_specs=[smem, vmem, vmem, smem, vmem, vmem, vmem],
        out_specs=(vmem, vmem, vmem, vmem, smem),
        scratch_shapes=[
            pltpu.VMEM(xy, jnp.float32),
            pltpu.VMEM(z, jnp.float32),
            pltpu.VMEM(tile, jnp.float32),
            pltpu.VMEM((n_brick,) + tile, jnp.float32),
            pltpu.VMEM((n_grp,) + tile, jnp.float32),
            pltpu.VMEM((n_brick,) + xy, jnp.float32),
            pltpu.VMEM((2,) + z, jnp.float32),
            dma((n_brick,)),
            dma((n_brick,)),
            dma((n_grp,)),
            dma((n_grp,)),
            dma((n_brick,)),
            dma((n_brick,)),
            dma((2,)),
            dma((2,)),
        ],
        compiler_params=pltpu.CompilerParams(
            collective_id=(3 if smooth else 1) if with_faces else 4, has_side_effects=True
        ),
    )(coef, field, bonds, masks, diag, rows, faces)


def assemble(coarse_diag, couplings, strides):
    extent = coarse_diag.shape[0]
    matrix = jnp.diag(coarse_diag)
    for coupling, stride in zip(couplings, strides):
        banded = coupling[: extent - stride]
        matrix = matrix - jnp.diag(banded, stride) - jnp.diag(banded, -stride)
    return matrix


def on_device(source, uptake, conductance, occupancy, assignment):
    face_size = BS * BS
    slot_count = PATCH_X * PATCH_Y
    slab_index = lax.axis_index("grp")
    brick_index = lax.axis_index("brick")
    brick_count = lax.axis_size("brick")
    across = brick_count // 2
    peer_ids = jnp.arange(brick_count, dtype=jnp.int32)
    patch_index = assignment[brick_index]
    patch_row = patch_index // across
    patch_column = patch_index % across

    def owner_of(row_shift, column_shift):
        row_target = patch_row + row_shift
        column_target = patch_column + column_shift
        inside = (
            (row_target >= 0) & (row_target < 2) & (column_target >= 0) & (column_target < across)
        )
        holder = jnp.sum(jnp.where(assignment == row_target * across + column_target, peer_ids, 0))
        return jnp.where(inside, holder, -1)

    wanted = jnp.stack([owner_of(1, 0), owner_of(-1, 0), owner_of(0, 1), owner_of(0, -1)])
    padded = jnp.pad(occupancy, 1)
    window = lax.dynamic_slice(
        padded,
        (slab_index, patch_row * PATCH_X, patch_column * PATCH_Y),
        (3, PATCH_X + 2, PATCH_Y + 2),
    ).astype(jnp.float32)
    centre = window[1, 1:-1, 1:-1].reshape(slot_count)
    toward = [
        window[1, 2:, 1:-1],
        window[1, :-2, 1:-1],
        window[1, 1:-1, 2:],
        window[1, 1:-1, :-2],
        window[2, 1:-1, 1:-1],
        window[0, 1:-1, 1:-1],
    ]
    first_axis = lax.broadcasted_iota(jnp.int32, (1, BS, face_size), 1)
    flat_axis = lax.broadcasted_iota(jnp.int32, (1, BS, face_size), 2)
    second_axis = flat_axis // BS
    third_axis = flat_axis % BS
    cube_third = lax.broadcasted_iota(jnp.int32, (1, BS, BS, BS), 3)
    borders = [
        first_axis == BS - 1,
        first_axis == 0,
        second_axis == BS - 1,
        second_axis == 0,
        third_axis == BS - 1,
        third_axis == 0,
    ]
    bonds = conductance[0, 0]
    live_here = centre[:, None, None]
    effective = []
    for direction in range(6):
        neighbour_live = toward[direction].reshape(slot_count)[:, None, None]
        active = jnp.where(borders[direction], live_here * neighbour_live, live_here)
        effective.append(bonds[direction] * active)
    absorb = uptake[0, 0]
    diagonal = absorb
    for direction in range(6):
        diagonal = diagonal + effective[direction]

    masks = jnp.stack(
        [
            jnp.stack([centre, centre * toward[direction].reshape(slot_count)], axis=1)
            for direction in range(6)
        ]
    ).reshape(-1)

    lane_ids = jnp.arange(face_size, dtype=jnp.int32)[:, None]
    layer_ids = BS * jnp.arange(BS, dtype=jnp.int32)[None, :]
    picker = jnp.concatenate([lane_ids == layer_ids, lane_ids == layer_ids + BS - 1], axis=1)
    picker = picker.astype(jnp.float32)

    def side_faces(field):
        picked = jnp.dot(
            field.reshape(slot_count * BS, face_size), picker, precision=lax.Precision.HIGHEST
        )
        z = picked.reshape(slot_count, BS, 2, BS).transpose(2, 0, 1, 3)
        xy = jnp.concatenate(
            [
                field[:, 0, :],
                field[:, BS - 1, :],
                field[0, :, :BS].reshape(1, face_size),
                field[slot_count - 1, :, face_size - BS :].reshape(1, face_size),
            ]
        )
        return xy, z.reshape(2 * slot_count, face_size)

    def pick(landed, holder, fill):
        offset = lax.rem(brick_index - holder + brick_count, brick_count)
        got = lax.dynamic_index_in_dim(landed, offset, keepdims=False)
        return jnp.where(holder >= 0, got, fill)

    def halo(field, xy_land, z_land, fill):
        xplus = pick(xy_land, wanted[0], fill)
        xminus = pick(xy_land, wanted[1], fill)
        yplus = pick(xy_land, wanted[2], fill)
        yminus = pick(xy_land, wanted[3], fill)
        rows = jnp.stack([xplus[:slot_count], xminus[slot_count : 2 * slot_count]])[:, :, None, :]
        beyond_yplus = jnp.stack([field[1, :, :BS], yplus[2 * slot_count].reshape(BS, BS)])
        beyond_yminus = jnp.stack(
            [yminus[2 * slot_count + 1].reshape(BS, BS), field[0, :, face_size - BS :]]
        )
        above = jnp.where(slab_index < grp_count - 1, z_land[1, :slot_count], fill)
        below = jnp.where(slab_index > 0, z_land[0, slot_count:], fill)
        faces = jnp.stack(
            [
                beyond_yplus,
                beyond_yminus,
                above.reshape(slot_count, BS, BS),
                below.reshape(slot_count, BS, BS),
            ]
        )
        return rows, faces

    slot_ids = jnp.arange(slot_count)
    brick_first = slot_ids // PATCH_Y
    brick_second = slot_ids % PATCH_Y
    inside = [
        (brick_first < PATCH_X - 1).astype(jnp.float32),
        (brick_first > 0).astype(jnp.float32),
        (brick_second < PATCH_Y - 1).astype(jnp.float32),
        (brick_second > 0).astype(jnp.float32),
    ]
    face_sums = [
        jnp.sum(effective[0][:, BS - 1, :], axis=1),
        jnp.sum(effective[1][:, 0, :], axis=1),
        jnp.sum(effective[2][:, :, face_size - BS :], axis=(1, 2)),
        jnp.sum(effective[3][:, :, :BS], axis=(1, 2)),
        jnp.sum(jnp.where(borders[4], effective[4], 0.0), axis=(1, 2)),
        jnp.sum(jnp.where(borders[5], effective[5], 0.0), axis=(1, 2)),
    ]
    coarse_diag = jnp.sum(absorb, axis=(1, 2))
    for direction in range(4):
        coarse_diag = coarse_diag + face_sums[direction] * inside[direction]
    coarse_diag = coarse_diag + face_sums[4] + face_sums[5]
    grp_count = lax.axis_size("grp")
    grp_ids = jnp.arange(grp_count, dtype=jnp.int32)

    def slab_slot(values):
        here = (grp_ids == slab_index).astype(jnp.float32)
        return here[:, None, None] * values[None]

    forcing = source[0, 0] * live_here

    def as_tile(values):
        rows = -(-values.shape[0] // 128)
        rows = -(-rows // 8) * 8
        return jnp.pad(values, (0, rows * 128 - values.shape[0])).reshape(rows, 128)

    record = jnp.stack(
        [
            coarse_diag,
            face_sums[0] * inside[0],
            face_sums[2] * inside[2],
            face_sums[4],
            jnp.sum(forcing, axis=(1, 2)),
        ]
    )
    brick_here = (peer_ids == brick_index).astype(jnp.float32)
    spread = (brick_here[:, None, None, None] * slab_slot(record)[None]).reshape(-1)
    summed, xy_land, z_land = exchange(as_tile(spread), forcing, diagonal, 2)
    summed = summed.reshape(-1)[: spread.shape[0]]
    xy_rows = 2 * slot_count + 2
    z_rows = 2 * slot_count
    residual_halo = halo(forcing, xy_land[:, :xy_rows], z_land[:, :z_rows], 0.0)
    diagonal_halo = halo(diagonal, xy_land[:, xy_rows:], z_land[:, z_rows:], 1.0)
    gathered = lax.dynamic_index_in_dim(
        summed.reshape(brick_count, grp_count, 5, slot_count), brick_index, keepdims=False
    )
    columns = jnp.transpose(gathered, (1, 0, 2)).reshape(5, -1)
    matrix = assemble(columns[0], (columns[1], columns[2], columns[3]), (PATCH_Y, 1, slot_count))
    factor = jnp.linalg.cholesky(matrix)

    def coarse_solve(terms):
        middle = lax.linalg.triangular_solve(factor, terms[:, None], left_side=True, lower=True)
        result = lax.linalg.triangular_solve(
            factor, middle, left_side=True, lower=True, transpose_a=True
        )
        return lax.dynamic_slice_in_dim(result[:, 0], slab_index * slot_count, slot_count)

    def round_trip(field, field_halo, coef, smooth, with_faces=True):
        out, total, xy_land, z_land, dot = one_round(
            field, bonds, masks, diagonal, *field_halo, coef, smooth, with_faces
        )
        total = total.reshape(-1)
        out_halo = halo(out, xy_land, z_land, 0.0) if with_faces else None
        if smooth:
            return out, dot[0], None, out_halo
        count = brick_count * grp_count * slot_count
        mine = lax.dynamic_index_in_dim(
            total[1 : 1 + count].reshape(brick_count, -1), brick_index, keepdims=False
        )
        return out, dot[0], mine, out_halo

    def precondition(residual_field, field_halo, terms):
        smoothed_halo = [OMEGA * part / scale for part, scale in zip(field_halo, diagonal_halo)]
        return round_trip(residual_field, smoothed_halo, coarse_solve(terms), True)

    no_coarse = jnp.zeros((slot_count,), jnp.float32)
    terms = columns[4]
    solution_field = jnp.zeros_like(forcing)
    residual = forcing
    search, energy, _, search_halo = precondition(residual, residual_halo, terms)
    for iteration in range(ITERS):
        mapped, curvature, mapped_terms, mapped_halo = round_trip(
            search, search_halo, no_coarse, False, iteration + 1 < ITERS
        )
        step_size = energy / curvature
        solution_field = solution_field + step_size * search
        residual = residual - step_size * mapped
        if iteration + 1 < ITERS:
            residual_halo = [
                part - step_size * change for part, change in zip(residual_halo, mapped_halo)
            ]
            terms = terms - step_size * mapped_terms
            smoothed, renewed, _, smoothed_halo = precondition(residual, residual_halo, terms)
            search = smoothed + renewed / energy * search
            search_halo = [
                part + renewed / energy * old for part, old in zip(smoothed_halo, search_halo)
            ]
            energy = renewed
    return (solution_field[None, None], residual[None, None])


def solution(mesh):
    return jax.shard_map(
        on_device,
        mesh=mesh,
        in_specs=(
            P("grp", "brick", None, None, None),
            P("grp", "brick", None, None, None),
            P("grp", "brick", None, None, None, None),
            P(),
            P(),
        ),
        out_specs=(P("grp", "brick", None, None, None), P("grp", "brick", None, None, None)),
        check_vma=False,
    )
```

```python
import functools

import jax
import jax.numpy as jnp
from jax import lax
from jax.experimental import pallas as pl
from jax.experimental.pallas import tpu as pltpu
from jax.sharding import PartitionSpec as P

MESH_IDS = pl.DeviceIdType.MESH

BS = 32
PATCH_X = 1
PATCH_Y = 2
ITERS = 3


OMEGA = 0.6


def share(
    x_ref, xy_ref, z_ref, o_ref, xy_out, z_out, landed_b, landed_g, landed_xy, landed_z,
    send_b, recv_b, send_g, recv_g, send_xy, recv_xy, send_z, recv_z, brick_peers, grp_peers,
    dot_ref=None, with_faces=True,
):
    here_brick = lax.axis_index("brick")
    here_grp = lax.axis_index("grp")
    n_brick = landed_b.shape[0]
    n_grp = landed_g.shape[0]

    def send(src, dst, sends, recvs, index, peer):
        copy = pltpu.make_async_remote_copy(
            src_ref=src,
            dst_ref=dst.at[index],
            send_sem=sends.at[index],
            recv_sem=recvs.at[index],
            device_id=peer,
            device_id_type=MESH_IDS,
        )
        copy.start()
        return copy

    face_copies = []
    if with_faces:
        face_copies = [
            send(z_ref, landed_z, send_z, recv_z, 0, grp_peers[0]),
            send(z_ref, landed_z, send_z, recv_z, 1, grp_peers[-1]),
        ]
        face_copies += [
            send(xy_ref, landed_xy, send_xy, recv_xy, k, peer)
            for k, peer in enumerate(brick_peers, start=1)
        ]
    copies = [
        send(x_ref, landed_b, send_b, recv_b, k, peer)
        for k, peer in enumerate(brick_peers, start=1)
    ]
    landed_b[0] = x_ref[...]
    for copy in copies:
        copy.wait()
    total = landed_b[lax.rem(here_brick, n_brick)]
    for j in range(1, n_brick):
        total = total + landed_b[lax.rem(here_brick + n_brick - j, n_brick)]
    o_ref[...] = total
    landed_g[0] = total
    copies = [
        send(o_ref, landed_g, send_g, recv_g, k, peer)
        for k, peer in enumerate(grp_peers, start=1)
    ]
    for copy in copies:
        copy.wait()
    total = landed_g[lax.rem(here_grp, n_grp)]
    for j in range(1, n_grp):
        total = total + landed_g[lax.rem(here_grp + n_grp - j, n_grp)]
    o_ref[...] = total
    for copy in face_copies:
        copy.wait()
    if with_faces:
        landed_xy[0] = xy_ref[...]
        xy_out[...] = landed_xy[...]
        z_out[...] = landed_z[...]
    else:
        xy_out[...] = jnp.zeros(xy_out.shape, jnp.float32)
        z_out[...] = jnp.zeros(z_out.shape, jnp.float32)
    if dot_ref is not None:
        tile_rows, tile_lanes = o_ref.shape
        first = lax.broadcasted_iota(jnp.int32, (tile_rows, tile_lanes), 0) * tile_lanes
        first = first + lax.broadcasted_iota(jnp.int32, (tile_rows, tile_lanes), 1)
        dot_ref[0] = jnp.sum(jnp.where(first == 0, total, 0.0))


def setup_faces(f_ref, xy_ref, z_ref, xy_base, z_base):
    slots, width, lanes = f_ref.shape
    pick = lax.broadcasted_iota(jnp.int32, (BS, lanes), 0)
    spot = lax.broadcasted_iota(jnp.int32, (BS, lanes), 1)
    spread_y = (spot % BS == pick).astype(jnp.float32)
    flat_mask = spot // BS == pick
    source_lane = lax.broadcasted_iota(jnp.int32, (lanes, BS), 0)
    place = lax.broadcasted_iota(jnp.int32, (lanes, BS), 1)
    layers = [
        (source_lane == offset + step * place).astype(jnp.float32)
        for offset, step in ((0, 1), (lanes - BS, 1), (0, BS), (BS - 1, BS))
    ]

    def spread(face, table):
        high = face.astype(jnp.bfloat16)
        rest = face - high.astype(jnp.float32)
        middle = rest.astype(jnp.bfloat16)
        low = (rest - middle.astype(jnp.float32)).astype(jnp.bfloat16)
        table = table.astype(jnp.bfloat16)
        parts = [
            jnp.dot(part, table, preferred_element_type=jnp.float32) for part in (high, middle, low)
        ]
        return (parts[0] + parts[1]) + parts[2]

    def flatten(layer):
        return jnp.sum(jnp.where(flat_mask, spread(layer, spread_y), 0.0), axis=0, keepdims=True)

    for s in range(slots):
        total = f_ref[s]
        xy_ref[pl.ds(xy_base + s, 1), :] = total[0:1, :]
        xy_ref[pl.ds(xy_base + slots + s, 1), :] = total[width - 1 : width, :]
        if s == 0:
            xy_ref[pl.ds(xy_base + 2 * slots, 1), :] = flatten(spread(total, layers[0]))
        if s == slots - 1:
            xy_ref[pl.ds(xy_base + 2 * slots + 1, 1), :] = flatten(spread(total, layers[1]))
        z_ref[pl.ds(z_base + s, 1), :] = flatten(spread(total, layers[2]))
        z_ref[pl.ds(z_base + slots + s, 1), :] = flatten(spread(total, layers[3]))


def exchange_kernel(
    record_ref, forcing_ref, diag_ref, o_ref, xy_out, z_out,
    x_ref, xy_ref, z_ref, landed_b, landed_g, landed_xy, landed_z,
    send_b, recv_b, send_g, recv_g, send_xy, recv_xy, send_z, recv_z,
):
    here_brick = lax.axis_index("brick")
    here_grp = lax.axis_index("grp")
    n_brick = landed_b.shape[0]
    n_grp = landed_g.shape[0]
    brick_peers = [(lax.rem(here_brick + k, n_brick), here_grp) for k in range(1, n_brick)]
    grp_peers = [(here_brick, lax.rem(here_grp + k, n_grp)) for k in range(1, n_grp)]
    barrier = pltpu.get_barrier_semaphore()
    for peer in brick_peers + grp_peers:
        pl.semaphore_signal(barrier, inc=1, device_id=peer, device_id_type=MESH_IDS)
    slots = forcing_ref.shape[0]
    setup_faces(forcing_ref, xy_ref, z_ref, 0, 0)
    setup_faces(diag_ref, xy_ref, z_ref, 2 * slots + 2, 2 * slots)
    tile_rows, tile_lanes = x_ref.shape
    flat = lax.broadcasted_iota(jnp.int32, (tile_rows, tile_lanes), 0) * tile_lanes
    flat = flat + lax.broadcasted_iota(jnp.int32, (tile_rows, tile_lanes), 1)
    count = record_ref.shape[0]
    base = (here_brick * n_grp + here_grp) * count
    tile = jnp.zeros((tile_rows, tile_lanes), jnp.float32)
    for i in range(count):
        tile = jnp.where(flat == base + i, record_ref[i], tile)
    x_ref[...] = tile
    pl.semaphore_wait(barrier, len(brick_peers) + len(grp_peers))

    share(
        x_ref, xy_ref, z_ref, o_ref, xy_out, z_out, landed_b, landed_g, landed_xy, landed_z,
        send_b, recv_b, send_g, recv_g, send_xy, recv_xy, send_z, recv_z, brick_peers, grp_peers,
    )


def exchange(record, forcing, diag, kernel_id):
    slots, _, lanes = forcing.shape
    total = lax.axis_size("brick") * lax.axis_size("grp") * record.shape[0]
    rows = -(-total // 128)
    tile = jax.ShapeDtypeStruct((-(-rows // 8) * 8, 128), jnp.float32)
    xy = jax.ShapeDtypeStruct((2 * (2 * slots + 2), lanes), jnp.float32)
    z = jax.ShapeDtypeStruct((2 * (2 * slots), lanes), jnp.float32)
    n_brick = lax.axis_size("brick")
    n_grp = lax.axis_size("grp")
    vmem = pl.BlockSpec(memory_space=pltpu.VMEM)
    dma = pltpu.SemaphoreType.DMA
    return pl.pallas_call(
        exchange_kernel,
        out_shape=(
            jax.ShapeDtypeStruct(tile.shape, jnp.float32),
            jax.ShapeDtypeStruct((n_brick,) + xy.shape, jnp.float32),
            jax.ShapeDtypeStruct((2,) + z.shape, jnp.float32),
        ),
        in_specs=[pl.BlockSpec(memory_space=pltpu.SMEM), vmem, vmem],
        out_specs=(vmem, vmem, vmem),
        scratch_shapes=[
            pltpu.VMEM(tile.shape, jnp.float32),
            pltpu.VMEM(xy.shape, jnp.float32),
            pltpu.VMEM(z.shape, jnp.float32),
            pltpu.VMEM((n_brick,) + tile.shape, jnp.float32),
            pltpu.VMEM((n_grp,) + tile.shape, jnp.float32),
            pltpu.VMEM((n_brick,) + xy.shape, jnp.float32),
            pltpu.VMEM((2,) + z.shape, jnp.float32),
            dma((n_brick,)),
            dma((n_brick,)),
            dma((n_grp,)),
            dma((n_grp,)),
            dma((n_brick,)),
            dma((n_brick,)),
            dma((2,)),
            dma((2,)),
        ],
        compiler_params=pltpu.CompilerParams(collective_id=kernel_id, has_side_effects=True),
    )(record, forcing, diag)


def stencil_body(
    coef_ref, f_ref, bonds_ref, masks_ref, diag_ref, rows_ref, faces_ref, o_ref, xy_ref, z_ref, smooth,
    with_faces=True,
):
    slots, width, lanes = f_ref.shape
    row = lax.broadcasted_iota(jnp.int32, (width, lanes), 0)
    lane = lax.broadcasted_iota(jnp.int32, (width, lanes), 1)
    pick = lax.broadcasted_iota(jnp.int32, (BS, lanes), 0)
    spot = lax.broadcasted_iota(jnp.int32, (BS, lanes), 1)
    spread_z = (spot // BS == pick).astype(jnp.float32)
    spread_y = (spot % BS == pick).astype(jnp.float32)

    def spread(face, table):
        high = face.astype(jnp.bfloat16)
        rest = face - high.astype(jnp.float32)
        middle = rest.astype(jnp.bfloat16)
        low = (rest - middle.astype(jnp.float32)).astype(jnp.bfloat16)
        table = table.astype(jnp.bfloat16)
        parts = [
            jnp.dot(part, table, preferred_element_type=jnp.float32) for part in (high, middle, low)
        ]
        return (parts[0] + parts[1]) + parts[2]

    borders = [
        row == width - 1,
        row == 0,
        lane >= lanes - BS,
        lane < BS,
        lane % BS == BS - 1,
        lane % BS == 0,
    ]
    source_lane = lax.broadcasted_iota(jnp.int32, (lanes, BS), 0)
    place = lax.broadcasted_iota(jnp.int32, (lanes, BS), 1)
    layers = [
        (source_lane == offset + step * place).astype(jnp.float32)
        for offset, step in ((0, 1), (lanes - BS, 1), (0, BS), (BS - 1, BS))
    ]
    flat_mask = spot // BS == pick

    def flatten(layer):
        spread_out = jnp.where(flat_mask, spread(layer, spread_y), 0.0)
        return jnp.sum(spread_out, axis=0, keepdims=True)

    dot = jnp.float32(0.0)
    sums = []
    for s in range(slots):
        ds = diag_ref[s]
        if smooth:
            rs = f_ref[s]
            fs = OMEGA * rs / ds
        else:
            fs = f_ref[s]
        xp = jnp.where(row == width - 1, rows_ref[0, s], pltpu.roll(fs, width - 1, 0))
        xm = jnp.where(row == 0, rows_ref[1, s], pltpu.roll(fs, 1, 0))
        yp = jnp.where(lane >= lanes - BS, spread(faces_ref[0, s], spread_y), pltpu.roll(fs, lanes - BS, 1))
        ym = jnp.where(lane < BS, spread(faces_ref[1, s], spread_y), pltpu.roll(fs, BS, 1))
        zp = jnp.where(lane % BS == BS - 1, spread(faces_ref[2, s], spread_z), pltpu.roll(fs, lanes - 1, 1))
        zm = jnp.where(lane % BS == 0, spread(faces_ref[3, s], spread_z), pltpu.roll(fs, 1, 1))
        total = ds * fs
        for d, beyond in enumerate([xp, xm, yp, ym, zp, zm]):
            base = 2 * (d * slots + s)
            active = jnp.where(borders[d], masks_ref[base + 1], masks_ref[base])
            total = total - bonds_ref[d, s] * active * beyond
        if smooth:
            total = fs + OMEGA * (rs - total) / ds
            total = total + coef_ref[s]
            dot = dot + jnp.sum(rs * total)
        else:
            dot = dot + jnp.sum(fs * total)
            sums.append(jnp.sum(total))
        o_ref[s] = total
        if not with_faces:
            continue
        xy_ref[pl.ds(s, 1), :] = total[0:1, :]
        xy_ref[pl.ds(slots + s, 1), :] = total[width - 1 : width, :]
        if s == 0:
            xy_ref[pl.ds(2 * slots, 1), :] = flatten(spread(total, layers[0]))
        if s == slots - 1:
            xy_ref[pl.ds(2 * slots + 1, 1), :] = flatten(spread(total, layers[1]))
        z_ref[pl.ds(s, 1), :] = flatten(spread(total, layers[2]))
        z_ref[pl.ds(slots + s, 1), :] = flatten(spread(total, layers[3]))
    return dot, sums


def round_kernel(
    coef_ref, f_ref, bonds_ref, masks_ref, diag_ref, rows_ref, faces_ref,
    o_ref, total_ref, xy_out, z_out, dot_ref,
    xy_buf, z_buf, tile_buf, landed_b, landed_g, landed_xy, landed_z,
    send_b, recv_b, send_g, recv_g, send_xy, recv_xy, send_z, recv_z, *, smooth, with_faces
):
    here_brick = lax.axis_index("brick")
    here_grp = lax.axis_index("grp")
    n_brick = landed_b.shape[0]
    n_grp = landed_g.shape[0]
    brick_peers = [(lax.rem(here_brick + k, n_brick), here_grp) for k in range(1, n_brick)]
    grp_peers = [(here_brick, lax.rem(here_grp + k, n_grp)) for k in range(1, n_grp)]
    barrier = pltpu.get_barrier_semaphore()
    for peer in brick_peers + grp_peers:
        pl.semaphore_signal(barrier, inc=1, device_id=peer, device_id_type=MESH_IDS)
    dot, sums = stencil_body(
        coef_ref, f_ref, bonds_ref, masks_ref, diag_ref, rows_ref, faces_ref, o_ref, xy_buf, z_buf,
        smooth, with_faces,
    )
    tile_rows, tile_lanes = tile_buf.shape
    flat = lax.broadcasted_iota(jnp.int32, (tile_rows, tile_lanes), 0) * tile_lanes
    flat = flat + lax.broadcasted_iota(jnp.int32, (tile_rows, tile_lanes), 1)
    tile = jnp.where(flat == 0, dot, 0.0)
    slots = f_ref.shape[0]
    for s, value in enumerate(sums):
        position = 1 + (here_brick * n_grp + here_grp) * slots + s
        tile = jnp.where(flat == position, value, tile)
    tile_buf[...] = tile
    pl.semaphore_wait(barrier, len(brick_peers) + len(grp_peers))
    share(
        tile_buf, xy_buf, z_buf, total_ref, xy_out, z_out, landed_b, landed_g, landed_xy, landed_z,
        send_b, recv_b, send_g, recv_g, send_xy, recv_xy, send_z, recv_z, brick_peers, grp_peers,
        dot_ref=dot_ref, with_faces=with_faces,
    )


def one_round(field, bonds, masks, diag, rows, faces, coef, smooth, with_faces=True):
    slots, _, lanes = field.shape
    n_brick = lax.axis_size("brick")
    n_grp = lax.axis_size("grp")
    tile = (8, 128)
    xy = (2 * slots + 2, lanes)
    z = (2 * slots, lanes)
    vmem = pl.BlockSpec(memory_space=pltpu.VMEM)
    smem = pl.BlockSpec(memory_space=pltpu.SMEM)
    dma = pltpu.SemaphoreType.DMA
    return pl.pallas_call(
        functools.partial(round_kernel, smooth=smooth, with_faces=with_faces),
        out_shape=(
            jax.ShapeDtypeStruct(field.shape, jnp.float32),
            jax.ShapeDtypeStruct(tile, jnp.float32),
            jax.ShapeDtypeStruct((n_brick,) + xy, jnp.float32),
            jax.ShapeDtypeStruct((2,) + z, jnp.float32),
            jax.ShapeDtypeStruct((1,), jnp.float32),
        ),
        in_specs=[smem, vmem, vmem, smem, vmem, vmem, vmem],
        out_specs=(vmem, vmem, vmem, vmem, smem),
        scratch_shapes=[
            pltpu.VMEM(xy, jnp.float32),
            pltpu.VMEM(z, jnp.float32),
            pltpu.VMEM(tile, jnp.float32),
            pltpu.VMEM((n_brick,) + tile, jnp.float32),
            pltpu.VMEM((n_grp,) + tile, jnp.float32),
            pltpu.VMEM((n_brick,) + xy, jnp.float32),
            pltpu.VMEM((2,) + z, jnp.float32),
            dma((n_brick,)),
            dma((n_brick,)),
            dma((n_grp,)),
            dma((n_grp,)),
            dma((n_brick,)),
            dma((n_brick,)),
            dma((2,)),
            dma((2,)),
        ],
        compiler_params=pltpu.CompilerParams(
            collective_id=(3 if smooth else 1) if with_faces else 4, has_side_effects=True
        ),
    )(coef, field, bonds, masks, diag, rows, faces)


def assemble(coarse_diag, couplings, strides):
    extent = coarse_diag.shape[0]
    matrix = jnp.diag(coarse_diag)
    for coupling, stride in zip(couplings, strides):
        banded = coupling[: extent - stride]
        matrix = matrix - jnp.diag(banded, stride) - jnp.diag(banded, -stride)
    return matrix


def on_device(source, uptake, conductance, occupancy, assignment):
    face_size = BS * BS
    slot_count = PATCH_X * PATCH_Y
    slab_index = lax.axis_index("grp")
    brick_index = lax.axis_index("brick")
    brick_count = lax.axis_size("brick")
    across = brick_count // 2
    peer_ids = jnp.arange(brick_count, dtype=jnp.int32)
    patch_index = assignment[brick_index]
    patch_row = patch_index // across
    patch_column = patch_index % across

    def owner_of(row_shift, column_shift):
        row_target = patch_row + row_shift
        column_target = patch_column + column_shift
        inside = (
            (row_target >= 0) & (row_target < 2) & (column_target >= 0) & (column_target < across)
        )
        holder = jnp.sum(jnp.where(assignment == row_target * across + column_target, peer_ids, 0))
        return jnp.where(inside, holder, -1)

    wanted = jnp.stack([owner_of(1, 0), owner_of(-1, 0), owner_of(0, 1), owner_of(0, -1)])
    padded = jnp.pad(occupancy, 1)
    window = lax.dynamic_slice(
        padded,
        (slab_index, patch_row * PATCH_X, patch_column * PATCH_Y),
        (3, PATCH_X + 2, PATCH_Y + 2),
    ).astype(jnp.float32)
    centre = window[1, 1:-1, 1:-1].reshape(slot_count)
    toward = [
        window[1, 2:, 1:-1],
        window[1, :-2, 1:-1],
        window[1, 1:-1, 2:],
        window[1, 1:-1, :-2],
        window[2, 1:-1, 1:-1],
        window[0, 1:-1, 1:-1],
    ]
    first_axis = lax.broadcasted_iota(jnp.int32, (1, BS, face_size), 1)
    flat_axis = lax.broadcasted_iota(jnp.int32, (1, BS, face_size), 2)
    second_axis = flat_axis // BS
    third_axis = flat_axis % BS
    cube_third = lax.broadcasted_iota(jnp.int32, (1, BS, BS, BS), 3)
    borders = [
        first_axis == BS - 1,
        first_axis == 0,
        second_axis == BS - 1,
        second_axis == 0,
        third_axis == BS - 1,
        third_axis == 0,
    ]
    bonds = conductance[0, 0]
    live_here = centre[:, None, None]
    effective = []
    for direction in range(6):
        neighbour_live = toward[direction].reshape(slot_count)[:, None, None]
        active = jnp.where(borders[direction], live_here * neighbour_live, live_here)
        effective.append(bonds[direction] * active)
    absorb = uptake[0, 0]
    diagonal = absorb
    for direction in range(6):
        diagonal = diagonal + effective[direction]

    masks = jnp.stack(
        [
            jnp.stack([centre, centre * toward[direction].reshape(slot_count)], axis=1)
            for direction in range(6)
        ]
    ).reshape(-1)

    lane_ids = jnp.arange(face_size, dtype=jnp.int32)[:, None]
    layer_ids = BS * jnp.arange(BS, dtype=jnp.int32)[None, :]
    picker = jnp.concatenate([lane_ids == layer_ids, lane_ids == layer_ids + BS - 1], axis=1)
    picker = picker.astype(jnp.float32)

    def side_faces(field):
        picked = jnp.dot(
            field.reshape(slot_count * BS, face_size), picker, precision=lax.Precision.HIGHEST
        )
        z = picked.reshape(slot_count, BS, 2, BS).transpose(2, 0, 1, 3)
        xy = jnp.concatenate(
            [
                field[:, 0, :],
                field[:, BS - 1, :],
                field[0, :, :BS].reshape(1, face_size),
                field[slot_count - 1, :, face_size - BS :].reshape(1, face_size),
            ]
        )
        return xy, z.reshape(2 * slot_count, face_size)

    def pick(landed, holder, fill):
        offset = lax.rem(brick_index - holder + brick_count, brick_count)
        got = lax.dynamic_index_in_dim(landed, offset, keepdims=False)
        return jnp.where(holder >= 0, got, fill)

    def halo(field, xy_land, z_land, fill):
        xplus = pick(xy_land, wanted[0], fill)
        xminus = pick(xy_land, wanted[1], fill)
        yplus = pick(xy_land, wanted[2], fill)
        yminus = pick(xy_land, wanted[3], fill)
        rows = jnp.stack([xplus[:slot_count], xminus[slot_count : 2 * slot_count]])[:, :, None, :]
        beyond_yplus = jnp.stack([field[1, :, :BS], yplus[2 * slot_count].reshape(BS, BS)])
        beyond_yminus = jnp.stack(
            [yminus[2 * slot_count + 1].reshape(BS, BS), field[0, :, face_size - BS :]]
        )
        above = jnp.where(slab_index < grp_count - 1, z_land[1, :slot_count], fill)
        below = jnp.where(slab_index > 0, z_land[0, slot_count:], fill)
        faces = jnp.stack(
            [
                beyond_yplus,
                beyond_yminus,
                above.reshape(slot_count, BS, BS),
                below.reshape(slot_count, BS, BS),
            ]
        )
        return rows, faces

    slot_ids = jnp.arange(slot_count)
    brick_first = slot_ids // PATCH_Y
    brick_second = slot_ids % PATCH_Y
    inside = [
        (brick_first < PATCH_X - 1).astype(jnp.float32),
        (brick_first > 0).astype(jnp.float32),
        (brick_second < PATCH_Y - 1).astype(jnp.float32),
        (brick_second > 0).astype(jnp.float32),
    ]
    face_sums = [
        jnp.sum(effective[0][:, BS - 1, :], axis=1),
        jnp.sum(effective[1][:, 0, :], axis=1),
        jnp.sum(effective[2][:, :, face_size - BS :], axis=(1, 2)),
        jnp.sum(effective[3][:, :, :BS], axis=(1, 2)),
        jnp.sum(jnp.where(borders[4], effective[4], 0.0), axis=(1, 2)),
        jnp.sum(jnp.where(borders[5], effective[5], 0.0), axis=(1, 2)),
    ]
    coarse_diag = jnp.sum(absorb, axis=(1, 2))
    for direction in range(4):
        coarse_diag = coarse_diag + face_sums[direction] * inside[direction]
    coarse_diag = coarse_diag + face_sums[4] + face_sums[5]
    grp_count = lax.axis_size("grp")
    grp_ids = jnp.arange(grp_count, dtype=jnp.int32)

    def slab_slot(values):
        here = (grp_ids == slab_index).astype(jnp.float32)
        return here[:, None, None] * values[None]

    forcing = source[0, 0] * live_here

    def as_tile(values):
        rows = -(-values.shape[0] // 128)
        rows = -(-rows // 8) * 8
        return jnp.pad(values, (0, rows * 128 - values.shape[0])).reshape(rows, 128)

    record = jnp.stack(
        [
            coarse_diag,
            face_sums[0] * inside[0],
            face_sums[2] * inside[2],
            face_sums[4],
            jnp.sum(forcing, axis=(1, 2)),
        ]
    )
    brick_here = (peer_ids == brick_index).astype(jnp.float32)
    summed, xy_land, z_land = exchange(record.reshape(-1), forcing, diagonal, 2)
    summed = summed.reshape(-1)[: brick_count * grp_count * record.size]
    xy_rows = 2 * slot_count + 2
    z_rows = 2 * slot_count
    residual_halo = halo(forcing, xy_land[:, :xy_rows], z_land[:, :z_rows], 0.0)
    diagonal_halo = halo(diagonal, xy_land[:, xy_rows:], z_land[:, z_rows:], 1.0)
    gathered = lax.dynamic_index_in_dim(
        summed.reshape(brick_count, grp_count, 5, slot_count), brick_index, keepdims=False
    )
    columns = jnp.transpose(gathered, (1, 0, 2)).reshape(5, -1)
    matrix = assemble(columns[0], (columns[1], columns[2], columns[3]), (PATCH_Y, 1, slot_count))
    factor = jnp.linalg.cholesky(matrix)

    def coarse_solve(terms):
        middle = lax.linalg.triangular_solve(factor, terms[:, None], left_side=True, lower=True)
        result = lax.linalg.triangular_solve(
            factor, middle, left_side=True, lower=True, transpose_a=True
        )
        return lax.dynamic_slice_in_dim(result[:, 0], slab_index * slot_count, slot_count)

    def round_trip(field, field_halo, coef, smooth, with_faces=True):
        out, total, xy_land, z_land, dot = one_round(
            field, bonds, masks, diagonal, *field_halo, coef, smooth, with_faces
        )
        total = total.reshape(-1)
        out_halo = halo(out, xy_land, z_land, 0.0) if with_faces else None
        if smooth:
            return out, dot[0], None, out_halo
        count = brick_count * grp_count * slot_count
        mine = lax.dynamic_index_in_dim(
            total[1 : 1 + count].reshape(brick_count, -1), brick_index, keepdims=False
        )
        return out, dot[0], mine, out_halo

    def precondition(residual_field, field_halo, terms):
        smoothed_halo = [OMEGA * part / scale for part, scale in zip(field_halo, diagonal_halo)]
        return round_trip(residual_field, smoothed_halo, coarse_solve(terms), True)

    no_coarse = jnp.zeros((slot_count,), jnp.float32)
    terms = columns[4]
    solution_field = jnp.zeros_like(forcing)
    residual = forcing
    search, energy, _, search_halo = precondition(residual, residual_halo, terms)
    for iteration in range(ITERS):
        mapped, curvature, mapped_terms, mapped_halo = round_trip(
            search, search_halo, no_coarse, False, iteration + 1 < ITERS
        )
        step_size = energy / curvature
        solution_field = solution_field + step_size * search
        residual = residual - step_size * mapped
        if iteration + 1 < ITERS:
            residual_halo = [
                part - step_size * change for part, change in zip(residual_halo, mapped_halo)
            ]
            terms = terms - step_size * mapped_terms
            smoothed, renewed, _, smoothed_halo = precondition(residual, residual_halo, terms)
            search = smoothed + renewed / energy * search
            search_halo = [
                part + renewed / energy * old for part, old in zip(smoothed_halo, search_halo)
            ]
            energy = renewed
    return (solution_field[None, None], residual[None, None])


def solution(mesh):
    return jax.shard_map(
        on_device,
        mesh=mesh,
        in_specs=(
            P("grp", "brick", None, None, None),
            P("grp", "brick", None, None, None),
            P("grp", "brick", None, None, None, None),
            P(),
            P(),
        ),
        out_specs=(P("grp", "brick", None, None, None), P("grp", "brick", None, None, None)),
        check_vma=False,
    )
```

```python
import functools

import jax
import jax.numpy as jnp
from jax import lax
from jax.experimental import pallas as pl
from jax.experimental.pallas import tpu as pltpu
from jax.sharding import PartitionSpec as P

MESH_IDS = pl.DeviceIdType.MESH

BS = 32
PATCH_X = 1
PATCH_Y = 2
ITERS = 3


OMEGA = 0.6


def share(
    x_ref, xy_ref, z_ref, o_ref, xy_out, z_out, landed_b, landed_g, landed_xy, landed_z,
    send_b, recv_b, send_g, recv_g, send_xy, recv_xy, send_z, recv_z, brick_peers, grp_peers,
    dot_ref=None, with_faces=True,
):
    here_brick = lax.axis_index("brick")
    here_grp = lax.axis_index("grp")
    n_brick = landed_b.shape[0]
    n_grp = landed_g.shape[0]

    def send(src, dst, sends, recvs, index, peer):
        copy = pltpu.make_async_remote_copy(
            src_ref=src,
            dst_ref=dst.at[index],
            send_sem=sends.at[index],
            recv_sem=recvs.at[index],
            device_id=peer,
            device_id_type=MESH_IDS,
        )
        copy.start()
        return copy

    face_copies = []
    if with_faces:
        face_copies = [
            send(z_ref, landed_z, send_z, recv_z, 0, grp_peers[0]),
            send(z_ref, landed_z, send_z, recv_z, 1, grp_peers[-1]),
        ]
        face_copies += [
            send(xy_ref, landed_xy, send_xy, recv_xy, k, peer)
            for k, peer in enumerate(brick_peers, start=1)
        ]
    copies = [
        send(x_ref, landed_b, send_b, recv_b, k, peer)
        for k, peer in enumerate(brick_peers, start=1)
    ]
    landed_b[0] = x_ref[...]
    for copy in copies:
        copy.wait()
    total = landed_b[lax.rem(here_brick, n_brick)]
    for j in range(1, n_brick):
        total = total + landed_b[lax.rem(here_brick + n_brick - j, n_brick)]
    o_ref[...] = total
    landed_g[0] = total
    copies = [
        send(o_ref, landed_g, send_g, recv_g, k, peer)
        for k, peer in enumerate(grp_peers, start=1)
    ]
    for copy in copies:
        copy.wait()
    total = landed_g[lax.rem(here_grp, n_grp)]
    for j in range(1, n_grp):
        total = total + landed_g[lax.rem(here_grp + n_grp - j, n_grp)]
    o_ref[...] = total
    for copy in face_copies:
        copy.wait()
    if with_faces:
        landed_xy[0] = xy_ref[...]
        xy_out[...] = landed_xy[...]
        z_out[...] = landed_z[...]
    else:
        xy_out[...] = jnp.zeros(xy_out.shape, jnp.float32)
        z_out[...] = jnp.zeros(z_out.shape, jnp.float32)
    if dot_ref is not None:
        tile_rows, tile_lanes = o_ref.shape
        first = lax.broadcasted_iota(jnp.int32, (tile_rows, tile_lanes), 0) * tile_lanes
        first = first + lax.broadcasted_iota(jnp.int32, (tile_rows, tile_lanes), 1)
        dot_ref[0] = jnp.sum(jnp.where(first == 0, total, 0.0))


def setup_faces(f_ref, xy_ref, z_ref, xy_base, z_base):
    slots, width, lanes = f_ref.shape
    pick = lax.broadcasted_iota(jnp.int32, (BS, lanes), 0)
    spot = lax.broadcasted_iota(jnp.int32, (BS, lanes), 1)
    spread_y = (spot % BS == pick).astype(jnp.float32)
    flat_mask = spot // BS == pick
    source_lane = lax.broadcasted_iota(jnp.int32, (lanes, BS), 0)
    place = lax.broadcasted_iota(jnp.int32, (lanes, BS), 1)
    layers = [
        (source_lane == offset + step * place).astype(jnp.float32)
        for offset, step in ((0, 1), (lanes - BS, 1), (0, BS), (BS - 1, BS))
    ]

    def spread(face, table):
        high = face.astype(jnp.bfloat16)
        rest = face - high.astype(jnp.float32)
        middle = rest.astype(jnp.bfloat16)
        low = (rest - middle.astype(jnp.float32)).astype(jnp.bfloat16)
        table = table.astype(jnp.bfloat16)
        parts = [
            jnp.dot(part, table, preferred_element_type=jnp.float32) for part in (high, middle, low)
        ]
        return (parts[0] + parts[1]) + parts[2]

    def flatten(layer):
        return jnp.sum(jnp.where(flat_mask, spread(layer, spread_y), 0.0), axis=0, keepdims=True)

    for s in range(slots):
        total = f_ref[s]
        xy_ref[pl.ds(xy_base + s, 1), :] = total[0:1, :]
        xy_ref[pl.ds(xy_base + slots + s, 1), :] = total[width - 1 : width, :]
        if s == 0:
            xy_ref[pl.ds(xy_base + 2 * slots, 1), :] = flatten(spread(total, layers[0]))
        if s == slots - 1:
            xy_ref[pl.ds(xy_base + 2 * slots + 1, 1), :] = flatten(spread(total, layers[1]))
        z_ref[pl.ds(z_base + s, 1), :] = flatten(spread(total, layers[2]))
        z_ref[pl.ds(z_base + slots + s, 1), :] = flatten(spread(total, layers[3]))


def exchange_kernel(
    record_ref, forcing_ref, diag_ref, o_ref, xy_out, z_out,
    x_ref, xy_ref, z_ref, landed_b, landed_g, landed_xy, landed_z,
    send_b, recv_b, send_g, recv_g, send_xy, recv_xy, send_z, recv_z,
):
    here_brick = lax.axis_index("brick")
    here_grp = lax.axis_index("grp")
    n_brick = landed_b.shape[0]
    n_grp = landed_g.shape[0]
    brick_peers = [(lax.rem(here_brick + k, n_brick), here_grp) for k in range(1, n_brick)]
    grp_peers = [(here_brick, lax.rem(here_grp + k, n_grp)) for k in range(1, n_grp)]
    barrier = pltpu.get_barrier_semaphore()
    for peer in brick_peers + grp_peers:
        pl.semaphore_signal(barrier, inc=1, device_id=peer, device_id_type=MESH_IDS)
    slots = forcing_ref.shape[0]
    setup_faces(forcing_ref, xy_ref, z_ref, 0, 0)
    setup_faces(diag_ref, xy_ref, z_ref, 2 * slots + 2, 2 * slots)
    tile_rows, tile_lanes = x_ref.shape
    flat = lax.broadcasted_iota(jnp.int32, (tile_rows, tile_lanes), 0) * tile_lanes
    flat = flat + lax.broadcasted_iota(jnp.int32, (tile_rows, tile_lanes), 1)
    count = record_ref.shape[0]
    base = (here_brick * n_grp + here_grp) * count
    tile = jnp.zeros((tile_rows, tile_lanes), jnp.float32)
    for i in range(count):
        tile = jnp.where(flat == base + i, record_ref[i], tile)
    x_ref[...] = tile
    pl.semaphore_wait(barrier, len(brick_peers) + len(grp_peers))

    share(
        x_ref, xy_ref, z_ref, o_ref, xy_out, z_out, landed_b, landed_g, landed_xy, landed_z,
        send_b, recv_b, send_g, recv_g, send_xy, recv_xy, send_z, recv_z, brick_peers, grp_peers,
    )


def exchange(record, forcing, diag, kernel_id):
    slots, _, lanes = forcing.shape
    total = lax.axis_size("brick") * lax.axis_size("grp") * record.shape[0]
    rows = -(-total // 128)
    tile = jax.ShapeDtypeStruct((-(-rows // 8) * 8, 128), jnp.float32)
    xy = jax.ShapeDtypeStruct((2 * (2 * slots + 2), lanes), jnp.float32)
    z = jax.ShapeDtypeStruct((2 * (2 * slots), lanes), jnp.float32)
    n_brick = lax.axis_size("brick")
    n_grp = lax.axis_size("grp")
    vmem = pl.BlockSpec(memory_space=pltpu.VMEM)
    dma = pltpu.SemaphoreType.DMA
    return pl.pallas_call(
        exchange_kernel,
        out_shape=(
            jax.ShapeDtypeStruct(tile.shape, jnp.float32),
            jax.ShapeDtypeStruct((n_brick,) + xy.shape, jnp.float32),
            jax.ShapeDtypeStruct((2,) + z.shape, jnp.float32),
        ),
        in_specs=[pl.BlockSpec(memory_space=pltpu.SMEM), vmem, vmem],
        out_specs=(vmem, vmem, vmem),
        scratch_shapes=[
            pltpu.VMEM(tile.shape, jnp.float32),
            pltpu.VMEM(xy.shape, jnp.float32),
            pltpu.VMEM(z.shape, jnp.float32),
            pltpu.VMEM((n_brick,) + tile.shape, jnp.float32),
            pltpu.VMEM((n_grp,) + tile.shape, jnp.float32),
            pltpu.VMEM((n_brick,) + xy.shape, jnp.float32),
            pltpu.VMEM((2,) + z.shape, jnp.float32),
            dma((n_brick,)),
            dma((n_brick,)),
            dma((n_grp,)),
            dma((n_grp,)),
            dma((n_brick,)),
            dma((n_brick,)),
            dma((2,)),
            dma((2,)),
        ],
        compiler_params=pltpu.CompilerParams(collective_id=kernel_id, has_side_effects=True),
    )(record, forcing, diag)


def stencil_body(
    coef_ref, f_ref, bonds_ref, masks_ref, diag_ref, rows_ref, faces_ref, o_ref, xy_ref, z_ref, smooth,
    with_faces=True,
):
    slots, width, lanes = f_ref.shape
    row = lax.broadcasted_iota(jnp.int32, (width, lanes), 0)
    lane = lax.broadcasted_iota(jnp.int32, (width, lanes), 1)
    pick = lax.broadcasted_iota(jnp.int32, (BS, lanes), 0)
    spot = lax.broadcasted_iota(jnp.int32, (BS, lanes), 1)
    spread_z = (spot // BS == pick).astype(jnp.float32)
    spread_y = (spot % BS == pick).astype(jnp.float32)

    def spread(face, table):
        high = face.astype(jnp.bfloat16)
        rest = face - high.astype(jnp.float32)
        middle = rest.astype(jnp.bfloat16)
        low = (rest - middle.astype(jnp.float32)).astype(jnp.bfloat16)
        table = table.astype(jnp.bfloat16)
        parts = [
            jnp.dot(part, table, preferred_element_type=jnp.float32) for part in (high, middle, low)
        ]
        return (parts[0] + parts[1]) + parts[2]

    borders = [
        row == width - 1,
        row == 0,
        lane >= lanes - BS,
        lane < BS,
        lane % BS == BS - 1,
        lane % BS == 0,
    ]
    source_lane = lax.broadcasted_iota(jnp.int32, (lanes, BS), 0)
    place = lax.broadcasted_iota(jnp.int32, (lanes, BS), 1)
    layers = [
        (source_lane == offset + step * place).astype(jnp.float32)
        for offset, step in ((0, 1), (lanes - BS, 1), (0, BS), (BS - 1, BS))
    ]
    flat_mask = spot // BS == pick

    def flatten(layer):
        spread_out = jnp.where(flat_mask, spread(layer, spread_y), 0.0)
        return jnp.sum(spread_out, axis=0, keepdims=True)

    dot = jnp.float32(0.0)
    sums = []
    for s in range(slots):
        ds = diag_ref[s]
        if smooth:
            rs = f_ref[s]
            fs = OMEGA * rs / ds
        else:
            fs = f_ref[s]
        xp = jnp.where(row == width - 1, rows_ref[0, s], pltpu.roll(fs, width - 1, 0))
        xm = jnp.where(row == 0, rows_ref[1, s], pltpu.roll(fs, 1, 0))
        yp = jnp.where(lane >= lanes - BS, spread(faces_ref[0, s], spread_y), pltpu.roll(fs, lanes - BS, 1))
        ym = jnp.where(lane < BS, spread(faces_ref[1, s], spread_y), pltpu.roll(fs, BS, 1))
        zp = jnp.where(lane % BS == BS - 1, spread(faces_ref[2, s], spread_z), pltpu.roll(fs, lanes - 1, 1))
        zm = jnp.where(lane % BS == 0, spread(faces_ref[3, s], spread_z), pltpu.roll(fs, 1, 1))
        total = ds * fs
        for d, beyond in enumerate([xp, xm, yp, ym, zp, zm]):
            base = 2 * (d * slots + s)
            active = jnp.where(borders[d], masks_ref[base + 1], masks_ref[base])
            total = total - bonds_ref[d, s] * active * beyond
        if smooth:
            total = fs + OMEGA * (rs - total) / ds
            total = total + coef_ref[s]
            dot = dot + jnp.sum(rs * total)
        else:
            dot = dot + jnp.sum(fs * total)
            sums.append(jnp.sum(total))
        o_ref[s] = total
        if not with_faces:
            continue
        xy_ref[pl.ds(s, 1), :] = total[0:1, :]
        xy_ref[pl.ds(slots + s, 1), :] = total[width - 1 : width, :]
        if s == 0:
            xy_ref[pl.ds(2 * slots, 1), :] = flatten(spread(total, layers[0]))
        if s == slots - 1:
            xy_ref[pl.ds(2 * slots + 1, 1), :] = flatten(spread(total, layers[1]))
        z_ref[pl.ds(s, 1), :] = flatten(spread(total, layers[2]))
        z_ref[pl.ds(slots + s, 1), :] = flatten(spread(total, layers[3]))
    return dot, sums


def round_kernel(
    coef_ref, f_ref, bonds_ref, masks_ref, diag_ref, rows_ref, faces_ref,
    o_ref, total_ref, xy_out, z_out, dot_ref,
    xy_buf, z_buf, tile_buf, landed_b, landed_g, landed_xy, landed_z,
    send_b, recv_b, send_g, recv_g, send_xy, recv_xy, send_z, recv_z, *, smooth, with_faces
):
    here_brick = lax.axis_index("brick")
    here_grp = lax.axis_index("grp")
    n_brick = landed_b.shape[0]
    n_grp = landed_g.shape[0]
    brick_peers = [(lax.rem(here_brick + k, n_brick), here_grp) for k in range(1, n_brick)]
    grp_peers = [(here_brick, lax.rem(here_grp + k, n_grp)) for k in range(1, n_grp)]
    barrier = pltpu.get_barrier_semaphore()
    for peer in brick_peers + grp_peers:
        pl.semaphore_signal(barrier, inc=1, device_id=peer, device_id_type=MESH_IDS)
    dot, sums = stencil_body(
        coef_ref, f_ref, bonds_ref, masks_ref, diag_ref, rows_ref, faces_ref, o_ref, xy_buf, z_buf,
        smooth, with_faces,
    )
    tile_rows, tile_lanes = tile_buf.shape
    flat = lax.broadcasted_iota(jnp.int32, (tile_rows, tile_lanes), 0) * tile_lanes
    flat = flat + lax.broadcasted_iota(jnp.int32, (tile_rows, tile_lanes), 1)
    tile = jnp.where(flat == 0, dot, 0.0)
    slots = f_ref.shape[0]
    for s, value in enumerate(sums):
        position = 1 + (here_brick * n_grp + here_grp) * slots + s
        tile = jnp.where(flat == position, value, tile)
    tile_buf[...] = tile
    pl.semaphore_wait(barrier, len(brick_peers) + len(grp_peers))
    share(
        tile_buf, xy_buf, z_buf, total_ref, xy_out, z_out, landed_b, landed_g, landed_xy, landed_z,
        send_b, recv_b, send_g, recv_g, send_xy, recv_xy, send_z, recv_z, brick_peers, grp_peers,
        dot_ref=dot_ref, with_faces=with_faces,
    )


def one_round(field, bonds, masks, diag, rows, faces, coef, smooth, with_faces=True):
    slots, _, lanes = field.shape
    n_brick = lax.axis_size("brick")
    n_grp = lax.axis_size("grp")
    tile = (8, 128)
    xy = (2 * slots + 2, lanes)
    z = (2 * slots, lanes)
    vmem = pl.BlockSpec(memory_space=pltpu.VMEM)
    smem = pl.BlockSpec(memory_space=pltpu.SMEM)
    dma = pltpu.SemaphoreType.DMA
    return pl.pallas_call(
        functools.partial(round_kernel, smooth=smooth, with_faces=with_faces),
        out_shape=(
            jax.ShapeDtypeStruct(field.shape, jnp.float32),
            jax.ShapeDtypeStruct(tile, jnp.float32),
            jax.ShapeDtypeStruct((n_brick,) + xy, jnp.float32),
            jax.ShapeDtypeStruct((2,) + z, jnp.float32),
            jax.ShapeDtypeStruct((1,), jnp.float32),
        ),
        in_specs=[smem, vmem, vmem, smem, vmem, vmem, vmem],
        out_specs=(vmem, vmem, vmem, vmem, smem),
        scratch_shapes=[
            pltpu.VMEM(xy, jnp.float32),
            pltpu.VMEM(z, jnp.float32),
            pltpu.VMEM(tile, jnp.float32),
            pltpu.VMEM((n_brick,) + tile, jnp.float32),
            pltpu.VMEM((n_grp,) + tile, jnp.float32),
            pltpu.VMEM((n_brick,) + xy, jnp.float32),
            pltpu.VMEM((2,) + z, jnp.float32),
            dma((n_brick,)),
            dma((n_brick,)),
            dma((n_grp,)),
            dma((n_grp,)),
            dma((n_brick,)),
            dma((n_brick,)),
            dma((2,)),
            dma((2,)),
        ],
        compiler_params=pltpu.CompilerParams(
            collective_id=(3 if smooth else 1) if with_faces else 4, has_side_effects=True
        ),
    )(coef, field, bonds, masks, diag, rows, faces)


def assemble(coarse_diag, couplings, strides):
    extent = coarse_diag.shape[0]
    matrix = jnp.diag(coarse_diag)
    for coupling, stride in zip(couplings, strides):
        banded = coupling[: extent - stride]
        matrix = matrix - jnp.diag(banded, stride) - jnp.diag(banded, -stride)
    return matrix


def on_device(source, uptake, conductance, occupancy, assignment):
    face_size = BS * BS
    slot_count = PATCH_X * PATCH_Y
    slab_index = lax.axis_index("grp")
    brick_index = lax.axis_index("brick")
    brick_count = lax.axis_size("brick")
    across = brick_count // 2
    peer_ids = jnp.arange(brick_count, dtype=jnp.int32)
    patch_index = assignment[brick_index]
    patch_row = patch_index // across
    patch_column = patch_index % across

    def owner_of(row_shift, column_shift):
        row_target = patch_row + row_shift
        column_target = patch_column + column_shift
        inside = (
            (row_target >= 0) & (row_target < 2) & (column_target >= 0) & (column_target < across)
        )
        holder = jnp.sum(jnp.where(assignment == row_target * across + column_target, peer_ids, 0))
        return jnp.where(inside, holder, -1)

    wanted = jnp.stack([owner_of(1, 0), owner_of(-1, 0), owner_of(0, 1), owner_of(0, -1)])
    padded = jnp.pad(occupancy, 1)
    window = lax.dynamic_slice(
        padded,
        (slab_index, patch_row * PATCH_X, patch_column * PATCH_Y),
        (3, PATCH_X + 2, PATCH_Y + 2),
    ).astype(jnp.float32)
    centre = window[1, 1:-1, 1:-1].reshape(slot_count)
    toward = [
        window[1, 2:, 1:-1],
        window[1, :-2, 1:-1],
        window[1, 1:-1, 2:],
        window[1, 1:-1, :-2],
        window[2, 1:-1, 1:-1],
        window[0, 1:-1, 1:-1],
    ]
    first_axis = lax.broadcasted_iota(jnp.int32, (1, BS, face_size), 1)
    flat_axis = lax.broadcasted_iota(jnp.int32, (1, BS, face_size), 2)
    second_axis = flat_axis // BS
    third_axis = flat_axis % BS
    cube_third = lax.broadcasted_iota(jnp.int32, (1, BS, BS, BS), 3)
    borders = [
        first_axis == BS - 1,
        first_axis == 0,
        second_axis == BS - 1,
        second_axis == 0,
        third_axis == BS - 1,
        third_axis == 0,
    ]
    bonds = conductance[0, 0]
    live_here = centre[:, None, None]
    effective = []
    for direction in range(6):
        neighbour_live = toward[direction].reshape(slot_count)[:, None, None]
        active = jnp.where(borders[direction], live_here * neighbour_live, live_here)
        effective.append(bonds[direction] * active)
    absorb = uptake[0, 0]
    diagonal = absorb
    for direction in range(6):
        diagonal = diagonal + effective[direction]

    masks = jnp.stack(
        [
            jnp.stack([centre, centre * toward[direction].reshape(slot_count)], axis=1)
            for direction in range(6)
        ]
    ).reshape(-1)

    lane_ids = jnp.arange(face_size, dtype=jnp.int32)[:, None]
    layer_ids = BS * jnp.arange(BS, dtype=jnp.int32)[None, :]
    picker = jnp.concatenate([lane_ids == layer_ids, lane_ids == layer_ids + BS - 1], axis=1)
    picker = picker.astype(jnp.float32)

    def side_faces(field):
        picked = jnp.dot(
            field.reshape(slot_count * BS, face_size), picker, precision=lax.Precision.HIGHEST
        )
        z = picked.reshape(slot_count, BS, 2, BS).transpose(2, 0, 1, 3)
        xy = jnp.concatenate(
            [
                field[:, 0, :],
                field[:, BS - 1, :],
                field[0, :, :BS].reshape(1, face_size),
                field[slot_count - 1, :, face_size - BS :].reshape(1, face_size),
            ]
        )
        return xy, z.reshape(2 * slot_count, face_size)

    def pick(landed, holder, fill):
        offset = lax.rem(brick_index - holder + brick_count, brick_count)
        got = lax.dynamic_index_in_dim(landed, offset, keepdims=False)
        return jnp.where(holder >= 0, got, fill)

    def halo(field, xy_land, z_land, fill):
        xplus = pick(xy_land, wanted[0], fill)
        xminus = pick(xy_land, wanted[1], fill)
        yplus = pick(xy_land, wanted[2], fill)
        yminus = pick(xy_land, wanted[3], fill)
        rows = jnp.stack([xplus[:slot_count], xminus[slot_count : 2 * slot_count]])[:, :, None, :]
        beyond_yplus = jnp.stack([field[1, :, :BS], yplus[2 * slot_count].reshape(BS, BS)])
        beyond_yminus = jnp.stack(
            [yminus[2 * slot_count + 1].reshape(BS, BS), field[0, :, face_size - BS :]]
        )
        above = jnp.where(slab_index < grp_count - 1, z_land[1, :slot_count], fill)
        below = jnp.where(slab_index > 0, z_land[0, slot_count:], fill)
        faces = jnp.stack(
            [
                beyond_yplus,
                beyond_yminus,
                above.reshape(slot_count, BS, BS),
                below.reshape(slot_count, BS, BS),
            ]
        )
        return rows, faces

    slot_ids = jnp.arange(slot_count)
    brick_first = slot_ids // PATCH_Y
    brick_second = slot_ids % PATCH_Y
    inside = [
        (brick_first < PATCH_X - 1).astype(jnp.float32),
        (brick_first > 0).astype(jnp.float32),
        (brick_second < PATCH_Y - 1).astype(jnp.float32),
        (brick_second > 0).astype(jnp.float32),
    ]
    face_sums = [
        jnp.sum(effective[0][:, BS - 1, :], axis=1),
        jnp.sum(effective[1][:, 0, :], axis=1),
        jnp.sum(effective[2][:, :, face_size - BS :], axis=(1, 2)),
        jnp.sum(effective[3][:, :, :BS], axis=(1, 2)),
        jnp.sum(jnp.where(borders[4], effective[4], 0.0), axis=(1, 2)),
        jnp.sum(jnp.where(borders[5], effective[5], 0.0), axis=(1, 2)),
    ]
    coarse_diag = jnp.sum(absorb, axis=(1, 2))
    for direction in range(4):
        coarse_diag = coarse_diag + face_sums[direction] * inside[direction]
    coarse_diag = coarse_diag + face_sums[4] + face_sums[5]
    grp_count = lax.axis_size("grp")
    grp_ids = jnp.arange(grp_count, dtype=jnp.int32)

    def slab_slot(values):
        here = (grp_ids == slab_index).astype(jnp.float32)
        return here[:, None, None] * values[None]

    forcing = source[0, 0] * live_here

    def as_tile(values):
        rows = -(-values.shape[0] // 128)
        rows = -(-rows // 8) * 8
        return jnp.pad(values, (0, rows * 128 - values.shape[0])).reshape(rows, 128)

    record = jnp.stack(
        [
            coarse_diag,
            face_sums[0] * inside[0],
            face_sums[2] * inside[2],
            face_sums[4],
            jnp.sum(forcing, axis=(1, 2)),
        ]
    )
    brick_here = (peer_ids == brick_index).astype(jnp.float32)
    summed, xy_land, z_land = exchange(record.reshape(-1), forcing, diagonal, 2)
    summed = summed.reshape(-1)[: brick_count * grp_count * record.size]
    xy_rows = 2 * slot_count + 2
    z_rows = 2 * slot_count
    residual_halo = halo(forcing, xy_land[:, :xy_rows], z_land[:, :z_rows], 0.0)
    diagonal_halo = halo(diagonal, xy_land[:, xy_rows:], z_land[:, z_rows:], 1.0)
    gathered = lax.dynamic_index_in_dim(
        summed.reshape(brick_count, grp_count, 5, slot_count), brick_index, keepdims=False
    )
    columns = jnp.transpose(gathered, (1, 0, 2)).reshape(5, -1)
    matrix = assemble(columns[0], (columns[1], columns[2], columns[3]), (PATCH_Y, 1, slot_count))
    factor = jnp.linalg.cholesky(matrix)

    identity = jnp.eye(factor.shape[0], dtype=jnp.float32)
    middle = lax.linalg.triangular_solve(factor, identity, left_side=True, lower=True)
    inverse = lax.linalg.triangular_solve(
        factor, middle, left_side=True, lower=True, transpose_a=True
    )
    own_rows = lax.dynamic_slice_in_dim(inverse, slab_index * slot_count, slot_count)

    def coarse_solve(terms):
        return jnp.dot(own_rows, terms, precision=lax.Precision.HIGHEST)

    def round_trip(field, field_halo, coef, smooth, with_faces=True):
        out, total, xy_land, z_land, dot = one_round(
            field, bonds, masks, diagonal, *field_halo, coef, smooth, with_faces
        )
        total = total.reshape(-1)
        out_halo = halo(out, xy_land, z_land, 0.0) if with_faces else None
        if smooth:
            return out, dot[0], None, out_halo
        count = brick_count * grp_count * slot_count
        mine = lax.dynamic_index_in_dim(
            total[1 : 1 + count].reshape(brick_count, -1), brick_index, keepdims=False
        )
        return out, dot[0], mine, out_halo

    def precondition(residual_field, field_halo, terms):
        smoothed_halo = [OMEGA * part / scale for part, scale in zip(field_halo, diagonal_halo)]
        return round_trip(residual_field, smoothed_halo, coarse_solve(terms), True)

    no_coarse = jnp.zeros((slot_count,), jnp.float32)
    terms = columns[4]
    solution_field = jnp.zeros_like(forcing)
    residual = forcing
    search, energy, _, search_halo = precondition(residual, residual_halo, terms)
    for iteration in range(ITERS):
        mapped, curvature, mapped_terms, mapped_halo = round_trip(
            search, search_halo, no_coarse, False, iteration + 1 < ITERS
        )
        step_size = energy / curvature
        solution_field = solution_field + step_size * search
        residual = residual - step_size * mapped
        if iteration + 1 < ITERS:
            residual_halo = [
                part - step_size * change for part, change in zip(residual_halo, mapped_halo)
            ]
            terms = terms - step_size * mapped_terms
            smoothed, renewed, _, smoothed_halo = precondition(residual, residual_halo, terms)
            search = smoothed + renewed / energy * search
            search_halo = [
                part + renewed / energy * old for part, old in zip(smoothed_halo, search_halo)
            ]
            energy = renewed
    return (solution_field[None, None], residual[None, None])


def solution(mesh):
    return jax.shard_map(
        on_device,
        mesh=mesh,
        in_specs=(
            P("grp", "brick", None, None, None),
            P("grp", "brick", None, None, None),
            P("grp", "brick", None, None, None, None),
            P(),
            P(),
        ),
        out_specs=(P("grp", "brick", None, None, None), P("grp", "brick", None, None, None)),
        check_vma=False,
    )
```
